32 devices in a mesh: branch: 4 (over y, core), segment: 2 (over x), tp: 4 (over z).
Axes of the slice: x: 2, y: 2, z: 4, core: 2. Of those that a mesh axis runs over, the one named last changes fastest.
Arguments:
- rollout: bfloat16 [576, 8192], P(('branch', 'segment')), may hold values from -6 to 6
- send_rows: int32 [576], P(('branch', 'segment')), may hold values from 0 to 71, as said below
- seq_lengths: int32 [2, 6], P('segment'), may hold values from 1 to 144, 288 in all within a row
- attn_gain: bfloat16 [4, 8192], P('branch'), may hold values from 0.099609375 to 1.8984375
- w_query: bfloat16 [4, 8192, 8192], P('branch', 'segment', 'tp'), may hold values from -1 to 1
- w_keyval: bfloat16 [4, 8192, 2048], P('branch', 'segment', 'tp'), may hold values from -1 to 1
- head_weight: bfloat16 [4, 8192], P('branch', 'tp'), may hold values from -0.0625 to 0.0625
- head_attn: bfloat16 [4, 8192], P('branch', 'tp'), may hold values from -0.25 to 0.25
Outputs:
- scores: float32 [4, 576], P(None, ('branch', 'segment'))
The draws below stay inside these ranges and needn't reach their ends.
Inputs may be any that keep to these rules, and one draw needn't show every extreme that they name: `send_rows`: each aligned block of 72 entries holds every number of 0 to 71 once.
All inputs are finite; a program needn't handle non-finite values.
Results may differ from the reference program's by a relative error of at most 0.006.
Values may be sent and summed in bfloat16 or wider, within the bound.
No kernel may reach another device: no remote copies, remote signals or barrier semaphores. Data moves between devices by JAX's collectives and lax.ppermute only.
A program may use at most 128 MiB of HBM per device.

```python
import math
import jax
import jax.numpy as jnp
import numpy as np
from jax import lax

D = 8192
HEAD = 128
HEADS = 64
KV_HEADS = 8
PACK = 288
SEQ_PACK = 6
MAXLEN = 144
SECTIONS = 4
PACKS = 2
TOKENS = 576
GEN_DEV = 72
PIECE = 36


def draw_send_rows(key, part):
    block_keys = jax.random.split(key, TOKENS // GEN_DEV)
    shuffled = jax.vmap(lambda one_key: jax.random.permutation(one_key, GEN_DEV))(block_keys)
    return shuffled.reshape(TOKENS).astype(jnp.int32)


def noise_weights(key, columns):
    scale = D ** (-0.5)
    values = jax.random.normal(key, (SECTIONS, D, columns), jnp.float32) * scale
    return jnp.clip(values, -6.0 * scale, 6.0 * scale)


def draw_rollout(key, part):
    noise_key = jax.random.fold_in(key, 1)
    rows = jax.random.normal(noise_key, (TOKENS, D), jnp.float32)
    return jnp.clip(rows, -6.0, 6.0).astype(jnp.bfloat16)


def draw_w_query(key, part):
    columns = HEADS * HEAD
    values = noise_weights(jax.random.fold_in(key, 5), columns)
    return jnp.clip(values, -1.0, 1.0).astype(jnp.bfloat16)


def draw_w_keyval(key, part):
    columns = 2 * KV_HEADS * HEAD
    values = noise_weights(jax.random.fold_in(key, 6), columns)
    return jnp.clip(values, -1.0, 1.0).astype(jnp.bfloat16)


def levels(own_key, shape, cuts, smallest, high):
    factor_of, own = 1.0, jax.random.fold_in(own_key, 6)
    for position, parts in cuts:
        draws = jnp.exp(jax.random.uniform(jax.random.fold_in(own, position), (parts,), jnp.float32, smallest / len(cuts), high / len(cuts)))
        factor_of = factor_of * jnp.repeat(draws, shape[position] // parts).reshape([-1 if axis == position else 1 for axis in range(len(shape))])
    return factor_of


def length_profile(number_of, total, bound, lean):
    portions = [(1 << 20) // math.isqrt(rank ** lean) + 1 for rank in range(2, number_of + 1)]
    surplus, holding = total - bound - (number_of - 1), [1] * (number_of - 1)
    while surplus > 0:
        movable = [i for i in range(number_of - 1) if holding[i] < bound]
        pool, left = sum([portions[i] for i in movable]), surplus
        for i in movable:
            extra = min(bound - holding[i], max(1, left * portions[i] // pool), surplus)
            holding[i] = holding[i] + extra
            surplus = surplus - extra
    return np.array([bound] + holding)


def ragged_sizes(rng, amount, total, reach, lean):
    if amount == 2:
        one = jax.random.randint(rng, (), max(1, total - reach), min(reach, total - 1) + 1)
        return jnp.stack([one, total - one])
    tallies = jnp.asarray(length_profile(amount, total, reach, lean), jnp.int32)
    twos = (amount - 1) // 2
    donor, taker = tallies[1:1 + 2 * twos:2], tallies[2:2 + 2 * twos:2]
    margin = jnp.minimum(donor - 1, reach - taker)
    shifted = jax.random.randint(jax.random.fold_in(rng, 1), (twos,), 0, 1 << 20) % (margin + 1)
    tallies = tallies.at[1:1 + 2 * twos:2].set(donor - shifted).at[2:2 + 2 * twos:2].set(taker + shifted)
    return tallies[jax.random.permutation(jax.random.fold_in(rng, 2), amount)]


def scatter_about(key, extent, deviation, bound, cuts=(), kind=jnp.bfloat16):
    factor_of = levels(key, extent, cuts, -0.22, 0.18) if cuts else 1.0
    result = jax.random.normal(key, extent, jnp.float32) * deviation * factor_of
    return jnp.minimum(jnp.maximum(result, -bound), bound).astype(kind)


def setup_inputs(seed: int = 0) -> dict:
    splits = jax.random.split(jax.random.key(seed), 9)
    rollout = draw_rollout(jax.random.fold_in(splits[8], 71), 0)
    send_rows = draw_send_rows(jax.random.fold_in(splits[8], 71), 0)
    seq_lengths = jax.vmap(lambda own: ragged_sizes(own, SEQ_PACK, PACK, MAXLEN, 2))(jax.random.split(splits[2], PACKS)).reshape((PACKS, SEQ_PACK)).astype(jnp.int32)
    attn_gain = jnp.clip(1.0 + 0.18 * jax.random.normal(splits[3], (SECTIONS, D), jnp.float32), 0.099609375, 1.8984375).astype(jnp.bfloat16)
    w_query = draw_w_query(jax.random.fold_in(splits[8], 71), 0)
    w_keyval = draw_w_keyval(jax.random.fold_in(splits[8], 71), 0)
    head_weight = scatter_about(splits[6], (SECTIONS, D), D ** -0.5, 0.0625, ((0, 4), (1, 4)))
    head_attn = scatter_about(splits[7], (SECTIONS, HEADS * HEAD), (HEADS * HEAD // 16) ** -0.5, 0.25, ((0, 4), (1, 4)))
    return {"rollout": rollout, "send_rows": send_rows, "seq_lengths": seq_lengths, "attn_gain": attn_gain, "w_query": w_query, "w_keyval": w_keyval, "head_weight": head_weight, "head_attn": head_attn}


epsilon = 1e-05

def score_pack(rows_in, lengths, norm_gain, query_weight, keyval_weight, head_rows, head_heads):
    rows_float = rows_in.astype(jnp.float32)
    mean_square = lax.optimization_barrier(jnp.mean(rows_float * rows_float, axis=-1, keepdims=True))
    normed = (rows_float * lax.rsqrt(mean_square + epsilon) * norm_gain.astype(jnp.float32)).astype(jnp.bfloat16)
    queries = jnp.dot(normed, query_weight, preferred_element_type=jnp.float32).astype(jnp.bfloat16)
    keyval = jnp.dot(normed, keyval_weight, preferred_element_type=jnp.float32).astype(jnp.bfloat16)
    queries = queries.reshape(PACK, HEADS, HEAD)
    key_rows = keyval[:, :KV_HEADS * HEAD].reshape(PACK, KV_HEADS, HEAD)
    value_rows = keyval[:, KV_HEADS * HEAD:].reshape(PACK, KV_HEADS, HEAD)
    group_size = HEADS // KV_HEADS
    key_rows = jnp.repeat(key_rows, group_size, axis=1)
    value_rows = jnp.repeat(value_rows, group_size, axis=1)
    positions = jnp.arange(PACK, dtype=jnp.int32)
    doc_ends = jnp.cumsum(lengths).astype(jnp.int32)
    doc_ids = lax.optimization_barrier(jnp.sum((positions[:, None] >= doc_ends[None, :]).astype(jnp.int32), axis=-1))
    visible = (doc_ids[:, None] == doc_ids[None, :]) & (positions[None, :] <= positions[:, None])
    logits = jnp.einsum('qhc,khc->hqk', queries.astype(jnp.float32), key_rows.astype(jnp.float32)) / math.sqrt(HEAD)
    logits = jnp.where(visible[None], logits, -1e+30)
    row_max = lax.optimization_barrier(jnp.max(logits, axis=-1, keepdims=True))
    expo = jnp.exp(logits - row_max)
    probabilities = (expo / lax.optimization_barrier(jnp.sum(expo, axis=-1, keepdims=True))).astype(jnp.bfloat16)
    attended = jnp.einsum('hqk,khc->qhc', probabilities.astype(jnp.float32), value_rows.astype(jnp.float32))
    attended = attended.reshape(PACK, HEADS * HEAD)
    direct = jnp.dot(rows_in, head_rows, preferred_element_type=jnp.float32)
    through = jnp.dot(attended, head_heads.astype(jnp.float32), precision=lax.Precision.HIGHEST)
    return direct + through

def reference(rollout, send_rows, seq_lengths, attn_gain, w_query, w_keyval, head_weight, head_attn):
    rank_rows = jnp.arange(PACK, dtype=jnp.int32)
    shard_ids = rank_rows // PIECE
    within = rank_rows % PIECE
    segment_ids = jnp.arange(PACKS, dtype=jnp.int32)
    flat_pos = (shard_ids[None, :] * GEN_DEV + segment_ids[:, None] * PIECE + within[None, :]).astype(jnp.int32)
    source = (shard_ids[None, :] * GEN_DEV + send_rows[flat_pos]).astype(jnp.int32)
    packed = rollout[source]

    def one_section(section_item):
        norm_gain, query_weight, keyval_weight, head_rows, head_heads = section_item

        def one_pack(pack_item):
            return score_pack(pack_item[0], pack_item[1], norm_gain, query_weight, keyval_weight, head_rows, head_heads)
        return lax.map(one_pack, (packed, seq_lengths))
    scores_packed = lax.map(one_section, (attn_gain, w_query, w_keyval, head_weight, head_attn))
    scores = jnp.zeros((SECTIONS, TOKENS), jnp.float32)
    scores = scores.at[:, source.reshape(-1)].set(scores_packed.reshape(SECTIONS, TOKENS))
    return scores
```

```python
import math

import jax
import jax.numpy as jnp
from jax import lax
from jax.experimental import pallas as pl
from jax.experimental.pallas import tpu as pltpu
from jax.sharding import PartitionSpec as P


HEAD = 128
HEADS = 64
KV_HEADS = 8
LANES = 128
LENGTHS_AT = 8

epsilon = 1e-05

ALL_AXES = ("branch", "segment", "tp")
HIGHEST = lax.Precision.HIGHEST
F32 = jnp.float32
BF16 = jnp.bfloat16


def whole(memory_space=pltpu.VMEM):
    return pl.BlockSpec(memory_space=memory_space)


def iota(shape, dimension):
    return lax.broadcasted_iota(jnp.int32, shape, dimension)


def prepare_kernel(ids_ref, lengths_ref, rows_hbm, send_hbm, mine_ref, theirs_ref, rows_ref, send_ref, sems):
    count, width = rows_ref.shape
    half = width // 2
    parts = sems.shape[0] - 1
    step = width // parts
    core, segment = ids_ref[0], ids_ref[1]
    copies = [pltpu.make_async_copy(send_hbm, send_ref, sems.at[parts])]
    for part in range(parts):
        at = pl.ds(part * step, step)
        copies.append(pltpu.make_async_copy(rows_hbm.at[:, at], rows_ref.at[:, at], sems.at[part]))
    for copy in copies:
        copy.start()
    copies[0].wait()
    send = send_ref[...]
    rolled = jnp.concatenate([send[:, count // 2:], send[:, :count // 2]], axis=1)
    order = jnp.where(core == 1, rolled, send)
    pick = (iota((count, count), 0) == order).astype(BF16)

    def ordered(part):
        out = lax.dot_general(pick, part, (((0,), (0,)), ((), ())), preferred_element_type=F32)
        return out.astype(BF16)

    lanes = jnp.zeros((count, LANES), F32)
    for part in range(parts):
        copies[1 + part].wait()
        square = rows_ref[:, part * step:(part + 1) * step].astype(F32)
        square = square * square
        for lane in range(0, step, LANES):
            lanes = lanes + square[:, lane:lane + LANES]
    chunk = 1024
    for start in range(0, half, chunk):
        for out_ref, which in ((theirs_ref, 1 - segment), (mine_ref, segment)):
            at = pl.multiple_of(which * half + start, chunk)
            out_ref[:, start:start + chunk] = ordered(rows_ref[:, pl.ds(at, chunk)])
    scale = lax.rsqrt(jnp.sum(lanes, axis=1, keepdims=True) * (1.0 / width) + epsilon)
    high = scale.astype(BF16).astype(F32)
    middle = (scale - high).astype(BF16).astype(F32)
    low = scale - high - middle
    lane = iota((count, LANES), 1)
    tail = jnp.where(lane == 0, high, jnp.where(lane == 1, middle, jnp.where(lane == 2, low, 0.0)))
    tail = ordered(tail.astype(BF16))
    for index in range(lengths_ref.shape[1]):
        length = lengths_ref[0, index].astype(F32).astype(BF16)
        tail = jnp.where(lane == LENGTHS_AT + index, length, tail)
    theirs_ref[:, half:] = tail
    mine_ref[:, half:] = tail


def prepare(ids, lengths, rows, send):
    count, width = rows.shape
    shape = jax.ShapeDtypeStruct((count, width // 2 + LANES), BF16)
    return pl.pallas_call(
        prepare_kernel,
        out_shape=(shape, shape),
        in_specs=[whole(pltpu.SMEM), whole(pltpu.SMEM), whole(pltpu.HBM), whole(pltpu.HBM)],
        out_specs=(whole(), whole()),
        scratch_shapes=[
            pltpu.VMEM((count, width), BF16),
            pltpu.VMEM((1, count), jnp.int32),
            pltpu.SemaphoreType.DMA((5,)),
        ],
        compiler_params=pltpu.CompilerParams(vmem_limit_bytes=12 << 20),
        name="prepare",
    )(ids, lengths, rows, send)


def chunk_kernel(ids_ref, near_ref, far_ref, gain_hbm, keyval_hbm, query_hbm, head_hbm,
                 rows_ref, own_ref, direct_ref, tail_ref, *refs):
    sends, (gain_ref, keyval_ref, query_ref, head_ref, sems) = refs[:-5], refs[-5:]
    send_ref = sends[0]
    count = near_ref.shape[0]
    half = rows_ref.shape[1]
    blocks, _, block = query_ref.shape
    core, segment, tp = ids_ref[0], ids_ref[1], ids_ref[3]
    columns = blocks * block
    gain_copy = pltpu.make_async_copy(gain_hbm.at[:, pl.ds(pl.multiple_of(segment * half, half), half)], gain_ref, sems.at[0])
    head_copy = pltpu.make_async_copy(head_hbm, head_ref, sems.at[1])
    keyval_copy = pltpu.make_async_copy(keyval_hbm, keyval_ref, sems.at[2])
    gain_copy.start()
    head_copy.start()
    keyval_copy.start()
    query_copies = []
    for index in range(blocks):
        at = pl.multiple_of((1 - segment) * columns + index * block, block)
        query_copies.append(pltpu.make_async_copy(query_hbm.at[:, pl.ds(at, block)], query_ref.at[index], sems.at[3 + index]))
        query_copies[-1].start()

    top = (iota((count, 1), 0) < count // 2).astype(jnp.int32)
    mask = (top ^ core) == 1

    def both(near, far):
        return jnp.concatenate([jnp.where(mask, near, far), jnp.where(mask, far, near)], axis=0)

    first_lanes = iota((count, LANES), 1) < 3

    def scale_of(ref):
        return jnp.sum(jnp.where(first_lanes, ref[:, half:].astype(F32), 0.0), axis=1, keepdims=True)

    scale = both(scale_of(near_ref), scale_of(far_ref))
    slice_width = head_ref.shape[1]
    holder = (tp * slice_width) // half == segment
    first = (tp * slice_width) % half
    chunk = 512
    direct = jnp.zeros((2 * count, LANES), F32)
    gain_copy.wait()
    head_copy.wait()
    for start in range(0, half, chunk):
        at = slice(start, start + chunk)
        rows = both(near_ref[:, at].astype(F32), far_ref[:, at].astype(F32))
        inside = jnp.logical_and(holder, jnp.logical_and(start >= first, start < first + slice_width))
        offset = pl.multiple_of(jnp.where(inside, start - first, 0), chunk)
        weight = jnp.where(inside, head_ref[:, pl.ds(offset, chunk)].astype(F32), 0.0)
        for lane in range(0, chunk, LANES):
            direct = direct + rows[:, lane:lane + LANES] * weight[:, lane:lane + LANES]
        rows_ref[:, at] = (rows * scale * gain_ref[:, at].astype(F32)).astype(BF16)
    direct_ref[...] = direct
    tail_ref[...] = near_ref[:, half:].astype(F32)[:8]

    keyval_copy.wait()
    keyval = jnp.dot(rows_ref[...], keyval_ref[...], preferred_element_type=F32)
    even = jnp.concatenate([keyval[:, :HEAD], keyval[:, 2 * HEAD:3 * HEAD]], axis=1)
    odd = jnp.concatenate([keyval[:, HEAD:2 * HEAD], keyval[:, 3 * HEAD:]], axis=1)
    own_ref[...] = jnp.where(segment == 0, even, odd)
    other = jnp.where(segment == 0, odd, even).astype(BF16)
    if len(sends) == 1:
        send_ref[:, columns:] = other
    else:
        sends[1][...] = other
    for index in range(blocks):
        query_copies[index].wait()
        send_ref[:, index * block:(index + 1) * block] = jnp.dot(
            rows_ref[...], query_ref[index], preferred_element_type=F32).astype(BF16)


def multiply_chunk(ids, near, far, gain, keyval, query, head, split):
    count, wide = near.shape
    half = wide - LANES
    columns = query.shape[1] // 2
    block = 256
    blocks = columns // block
    rows = 2 * count
    widths = (columns, 2 * HEAD) if split else (columns + 2 * HEAD,)
    return pl.pallas_call(
        chunk_kernel,
        out_shape=(
            jax.ShapeDtypeStruct((rows, half), BF16),
            jax.ShapeDtypeStruct((rows, 2 * HEAD), F32),
            jax.ShapeDtypeStruct((rows, LANES), F32),
            jax.ShapeDtypeStruct((8, LANES), F32),
        ) + tuple(jax.ShapeDtypeStruct((rows, width), BF16) for width in widths),
        in_specs=[whole(pltpu.SMEM), whole(), whole()] + [whole(pltpu.HBM)] * 4,
        out_specs=(whole(),) * (4 + len(widths)),
        scratch_shapes=[
            pltpu.VMEM((1, half), BF16),
            pltpu.VMEM(keyval.shape, BF16),
            pltpu.VMEM((blocks, half, block), BF16),
            pltpu.VMEM(head.shape, BF16),
            pltpu.SemaphoreType.DMA((3 + blocks,)),
        ],
        compiler_params=pltpu.CompilerParams(vmem_limit_bytes=28 << 20),
        cost_estimate=pl.CostEstimate(
            flops=2 * rows * half * (columns + keyval.shape[1]), transcendentals=0,
            bytes_accessed=2 * half * (columns + keyval.shape[1])),
        name="chunk",
    )(ids, near, far, gain, keyval, query, head)


def own_kernel(ids_ref, a_ref, b_ref, c_ref, d_ref, query_hbm, out_ref, rows_ref, query_ref, sems):
    blocks, _, block = query_ref.shape
    columns = blocks * block
    copies = []
    for index in range(blocks):
        at = pl.multiple_of(ids_ref[1] * columns + index * block, block)
        copies.append(pltpu.make_async_copy(query_hbm.at[:, pl.ds(at, block)], query_ref.at[index], sems.at[index]))
        copies[-1].start()
    count = a_ref.shape[0]
    for index, ref in enumerate((a_ref, b_ref, c_ref, d_ref)):
        rows_ref[index * count:(index + 1) * count, :] = ref[...]
    for index in range(blocks):
        copies[index].wait()
        out_ref[:, index * block:(index + 1) * block] = jnp.dot(
            rows_ref[...], query_ref[index], preferred_element_type=F32)


def own_queries(ids, chunks, query):
    count, half = chunks[0].shape
    columns = query.shape[1] // 2
    block = 256
    blocks = columns // block
    return pl.pallas_call(
        own_kernel,
        out_shape=jax.ShapeDtypeStruct((4 * count, columns), F32),
        in_specs=[whole(pltpu.SMEM)] + [whole()] * 4 + [whole(pltpu.HBM)],
        out_specs=whole(),
        scratch_shapes=[
            pltpu.VMEM((4 * count, half), BF16),
            pltpu.VMEM((blocks, half, block), BF16),
            pltpu.SemaphoreType.DMA((blocks,)),
        ],
        compiler_params=pltpu.CompilerParams(vmem_limit_bytes=32 << 20),
        cost_estimate=pl.CostEstimate(
            flops=8 * count * half * columns, transcendentals=0, bytes_accessed=2 * half * columns),
        name="own_queries",
    )(ids, *chunks, query)


def by_pack(parts, pack):
    count = parts[0].shape[0] // 2
    return jnp.concatenate([part[pack * count:(pack + 1) * count] for part in parts], axis=0)


def keyval_kernel(ids_ref, *refs):
    owns, recvs = refs[:4], refs[4:8]
    keep_ref, first_ref, second_ref = refs[8:]
    tp = ids_ref[3]
    sums = [own[...] + recv[:, recv.shape[1] - 2 * HEAD:].astype(F32) for own, recv in zip(owns, recvs)]
    rows = 2 * owns[0].shape[0]
    for pack in range(2):
        at = slice(pack * rows, (pack + 1) * rows)
        part = by_pack(sums, pack)
        low, high = part[:, :HEAD], part[:, HEAD:]
        keep_ref[at, :] = jnp.where(tp == 3, high, low).astype(BF16)
        first_ref[at, :] = jnp.where(tp < 2, high, low).astype(BF16)
        second_ref[at, :] = jnp.where(tp == 2, high, low).astype(BF16)


def sum_keyval(ids, owns, recvs):
    rows = 4 * owns[0].shape[0]
    shape = jax.ShapeDtypeStruct((rows, HEAD), BF16)
    return pl.pallas_call(
        keyval_kernel,
        out_shape=(shape, shape, shape),
        in_specs=[whole(pltpu.SMEM)] + [whole()] * 8,
        out_specs=(whole(),) * 3,
        compiler_params=pltpu.CompilerParams(vmem_limit_bytes=8 << 20),
        name="sum_keyval",
    )(ids, *owns, *recvs)


def owner_of(row, pack, ids_ref, piece_rows):
    index = jnp.zeros_like(row)
    for step in range(1, 8):
        index = index + (row >= step * piece_rows).astype(jnp.int32)
    chip, low = index >> 1, index & 1
    shard = (((chip >> 1) ^ ids_ref[2]) * 2 + (low ^ pack)) * 2 + ((chip & 1) ^ ids_ref[1])
    return shard, row - index * piece_rows


def attention_kernel(ids_ref, lengths_ref, tail_ref, own_ref, *refs):
    recvs, (keep_ref, first_ref, second_ref, gain_ref), directs = refs[:4], refs[4:8], refs[8:12]
    out_ref, bias_ref, value_ref = refs[12:]
    segment, tp = ids_ref[1], ids_ref[3]
    count = recvs[0].shape[0]
    rows = 2 * count
    piece_rows = rows // 8
    heads = own_ref.shape[1] // HEAD
    devices = out_ref.shape[0]
    wide = out_ref.shape[1] // 2
    scale = math.log2(math.e) / math.sqrt(HEAD)
    tail = tail_ref[:1, :].astype(jnp.int32)
    lane = iota((rows, wide), 1)
    keys_all = jnp.where(tp == 0, keep_ref[...], jnp.where(tp == 2, second_ref[...], first_ref[...]))
    value_ref[:, :HEAD] = jnp.where(tp == 3, keep_ref[...], jnp.where(tp == 1, second_ref[...], first_ref[...]))
    value_ref[:, HEAD:] = jnp.ones((2 * rows, HEAD), BF16)
    through = jnp.zeros((devices, wide), F32)
    direct = jnp.zeros((devices, wide), F32)
    for pack in range(2):
        def place(row):
            shard, inner = owner_of(row, pack, ids_ref, piece_rows)
            position = shard * piece_rows + inner
            end = jnp.zeros((1, 1), jnp.int32)
            doc = jnp.zeros_like(position)
            for index in range(lengths_ref.shape[1]):
                at = LENGTHS_AT + index
                end = end + jnp.where(segment == pack, lengths_ref[0, index], tail[:, at:at + 1])
                doc = doc + (position >= end).astype(jnp.int32)
            return position, doc

        row_position, row_doc = place(iota((rows, 1), 0))
        col_position, col_doc = place(iota((1, rows), 1))
        visible = jnp.logical_and(row_doc == col_doc, col_position <= row_position)
        bias_ref[...] = jnp.where(visible, 0.0, -1e30)
        keys = keys_all[pack * rows:(pack + 1) * rows]
        total = jnp.zeros((rows, HEAD), F32)
        for head in range(heads):
            at = slice(head * HEAD, (head + 1) * HEAD)
            parts = [own_ref[index * count:(index + 1) * count, at] + recv[:, at].astype(F32)
                     for index, recv in enumerate(recvs)]
            query = (by_pack(parts, pack) * scale).astype(BF16)
            logits = lax.dot_general(query, keys, (((1,), (1,)), ((), ())), preferred_element_type=F32)
            logits = logits + bias_ref[...]
            expo = jnp.exp2(logits - jnp.max(logits, axis=1, keepdims=True)).astype(BF16)
            both = jnp.dot(expo, value_ref[pack * rows:(pack + 1) * rows, :], preferred_element_type=F32)
            offset = pl.multiple_of(segment * heads * HEAD + head * HEAD, HEAD)
            total = total + both[:, :HEAD] / both[:, HEAD:] * gain_ref[:, pl.ds(offset, HEAD)].astype(F32)

        _, inner = owner_of(iota((rows, 1), 0), pack, ids_ref, piece_rows)
        shard_row, _ = owner_of(iota((1, rows), 1), pack, ids_ref, piece_rows)
        chosen = ((iota((devices, 1), 0) >> 2) == shard_row).astype(F32)
        hit = lane == inner + pack * piece_rows

        def send(column):
            return jnp.dot(chosen, jnp.where(hit, column, 0.0), precision=HIGHEST, preferred_element_type=F32)

        through = through + send(jnp.sum(total, axis=1, keepdims=True))
        direct = direct + send(jnp.sum(by_pack([ref[...] for ref in directs], pack), axis=1, keepdims=True))
    out_ref[:, :wide] = through
    out_ref[:, wide:] = direct


def attention(ids, lengths, tail, own, recvs, keep, first, second, gain, directs, devices):
    rows = own.shape[0] // 2
    return pl.pallas_call(
        attention_kernel,
        out_shape=jax.ShapeDtypeStruct((devices, 2 * LANES), F32),
        in_specs=[whole(pltpu.SMEM), whole(pltpu.SMEM)] + [whole()] * 14,
        out_specs=whole(),
        scratch_shapes=[
            pltpu.VMEM((rows, rows), F32),
            pltpu.VMEM((2 * rows, 2 * HEAD), BF16),
        ],
        compiler_params=pltpu.CompilerParams(vmem_limit_bytes=28 << 20),
        name="attend",
    )(ids, lengths, tail, own, *recvs, keep, first, second, gain, *directs)


def finish_kernel(recv_ref, send_ref, out_ref):
    models, count = out_ref.shape
    devices, width = recv_ref.shape
    model_of = iota((models, devices), 1) // (devices // models)
    chosen = (model_of == iota((models, devices), 0)).astype(F32)
    sums = jnp.dot(chosen, recv_ref[...], precision=HIGHEST, preferred_element_type=F32)
    pick = (iota((count, count), 0) == send_ref[...]).astype(F32)
    half = width // 2
    both = sums[:, :count] + sums[:, half:half + count]
    out_ref[...] = lax.dot_general(
        both, pick, (((1,), (1,)), ((), ())), precision=HIGHEST, preferred_element_type=F32)


def finish(recv, send, models):
    count = send.shape[1]
    return pl.pallas_call(
        finish_kernel,
        out_shape=jax.ShapeDtypeStruct((models, count), F32),
        in_specs=[whole()] * 2,
        out_specs=whole(),
        compiler_params=pltpu.CompilerParams(vmem_limit_bytes=8 << 20),
        name="finish",
    )(recv, send)


def paired(rollout, send_rows, seq_lengths, attn_gain, w_query, w_keyval, head_weight, head_attn):
    n_branch = lax.axis_size("branch")
    branch = lax.axis_index("branch")
    segment = lax.axis_index("segment")
    tp = lax.axis_index("tp")
    send = send_rows.reshape(1, -1)
    ids = jnp.stack([branch & 1, segment, branch >> 1, tp]).astype(jnp.int32)

    core_pairs = [(i, i ^ 1) for i in range(n_branch)]
    y_pairs = [(i, i ^ 2) for i in range(n_branch)]
    x_pairs = [(0, 1), (1, 0)]

    def swap(piece):
        return lax.ppermute(piece, "branch", core_pairs)

    def across(part):
        return lax.ppermute(part, "segment", x_pairs)

    def in_hbm(array):
        return pltpu.with_memory_space_constraint(array, pltpu.HBM)

    rollout, send, attn_gain, head_weight, seq_lengths = map(
        in_hbm, (rollout, send, attn_gain, head_weight, seq_lengths))
    wq, wkv = in_hbm(w_query[0]), in_hbm(w_keyval[0])
    mine, theirs = prepare(ids, seq_lengths, rollout, send)
    from_x = across(theirs)
    from_y = lax.ppermute(mine, "branch", y_pairs)
    from_d = lax.ppermute(from_x, "branch", y_pairs)

    rows, owns, directs, tails, received = [], [], [], [], []
    for name, piece in (("own", mine), ("x", from_x), ("y", from_y), ("d", from_d)):
        far = swap(piece)
        row, own, direct, tail, *sends = multiply_chunk(
            ids, piece, far, attn_gain, wkv, wq, head_weight, name == "d")
        for index, part in reversed(list(enumerate(sends))):
            sends[index] = across(part)
        rows.append(row)
        owns.append(own)
        directs.append(direct)
        tails.append(tail)
        received.append(sends)
    order = (1, 0, 3, 2)
    keep, first, second = sum_keyval(ids, owns, [received[index][-1] for index in order])
    first = lax.ppermute(first, "tp", [(0, 1), (2, 0), (1, 3), (3, 2)])
    second = lax.ppermute(second, "tp", [(2, 1), (1, 2)])
    own = own_queries(ids, rows, wq)
    devices = n_branch * 2 * lax.axis_size("tp")
    outgoing = attention(
        ids, seq_lengths, tails[1], own, [received[index][0] for index in order],
        keep, first, second, head_attn, directs, devices)
    incoming = lax.all_to_all(outgoing, ALL_AXES, split_axis=0, concat_axis=0, tiled=True)
    return finish(incoming, send, n_branch)


def general(rollout, send_rows, seq_lengths, attn_gain, w_query, w_keyval, head_weight, head_attn):
    n_branch = lax.axis_size("branch")
    n_segment = lax.axis_size("segment")
    gen_rows = rollout.shape[0]
    piece_rows = gen_rows // n_segment
    row_width = rollout.shape[1]
    ordered = jnp.take(rollout, send_rows, axis=0).reshape(n_segment, piece_rows, row_width)
    copies = jnp.broadcast_to(ordered[None], (n_branch, n_segment, piece_rows, row_width))
    copies = copies.reshape(n_branch * n_segment, piece_rows, row_width)
    arrived = lax.all_to_all(copies, ("branch", "segment"), split_axis=0, concat_axis=0, tiled=True)
    packed = arrived.reshape(-1, row_width)
    pack_rows = packed.shape[0]
    rows_float = packed.astype(jnp.float32)
    mean_square = jnp.mean(rows_float * rows_float, axis=-1, keepdims=True)
    normed = (
        rows_float * lax.rsqrt(mean_square + epsilon) * attn_gain[0].astype(jnp.float32)
    ).astype(jnp.bfloat16)
    query_acc = jnp.dot(
        normed,
        lax.all_gather(w_query, "segment", axis=1, tiled=True)[0],
        preferred_element_type=jnp.float32,
    )
    keyval_acc = jnp.dot(
        normed,
        lax.all_gather(w_keyval, "segment", axis=1, tiled=True)[0],
        preferred_element_type=jnp.float32,
    )
    queries = query_acc.astype(jnp.bfloat16)
    keyval_part = keyval_acc.astype(jnp.bfloat16)
    keyval = lax.all_gather(keyval_part, "tp", axis=1, tiled=True)
    tp_index = lax.axis_index("tp")
    heads_here = queries.shape[1] // HEAD
    group_size = HEADS // KV_HEADS
    per_group = min(heads_here, group_size)
    group_span = heads_here // per_group
    kv_first = tp_index * heads_here // group_size
    key_rows = lax.dynamic_slice_in_dim(keyval, kv_first * HEAD, group_span * HEAD, 1)
    value_rows = lax.dynamic_slice_in_dim(
        keyval, KV_HEADS * HEAD + kv_first * HEAD, group_span * HEAD, 1
    )
    key_rows = key_rows.reshape(pack_rows, group_span, HEAD)
    value_rows = value_rows.reshape(pack_rows, group_span, HEAD)
    queries = queries.reshape(pack_rows, group_span, per_group, HEAD)
    positions = jnp.arange(pack_rows, dtype=jnp.int32)
    doc_ends = jnp.cumsum(seq_lengths[0])
    doc_ids = jnp.sum((positions[:, None] >= doc_ends[None, :]).astype(jnp.int32), axis=-1)
    visible = (doc_ids[:, None] == doc_ids[None, :]) & (positions[None, :] <= positions[:, None])
    logits = jnp.einsum(
        "qgpc,kgc->gpqk", queries, key_rows, preferred_element_type=jnp.float32
    ) / math.sqrt(HEAD)
    logits = jnp.where(visible[None, None], logits, -1e30)
    row_max = jnp.max(logits, axis=-1, keepdims=True)
    expo = jnp.exp(logits - row_max)
    probabilities = (expo / jnp.sum(expo, axis=-1, keepdims=True)).astype(jnp.bfloat16)
    attended = jnp.einsum(
        "gpqk,kgc->qgpc", probabilities, value_rows, preferred_element_type=jnp.float32
    )
    attended = attended.reshape(pack_rows, heads_here * HEAD)
    slice_width = head_weight.shape[1]
    own_columns = lax.dynamic_slice_in_dim(packed, tp_index * slice_width, slice_width, 1)
    direct = jnp.dot(own_columns, head_weight[0], preferred_element_type=jnp.float32)
    through = jnp.dot(attended, head_attn[0].astype(jnp.float32), precision=lax.Precision.HIGHEST)
    totals = lax.psum(direct + through, "tp")
    outgoing = totals.reshape(n_branch * n_segment, piece_rows)
    incoming = lax.all_to_all(
        outgoing, ("branch", "segment"), split_axis=0, concat_axis=0, tiled=True
    )
    incoming = incoming.reshape(n_branch, n_segment * piece_rows)
    scores = jnp.zeros((n_branch, gen_rows), jnp.float32).at[:, send_rows].set(incoming)
    return scores


def solution(mesh):
    sizes = tuple(mesh.shape[axis] for axis in ALL_AXES)
    pairwise = sizes == (4, 2, 4)
    local = paired if pairwise else general
    return jax.shard_map(
        local,
        mesh=mesh,
        in_specs=(
            P(("branch", "segment"), None),
            P(("branch", "segment")),
            P("segment", None),
            P("branch", None),
            P("branch", "segment", "tp"),
            P("branch", "segment", "tp"),
            P("branch", "tp"),
            P("branch", "tp"),
        ),
        out_specs=P(None, ("branch", "segment")),
        check_vma=False,
    )
```

```python
import functools
import math

import jax
import jax.numpy as jnp
from jax import lax
from jax.experimental import pallas as pl
from jax.experimental.pallas import tpu as pltpu
from jax.sharding import PartitionSpec as P


HEAD = 128
HEADS = 64
KV_HEADS = 8
LANES = 128
LENGTHS_AT = 8

epsilon = 1e-05

ALL_AXES = ("branch", "segment", "tp")
HIGHEST = lax.Precision.HIGHEST
F32 = jnp.float32
BF16 = jnp.bfloat16


def whole(memory_space=pltpu.VMEM):
    return pl.BlockSpec(memory_space=memory_space)


def iota(shape, dimension):
    return lax.broadcasted_iota(jnp.int32, shape, dimension)


def prepare_kernel(ids_ref, lengths_ref, rows_hbm, send_hbm, mine_ref, theirs_ref, rows_ref, send_ref, sems):
    count, width = rows_ref.shape
    half = width // 2
    parts = sems.shape[0] - 1
    step = width // parts
    core, segment = ids_ref[0], ids_ref[1]
    copies = [pltpu.make_async_copy(send_hbm, send_ref, sems.at[parts])]
    for part in range(parts):
        at = pl.ds(part * step, step)
        copies.append(pltpu.make_async_copy(rows_hbm.at[:, at], rows_ref.at[:, at], sems.at[part]))
    for copy in copies:
        copy.start()
    copies[0].wait()
    send = send_ref[...]
    rolled = jnp.concatenate([send[:, count // 2:], send[:, :count // 2]], axis=1)
    order = jnp.where(core == 1, rolled, send)
    pick = (iota((count, count), 0) == order).astype(BF16)

    def ordered(part):
        out = lax.dot_general(pick, part, (((0,), (0,)), ((), ())), preferred_element_type=F32)
        return out.astype(BF16)

    lanes = jnp.zeros((count, LANES), F32)
    for part in range(parts):
        copies[1 + part].wait()
        square = rows_ref[:, part * step:(part + 1) * step].astype(F32)
        square = square * square
        for lane in range(0, step, LANES):
            lanes = lanes + square[:, lane:lane + LANES]
    chunk = 1024
    for start in range(0, half, chunk):
        for out_ref, which in ((theirs_ref, 1 - segment), (mine_ref, segment)):
            at = pl.multiple_of(which * half + start, chunk)
            out_ref[:, start:start + chunk] = ordered(rows_ref[:, pl.ds(at, chunk)])
    scale = lax.rsqrt(jnp.sum(lanes, axis=1, keepdims=True) * (1.0 / width) + epsilon)
    high = scale.astype(BF16).astype(F32)
    middle = (scale - high).astype(BF16).astype(F32)
    low = scale - high - middle
    lane = iota((count, LANES), 1)
    tail = jnp.where(lane == 0, high, jnp.where(lane == 1, middle, jnp.where(lane == 2, low, 0.0)))
    tail = ordered(tail.astype(BF16))
    for index in range(lengths_ref.shape[1]):
        length = lengths_ref[0, index].astype(F32).astype(BF16)
        tail = jnp.where(lane == LENGTHS_AT + index, length, tail)
    theirs_ref[:, half:] = tail
    mine_ref[:, half:] = tail


def prepare(ids, lengths, rows, send):
    count, width = rows.shape
    shape = jax.ShapeDtypeStruct((count, width // 2 + LANES), BF16)
    return pl.pallas_call(
        prepare_kernel,
        out_shape=(shape, shape),
        in_specs=[whole(pltpu.SMEM), whole(pltpu.SMEM), whole(pltpu.HBM), whole(pltpu.HBM)],
        out_specs=(whole(), whole()),
        scratch_shapes=[
            pltpu.VMEM((count, width), BF16),
            pltpu.VMEM((1, count), jnp.int32),
            pltpu.SemaphoreType.DMA((5,)),
        ],
        compiler_params=pltpu.CompilerParams(vmem_limit_bytes=12 << 20),
        name="prepare",
    )(ids, lengths, rows, send)


def chunk_kernel(ids_ref, *refs, chips, sends):
    pieces, refs = refs[:2 * chips], refs[2 * chips:]
    gain_hbm, keyval_hbm, query_hbm, head_hbm = refs[:4]
    rows_ref, own_ref, direct_ref, tail_ref = refs[4:8]
    send_refs = refs[8:8 + sends]
    gain_ref, keyval_ref, query_ref, head_ref, sems = refs[8 + sends:]
    count = pieces[0].shape[0]
    half = rows_ref.shape[1]
    blocks, _, block = query_ref.shape
    core, segment, tp = ids_ref[0], ids_ref[1], ids_ref[3]
    columns = blocks * block
    gain_copy = pltpu.make_async_copy(
        gain_hbm.at[:, pl.ds(pl.multiple_of(segment * half, half), half)], gain_ref, sems.at[0])
    head_copy = pltpu.make_async_copy(head_hbm, head_ref, sems.at[1])
    keyval_copy = pltpu.make_async_copy(keyval_hbm, keyval_ref, sems.at[2])
    gain_copy.start()
    head_copy.start()
    keyval_copy.start()
    query_copies = []
    for index in range(blocks):
        at = pl.multiple_of((1 - segment) * columns + index * block, block)
        query_copies.append(pltpu.make_async_copy(
            query_hbm.at[:, pl.ds(at, block)], query_ref.at[index], sems.at[3 + index]))
        query_copies[-1].start()

    top = (iota((count, 1), 0) < count // 2).astype(jnp.int32)
    mask = (top ^ core) == 1

    def sorted_rows(values):
        near, far = values[0::2], values[1::2]
        return jnp.concatenate(
            [part for n, f in zip(near, far) for part in (jnp.where(mask, n, f), jnp.where(mask, f, n))], axis=0)

    first_lanes = iota((count, LANES), 1) < 3
    scale = sorted_rows([
        jnp.sum(jnp.where(first_lanes, ref[:, half:].astype(F32), 0.0), axis=1, keepdims=True) for ref in pieces])
    slice_width = head_ref.shape[1]
    holder = (tp * slice_width) // half == segment
    first = (tp * slice_width) % half
    chunk = 512
    direct = jnp.zeros((2 * chips * count, LANES), F32)
    gain_copy.wait()
    head_copy.wait()
    for start in range(0, half, chunk):
        at = slice(start, start + chunk)
        rows = sorted_rows([ref[:, at].astype(F32) for ref in pieces])
        inside = jnp.logical_and(holder, jnp.logical_and(start >= first, start < first + slice_width))
        offset = pl.multiple_of(jnp.where(inside, start - first, 0), chunk)
        weight = jnp.where(inside, head_ref[:, pl.ds(offset, chunk)].astype(F32), 0.0)
        for lane in range(0, chunk, LANES):
            direct = direct + rows[:, lane:lane + LANES] * weight[:, lane:lane + LANES]
        rows_ref[:, at] = (rows * scale * gain_ref[:, at].astype(F32)).astype(BF16)
    direct_ref[...] = direct
    tail_ref[...] = pieces[0][:, half:].astype(F32)[:8]

    keyval_copy.wait()
    keyval = jnp.dot(rows_ref[...], keyval_ref[...], preferred_element_type=F32)
    even = jnp.concatenate([keyval[:, :HEAD], keyval[:, 2 * HEAD:3 * HEAD]], axis=1)
    odd = jnp.concatenate([keyval[:, HEAD:2 * HEAD], keyval[:, 3 * HEAD:]], axis=1)
    own_ref[...] = jnp.where(segment == 0, even, odd)
    other = jnp.where(segment == 0, odd, even).astype(BF16)
    if sends == 1:
        send_refs[0][:, columns:] = other
    else:
        send_refs[1][...] = other
    for index in range(blocks):
        query_copies[index].wait()
        send_refs[0][:, index * block:(index + 1) * block] = jnp.dot(
            rows_ref[...], query_ref[index], preferred_element_type=F32).astype(BF16)


def multiply_chunk(ids, pieces, gain, keyval, query, head, split):
    count, wide = pieces[0].shape
    half = wide - LANES
    columns = query.shape[1] // 2
    block = 256
    blocks = columns // block
    chips = len(pieces) // 2
    rows = 2 * chips * count
    widths = (columns, 2 * HEAD) if split else (columns + 2 * HEAD,)
    return pl.pallas_call(
        functools.partial(chunk_kernel, chips=chips, sends=len(widths)),
        out_shape=(
            jax.ShapeDtypeStruct((rows, half), BF16),
            jax.ShapeDtypeStruct((rows, 2 * HEAD), F32),
            jax.ShapeDtypeStruct((rows, LANES), F32),
            jax.ShapeDtypeStruct((8, LANES), F32),
        ) + tuple(jax.ShapeDtypeStruct((rows, width), BF16) for width in widths),
        in_specs=[whole(pltpu.SMEM)] + [whole()] * len(pieces) + [whole(pltpu.HBM)] * 4,
        out_specs=(whole(),) * (4 + len(widths)),
        scratch_shapes=[
            pltpu.VMEM((1, half), BF16),
            pltpu.VMEM(keyval.shape, BF16),
            pltpu.VMEM((blocks, half, block), BF16),
            pltpu.VMEM(head.shape, BF16),
            pltpu.SemaphoreType.DMA((3 + blocks,)),
        ],
        compiler_params=pltpu.CompilerParams(vmem_limit_bytes=32 << 20),
        cost_estimate=pl.CostEstimate(
            flops=2 * rows * half * (columns + keyval.shape[1]), transcendentals=0,
            bytes_accessed=2 * half * (columns + keyval.shape[1])),
        name="chunk",
    )(ids, *pieces, gain, keyval, query, head)


def own_kernel(ids_ref, rows_ref, query_hbm, out_ref, query_ref, sems):
    blocks, _, block = query_ref.shape
    columns = blocks * block
    copies = []
    for index in range(blocks):
        at = pl.multiple_of(ids_ref[1] * columns + index * block, block)
        copies.append(pltpu.make_async_copy(query_hbm.at[:, pl.ds(at, block)], query_ref.at[index], sems.at[index]))
        copies[-1].start()
    for index in range(blocks):
        copies[index].wait()
        out_ref[:, index * block:(index + 1) * block] = jnp.dot(
            rows_ref[...], query_ref[index], preferred_element_type=F32)


def own_queries(ids, rows, query):
    count, half = rows.shape
    columns = query.shape[1] // 2
    block = 256
    blocks = columns // block
    return pl.pallas_call(
        own_kernel,
        out_shape=jax.ShapeDtypeStruct((count, columns), F32),
        in_specs=[whole(pltpu.SMEM), whole(), whole(pltpu.HBM)],
        out_specs=whole(),
        scratch_shapes=[
            pltpu.VMEM((blocks, half, block), BF16),
            pltpu.SemaphoreType.DMA((blocks,)),
        ],
        compiler_params=pltpu.CompilerParams(vmem_limit_bytes=20 << 20),
        cost_estimate=pl.CostEstimate(
            flops=2 * count * half * columns, transcendentals=0, bytes_accessed=2 * half * columns),
        name="own_queries",
    )(ids, rows, query)


def slabs(refs, starts, count, at=slice(None)):
    return [ref[start:start + count, at].astype(F32) for ref, start in zip(refs, starts)]


def by_pack(parts, pack):
    count = parts[0].shape[0] // 2
    return jnp.concatenate([part[pack * count:(pack + 1) * count] for part in parts], axis=0)


def keyval_kernel(ids_ref, *refs, starts, recv_starts):
    chips = len(starts)
    owns, recvs = refs[:chips], refs[chips:2 * chips]
    keep_ref, first_ref, second_ref = refs[2 * chips:]
    tp = ids_ref[3]
    count = keep_ref.shape[0] // chips
    mine = slabs(owns, starts, count)
    theirs = [slabs((ref,), (start,), count, slice(ref.shape[1] - 2 * HEAD, ref.shape[1]))[0]
              for ref, start in zip(recvs, recv_starts)]
    sums = [own + recv for own, recv in zip(mine, theirs)]
    both = jnp.concatenate([by_pack(sums, pack) for pack in range(2)], axis=0)
    low, high = both[:, :HEAD], both[:, HEAD:]
    keep_ref[...] = jnp.where(tp == 3, high, low).astype(BF16)
    first_ref[...] = jnp.where(tp < 2, high, low).astype(BF16)
    second_ref[...] = jnp.where(tp == 2, high, low).astype(BF16)


def sum_keyval(ids, owns, starts, recvs, recv_starts, count):
    shape = jax.ShapeDtypeStruct((len(owns) * count, HEAD), BF16)
    return pl.pallas_call(
        functools.partial(keyval_kernel, starts=starts, recv_starts=recv_starts),
        out_shape=(shape, shape, shape),
        in_specs=[whole(pltpu.SMEM)] + [whole()] * (2 * len(owns)),
        out_specs=(whole(),) * 3,
        compiler_params=pltpu.CompilerParams(vmem_limit_bytes=8 << 20),
        name="sum_keyval",
    )(ids, *owns, *recvs)


def owner_of(row, pack, ids_ref, piece_rows):
    index = jnp.zeros_like(row)
    for step in range(1, 8):
        index = index + (row >= step * piece_rows).astype(jnp.int32)
    slot, low = index >> 1, index & 1
    chip = slot ^ (slot >> 1)
    shard = (((chip >> 1) ^ ids_ref[2]) * 2 + (low ^ pack)) * 2 + ((chip & 1) ^ ids_ref[1])
    return shard, row - index * piece_rows


def attention_kernel(ids_ref, lengths_ref, tail_ref, *refs, slot, starts, recv_starts, more):
    chips = len(starts)
    owns, recvs, directs = (refs[index * chips:(index + 1) * chips] for index in range(3))
    refs = refs[3 * chips:]
    firsts, lates, gain_ref = refs[0:3], refs[3:6], refs[6]
    before_ref = refs[7] if more else None
    out_ref, bias_ref = refs[7 + more:]
    segment, tp = ids_ref[1], ids_ref[3]
    rows = bias_ref.shape[1]
    slab = rows // 2
    queries = bias_ref.shape[0]
    base = slot * (slab // 2)
    piece_rows = rows // 8
    heads = owns[0].shape[1] // HEAD
    devices = out_ref.shape[0]
    wide = out_ref.shape[1] // 2
    scale = math.log2(math.e) / math.sqrt(HEAD)
    tail = tail_ref[:1, :].astype(jnp.int32)
    lane = iota((queries, wide), 1)

    def chosen_keys(refs):
        keep, first, second = (ref[...].astype(F32) for ref in refs)
        return (jnp.where(tp == 0, keep, jnp.where(tp == 2, second, first)),
                jnp.where(tp == 3, keep, jnp.where(tp == 1, second, first)))

    early, late = chosen_keys(firsts), chosen_keys(lates)
    through = jnp.zeros((devices, wide), F32)
    direct = jnp.zeros((devices, wide), F32)
    for pack in range(2):
        def place(row):
            shard, inner = owner_of(row, pack, ids_ref, piece_rows)
            position = shard * piece_rows + inner
            end = jnp.zeros((1, 1), jnp.int32)
            doc = jnp.zeros_like(position)
            for index in range(lengths_ref.shape[1]):
                at = LENGTHS_AT + index
                end = end + jnp.where(segment == pack, lengths_ref[0, index], tail[:, at:at + 1])
                doc = doc + (position >= end).astype(jnp.int32)
            return position, doc

        row_position, row_doc = place(iota((queries, 1), 0) + base)
        col_position, col_doc = place(iota((1, rows), 1))
        visible = jnp.logical_and(row_doc == col_doc, col_position <= row_position)
        bias_ref[...] = jnp.where(visible, 0.0, -1e30)
        keys, values = (
            jnp.concatenate([part[pack * (part.shape[0] // 2):(pack + 1) * (part.shape[0] // 2)]
                             for part in parts], axis=0).astype(BF16)
            for parts in zip(early, late))
        values = jnp.concatenate([values, jnp.ones((rows, HEAD), BF16)], axis=1)
        total = jnp.zeros((queries, HEAD), F32)
        for head in range(heads):
            at = slice(head * HEAD, (head + 1) * HEAD)
            parts = [own + recv for own, recv in zip(
                slabs(owns, starts, slab, at), slabs(recvs, recv_starts, slab, at))]
            query = (by_pack(parts, pack) * scale).astype(BF16)
            logits = lax.dot_general(query, keys, (((1,), (1,)), ((), ())), preferred_element_type=F32)
            logits = logits + bias_ref[...]
            expo = jnp.exp2(logits - jnp.max(logits, axis=1, keepdims=True)).astype(BF16)
            both = jnp.dot(expo, values, preferred_element_type=F32)
            offset = pl.multiple_of(segment * heads * HEAD + head * HEAD, HEAD)
            total = total + both[:, :HEAD] / both[:, HEAD:] * gain_ref[:, pl.ds(offset, HEAD)].astype(F32)

        _, inner = owner_of(iota((queries, 1), 0) + base, pack, ids_ref, piece_rows)
        shard_row, _ = owner_of(iota((1, queries), 1) + base, pack, ids_ref, piece_rows)
        chosen = ((iota((devices, 1), 0) >> 2) == shard_row).astype(F32)
        hit = lane == inner + pack * piece_rows

        def send(column):
            return jnp.dot(chosen, jnp.where(hit, column, 0.0), precision=HIGHEST, preferred_element_type=F32)

        through = through + send(jnp.sum(total, axis=1, keepdims=True))
        direct = direct + send(jnp.sum(by_pack(slabs(directs, starts, slab), pack), axis=1, keepdims=True))
    if more:
        through = through + before_ref[:, :wide]
        direct = direct + before_ref[:, wide:]
    out_ref[:, :wide] = through
    out_ref[:, wide:] = direct


def attention(ids, lengths, tail, owns, starts, recvs, recv_starts, directs, firsts, lates, gain, devices,
              slot, before):
    rows = firsts[0].shape[0] // 2 + lates[0].shape[0] // 2
    queries = len(owns) * (rows // 4)
    return pl.pallas_call(
        functools.partial(
            attention_kernel, slot=slot, starts=starts, recv_starts=recv_starts, more=len(before)),
        out_shape=jax.ShapeDtypeStruct((devices, 2 * LANES), F32),
        in_specs=[whole(pltpu.SMEM), whole(pltpu.SMEM)] + [whole()] * (8 + 3 * len(owns) + len(before)),
        out_specs=whole(),
        scratch_shapes=[pltpu.VMEM((queries, rows), F32)],
        compiler_params=pltpu.CompilerParams(vmem_limit_bytes=24 << 20),
        name="attend",
    )(ids, lengths, tail, *owns, *recvs, *directs, *firsts, *lates, gain, *before)


def finish_kernel(recv_ref, send_ref, out_ref):
    models, count = out_ref.shape
    devices, width = recv_ref.shape
    model_of = iota((models, devices), 1) // (devices // models)
    chosen = (model_of == iota((models, devices), 0)).astype(F32)
    sums = jnp.dot(chosen, recv_ref[...], precision=HIGHEST, preferred_element_type=F32)
    pick = (iota((count, count), 0) == send_ref[...]).astype(F32)
    half = width // 2
    both = sums[:, :count] + sums[:, half:half + count]
    out_ref[...] = lax.dot_general(
        both, pick, (((1,), (1,)), ((), ())), precision=HIGHEST, preferred_element_type=F32)


def finish(recv, send, models):
    count = send.shape[1]
    return pl.pallas_call(
        finish_kernel,
        out_shape=jax.ShapeDtypeStruct((models, count), F32),
        in_specs=[whole()] * 2,
        out_specs=whole(),
        compiler_params=pltpu.CompilerParams(vmem_limit_bytes=8 << 20),
        name="finish",
    )(recv, send)


def paired(rollout, send_rows, seq_lengths, attn_gain, w_query, w_keyval, head_weight, head_attn):
    n_branch = lax.axis_size("branch")
    branch = lax.axis_index("branch")
    segment = lax.axis_index("segment")
    tp = lax.axis_index("tp")
    send = send_rows.reshape(1, -1)
    ids = jnp.stack([branch & 1, segment, branch >> 1, tp]).astype(jnp.int32)

    core_pairs = [(i, i ^ 1) for i in range(n_branch)]
    y_pairs = [(i, i ^ 2) for i in range(n_branch)]
    x_pairs = [(0, 1), (1, 0)]

    def swap(piece):
        return lax.ppermute(piece, "branch", core_pairs)

    def across(part):
        return lax.ppermute(part, "segment", x_pairs)

    def in_hbm(array):
        return pltpu.with_memory_space_constraint(array, pltpu.HBM)

    packing = send
    rollout, send, attn_gain, head_weight, seq_lengths = map(
        in_hbm, (rollout, send, attn_gain, head_weight, seq_lengths))
    wq, wkv = in_hbm(w_query[0]), in_hbm(w_keyval[0])
    mine, theirs = prepare(ids, seq_lengths, rollout, send)
    from_x = across(theirs)
    from_y = lax.ppermute(mine, "branch", y_pairs)
    from_d = lax.ppermute(from_x, "branch", y_pairs)

    slab = 2 * mine.shape[0]
    local, direct, query, received = {}, {}, {}, {}
    for name, pieces in (("own", (mine,)), ("xy", (from_x, from_y)), ("d", (from_d,))):
        pieces = [part for piece in pieces for part in (piece, swap(piece))]
        rows, local[name], direct[name], lengths, *sends = multiply_chunk(
            ids, pieces, attn_gain, wkv, wq, head_weight, name != "own")
        if name == "xy":
            tail = lengths
        for index, part in reversed(list(enumerate(sends))):
            sends[index] = across(part)
        received[name] = sends
        query[name] = own_queries(ids, rows, wq)

    keep, first, second = sum_keyval(
        ids, [local["own"], local["xy"], local["d"]], (0, 0, 0),
        [received["xy"][1], received["own"][0], received["xy"][1]], (0, 0, slab), slab)
    hand_first, hand_second = [(0, 1), (2, 0), (1, 3), (3, 2)], [(2, 1), (1, 2)]
    first = lax.ppermute(first, "tp", hand_first)
    second = lax.ppermute(second, "tp", hand_second)
    early = (keep, first, second)
    keep, first, second = sum_keyval(
        ids, [local["xy"]], (slab,), [received["d"][1]], (0,), slab)
    first = lax.ppermute(first, "tp", hand_first)
    second = lax.ppermute(second, "tp", hand_second)
    late = (keep, first, second)
    devices = n_branch * 2 * lax.axis_size("tp")
    outgoing = attention(
        ids, seq_lengths, tail, [query["own"], query["xy"], query["d"]], (0, 0, 0),
        [received["xy"][0], received["own"][0], received["xy"][0]], (0, 0, slab),
        [direct["own"], direct["xy"], direct["d"]], early, late, head_attn, devices, 0, [])
    outgoing = attention(
        ids, seq_lengths, tail, [query["xy"]], (slab,), [received["d"][0]], (0,),
        [direct["xy"]], early, late, head_attn, devices, 3, [outgoing])
    incoming = lax.all_to_all(outgoing, ALL_AXES, split_axis=0, concat_axis=0, tiled=True)
    return finish(incoming, packing, n_branch)


def general(rollout, send_rows, seq_lengths, attn_gain, w_query, w_keyval, head_weight, head_attn):
    n_branch = lax.axis_size("branch")
    n_segment = lax.axis_size("segment")
    gen_rows = rollout.shape[0]
    piece_rows = gen_rows // n_segment
    row_width = rollout.shape[1]
    ordered = jnp.take(rollout, send_rows, axis=0).reshape(n_segment, piece_rows, row_width)
    copies = jnp.broadcast_to(ordered[None], (n_branch, n_segment, piece_rows, row_width))
    copies = copies.reshape(n_branch * n_segment, piece_rows, row_width)
    arrived = lax.all_to_all(copies, ("branch", "segment"), split_axis=0, concat_axis=0, tiled=True)
    packed = arrived.reshape(-1, row_width)
    pack_rows = packed.shape[0]
    rows_float = packed.astype(jnp.float32)
    mean_square = jnp.mean(rows_float * rows_float, axis=-1, keepdims=True)
    normed = (
        rows_float * lax.rsqrt(mean_square + epsilon) * attn_gain[0].astype(jnp.float32)
    ).astype(jnp.bfloat16)
    query_acc = jnp.dot(
        normed,
        lax.all_gather(w_query, "segment", axis=1, tiled=True)[0],
        preferred_element_type=jnp.float32,
    )
    keyval_acc = jnp.dot(
        normed,
        lax.all_gather(w_keyval, "segment", axis=1, tiled=True)[0],
        preferred_element_type=jnp.float32,
    )
    queries = query_acc.astype(jnp.bfloat16)
    keyval_part = keyval_acc.astype(jnp.bfloat16)
    keyval = lax.all_gather(keyval_part, "tp", axis=1, tiled=True)
    tp_index = lax.axis_index("tp")
    heads_here = queries.shape[1] // HEAD
    group_size = HEADS // KV_HEADS
    per_group = min(heads_here, group_size)
    group_span = heads_here // per_group
    kv_first = tp_index * heads_here // group_size
    key_rows = lax.dynamic_slice_in_dim(keyval, kv_first * HEAD, group_span * HEAD, 1)
    value_rows = lax.dynamic_slice_in_dim(
        keyval, KV_HEADS * HEAD + kv_first * HEAD, group_span * HEAD, 1
    )
    key_rows = key_rows.reshape(pack_rows, group_span, HEAD)
    value_rows = value_rows.reshape(pack_rows, group_span, HEAD)
    queries = queries.reshape(pack_rows, group_span, per_group, HEAD)
    positions = jnp.arange(pack_rows, dtype=jnp.int32)
    doc_ends = jnp.cumsum(seq_lengths[0])
    doc_ids = jnp.sum((positions[:, None] >= doc_ends[None, :]).astype(jnp.int32), axis=-1)
    visible = (doc_ids[:, None] == doc_ids[None, :]) & (positions[None, :] <= positions[:, None])
    logits = jnp.einsum(
        "qgpc,kgc->gpqk", queries, key_rows, preferred_element_type=jnp.float32
    ) / math.sqrt(HEAD)
    logits = jnp.where(visible[None, None], logits, -1e30)
    row_max = jnp.max(logits, axis=-1, keepdims=True)
    expo = jnp.exp(logits - row_max)
    probabilities = (expo / jnp.sum(expo, axis=-1, keepdims=True)).astype(jnp.bfloat16)
    attended = jnp.einsum(
        "gpqk,kgc->qgpc", probabilities, value_rows, preferred_element_type=jnp.float32
    )
    attended = attended.reshape(pack_rows, heads_here * HEAD)
    slice_width = head_weight.shape[1]
    own_columns = lax.dynamic_slice_in_dim(packed, tp_index * slice_width, slice_width, 1)
    direct = jnp.dot(own_columns, head_weight[0], preferred_element_type=jnp.float32)
    through = jnp.dot(attended, head_attn[0].astype(jnp.float32), precision=lax.Precision.HIGHEST)
    totals = lax.psum(direct + through, "tp")
    outgoing = totals.reshape(n_branch * n_segment, piece_rows)
    incoming = lax.all_to_all(
        outgoing, ("branch", "segment"), split_axis=0, concat_axis=0, tiled=True
    )
    incoming = incoming.reshape(n_branch, n_segment * piece_rows)
    scores = jnp.zeros((n_branch, gen_rows), jnp.float32).at[:, send_rows].set(incoming)
    return scores


def solution(mesh):
    sizes = tuple(mesh.shape[axis] for axis in ALL_AXES)
    pairwise = sizes == (4, 2, 4)
    local = paired if pairwise else general
    return jax.shard_map(
        local,
        mesh=mesh,
        in_specs=(
            P(("branch", "segment"), None),
            P(("branch", "segment")),
            P("segment", None),
            P("branch", None),
            P("branch", "segment", "tp"),
            P("branch", "segment", "tp"),
            P("branch", "tp"),
            P("branch", "tp"),
        ),
        out_specs=P(None, ("branch", "segment")),
        check_vma=False,
    )
```

```python
import functools
import math

import jax
import jax.numpy as jnp
from jax import lax
from jax.experimental import pallas as pl
from jax.experimental.pallas import tpu as pltpu
from jax.sharding import PartitionSpec as P


HEAD = 128
HEADS = 64
KV_HEADS = 8
LANES = 128
LENGTHS_AT = 8

epsilon = 1e-05

ALL_AXES = ("branch", "segment", "tp")
HIGHEST = lax.Precision.HIGHEST
F32 = jnp.float32
BF16 = jnp.bfloat16


def whole(memory_space=pltpu.VMEM):
    return pl.BlockSpec(memory_space=memory_space)


def iota(shape, dimension):
    return lax.broadcasted_iota(jnp.int32, shape, dimension)


def prepare_kernel(ids_ref, lengths_ref, rows_hbm, send_hbm, mine_ref, theirs_ref, rows_ref, send_ref, sems):
    count, width = rows_ref.shape
    half = width // 2
    parts = sems.shape[0] - 1
    step = width // parts
    core, segment = ids_ref[0], ids_ref[1]
    copies = [pltpu.make_async_copy(send_hbm, send_ref, sems.at[parts])]
    for part in range(parts):
        at = pl.ds(part * step, step)
        copies.append(pltpu.make_async_copy(rows_hbm.at[:, at], rows_ref.at[:, at], sems.at[part]))
    for copy in copies:
        copy.start()
    copies[0].wait()
    send = send_ref[...]
    rolled = jnp.concatenate([send[:, count // 2:], send[:, :count // 2]], axis=1)
    order = jnp.where(core == 1, rolled, send)
    pick = (iota((count, count), 0) == order).astype(BF16)

    def ordered(part):
        out = lax.dot_general(pick, part, (((0,), (0,)), ((), ())), preferred_element_type=F32)
        return out.astype(BF16)

    lanes = jnp.zeros((count, LANES), F32)
    for part in range(parts):
        copies[1 + part].wait()
        square = rows_ref[:, part * step:(part + 1) * step].astype(F32)
        square = square * square
        for lane in range(0, step, LANES):
            lanes = lanes + square[:, lane:lane + LANES]
    chunk = 1024
    for start in range(0, half, chunk):
        for out_ref, which in ((theirs_ref, 1 - segment), (mine_ref, segment)):
            at = pl.multiple_of(which * half + start, chunk)
            out_ref[:, start:start + chunk] = ordered(rows_ref[:, pl.ds(at, chunk)])
    scale = lax.rsqrt(jnp.sum(lanes, axis=1, keepdims=True) * (1.0 / width) + epsilon)
    high = scale.astype(BF16).astype(F32)
    middle = (scale - high).astype(BF16).astype(F32)
    low = scale - high - middle
    lane = iota((count, LANES), 1)
    tail = jnp.where(lane == 0, high, jnp.where(lane == 1, middle, jnp.where(lane == 2, low, 0.0)))
    tail = ordered(tail.astype(BF16))
    for index in range(lengths_ref.shape[1]):
        length = lengths_ref[0, index].astype(F32).astype(BF16)
        tail = jnp.where(lane == LENGTHS_AT + index, length, tail)
    theirs_ref[:, half:] = tail
    mine_ref[:, half:] = tail


def prepare(ids, lengths, rows, send):
    count, width = rows.shape
    shape = jax.ShapeDtypeStruct((count, width // 2 + LANES), BF16)
    return pl.pallas_call(
        prepare_kernel,
        out_shape=(shape, shape),
        in_specs=[whole(pltpu.SMEM), whole(pltpu.SMEM), whole(pltpu.HBM), whole(pltpu.HBM)],
        out_specs=(whole(), whole()),
        scratch_shapes=[
            pltpu.VMEM((count, width), BF16),
            pltpu.VMEM((1, count), jnp.int32),
            pltpu.SemaphoreType.DMA((5,)),
        ],
        compiler_params=pltpu.CompilerParams(vmem_limit_bytes=12 << 20),
        name="prepare",
    )(ids, lengths, rows, send)


BLOCK = 256


def column_copies(source, first, target, sems):
    blocks = target.shape[1] // BLOCK
    return [
        pltpu.make_async_copy(
            source.at[:, pl.ds(pl.multiple_of(first + index * BLOCK, BLOCK), BLOCK)],
            target.at[:, pl.ds(index * BLOCK, BLOCK)], sems.at[index])
        for index in range(blocks)]


def chunk_body(ids_ref, pieces, gain_ref, head_ref, keyval_ref, query_ref, outs, waits):
    rows_ref, own_ref, direct_ref, tail_ref = outs[:4]
    sends = outs[4:]
    count = pieces[0].shape[0]
    half = rows_ref.shape[1]
    core, segment = ids_ref[0], ids_ref[1]
    columns = query_ref.shape[1]
    top = (iota((count, 1), 0) < count // 2).astype(jnp.int32)
    mask = (top ^ core) == 1

    def sorted_rows(values):
        near, far = values[0::2], values[1::2]
        return jnp.concatenate(
            [part for n, f in zip(near, far) for part in (jnp.where(mask, n, f), jnp.where(mask, f, n))], axis=0)

    first_lanes = iota((count, LANES), 1) < 3
    scale = sorted_rows([
        jnp.sum(jnp.where(first_lanes, ref[:, half:].astype(F32), 0.0), axis=1, keepdims=True) for ref in pieces])
    chunk = 512
    direct = jnp.zeros((direct_ref.shape[0], LANES), F32)
    for start in range(0, half, chunk):
        at = slice(start, start + chunk)
        rows = sorted_rows([ref[:, at].astype(F32) for ref in pieces])
        weight = head_ref[:, at].astype(F32)
        for lane in range(0, chunk, LANES):
            direct = direct + rows[:, lane:lane + LANES] * weight[:, lane:lane + LANES]
        rows_ref[:, at] = (rows * scale * gain_ref[:, at].astype(F32)).astype(BF16)
    direct_ref[...] = direct
    tail_ref[...] = pieces[0][:, half:].astype(F32)[:8]

    for wait in waits[:keyval_ref.shape[1] // BLOCK]:
        wait()
    keyval = jnp.dot(rows_ref[...], keyval_ref[...], preferred_element_type=F32)
    even = jnp.concatenate([keyval[:, :HEAD], keyval[:, 2 * HEAD:3 * HEAD]], axis=1)
    odd = jnp.concatenate([keyval[:, HEAD:2 * HEAD], keyval[:, 3 * HEAD:]], axis=1)
    own_ref[...] = jnp.where(segment == 0, even, odd)
    other = jnp.where(segment == 0, odd, even).astype(BF16)
    if len(sends) == 1:
        sends[0][:, columns:] = other
    else:
        sends[1][...] = other
    waits = waits[keyval_ref.shape[1] // BLOCK:]
    for index in range(columns // BLOCK):
        if waits:
            waits[index]()
        at = slice(index * BLOCK, (index + 1) * BLOCK)
        sends[0][:, at] = jnp.dot(rows_ref[...], query_ref[:, at], preferred_element_type=F32).astype(BF16)


def first_chunk_kernel(ids_ref, near_ref, far_ref, gain_hbm, head_hbm, keyval_hbm, query_hbm, *refs):
    outs, (gain_ref, head_ref, keyval_ref, query_ref), (part_ref, small_sems, sems) = refs[:5], refs[5:9], refs[9:]
    half = outs[0].shape[1]
    segment, tp = ids_ref[1], ids_ref[3]
    small = [
        pltpu.make_async_copy(
            gain_hbm.at[:, pl.ds(pl.multiple_of(segment * half, half), half)], gain_ref, small_sems.at[0]),
        pltpu.make_async_copy(head_hbm, part_ref, small_sems.at[1]),
    ]
    blocks = keyval_ref.shape[1] // BLOCK
    large = column_copies(keyval_hbm, 0, keyval_ref, sems)
    large += column_copies(query_hbm, (1 - segment) * query_ref.shape[1], query_ref, sems.at[pl.ds(blocks, query_ref.shape[1] // BLOCK)])
    for copy in small + large:
        copy.start()
    for copy in small:
        copy.wait()
    width = part_ref.shape[1]
    head_ref[...] = jnp.zeros_like(head_ref)

    @pl.when((tp * width) // half == segment)
    def _():
        head_ref[:, pl.ds(pl.multiple_of((tp * width) % half, width), width)] = part_ref[...]

    chunk_body(ids_ref, (near_ref, far_ref), gain_ref, head_ref, keyval_ref, query_ref, outs,
               [copy.wait for copy in large])


def next_chunk_kernel(ids_ref, *refs, chips):
    pieces, refs = refs[:2 * chips], refs[2 * chips:]
    chunk_body(ids_ref, pieces, *refs[:4], refs[4:], [])


def chunk_shapes(rows, half, widths):
    return (
        jax.ShapeDtypeStruct((rows, half), BF16),
        jax.ShapeDtypeStruct((rows, 2 * HEAD), F32),
        jax.ShapeDtypeStruct((rows, LANES), F32),
        jax.ShapeDtypeStruct((8, LANES), F32),
    ) + tuple(jax.ShapeDtypeStruct((rows, width), BF16) for width in widths)


def first_chunk(ids, near, far, gain, head, keyval, query):
    count, wide = near.shape
    half = wide - LANES
    columns = query.shape[1] // 2
    shapes = chunk_shapes(2 * count, half, (columns + 2 * HEAD,)) + tuple(
        jax.ShapeDtypeStruct(shape, BF16) for shape in ((1, half), (1, half), keyval.shape, (half, columns)))
    out = pl.pallas_call(
        first_chunk_kernel,
        out_shape=shapes,
        in_specs=[whole(pltpu.SMEM), whole(), whole()] + [whole(pltpu.HBM)] * 4,
        out_specs=(whole(),) * len(shapes),
        scratch_shapes=[
            pltpu.VMEM(head.shape, BF16),
            pltpu.SemaphoreType.DMA((2,)),
            pltpu.SemaphoreType.DMA(((columns + keyval.shape[1]) // BLOCK,)),
        ],
        compiler_params=pltpu.CompilerParams(vmem_limit_bytes=24 << 20),
        name="first_chunk",
    )(ids, near, far, gain, head, keyval, query)
    return out[:5], out[5:]


def next_chunk(ids, pieces, weights):
    count, wide = pieces[0].shape
    chips = len(pieces) // 2
    shapes = chunk_shapes(2 * chips * count, wide - LANES, (weights[3].shape[1], 2 * HEAD))
    return pl.pallas_call(
        functools.partial(next_chunk_kernel, chips=chips),
        out_shape=shapes,
        in_specs=[whole(pltpu.SMEM)] + [whole()] * (len(pieces) + 4),
        out_specs=(whole(),) * len(shapes),
        compiler_params=pltpu.CompilerParams(vmem_limit_bytes=24 << 20),
        name="next_chunk",
    )(ids, *pieces, *weights)


def own_body(rows_ref, query_ref, out_ref, waits):
    for index in range(query_ref.shape[1] // BLOCK):
        if waits:
            waits[index]()
        at = slice(index * BLOCK, (index + 1) * BLOCK)
        out_ref[:, at] = jnp.dot(rows_ref[...], query_ref[:, at], preferred_element_type=F32)


def first_own_kernel(ids_ref, rows_ref, query_hbm, out_ref, query_ref, sems):
    copies = column_copies(query_hbm, ids_ref[1] * query_ref.shape[1], query_ref, sems)
    for copy in copies:
        copy.start()
    own_body(rows_ref, query_ref, out_ref, [copy.wait for copy in copies])


def next_own_kernel(rows_ref, query_ref, out_ref):
    own_body(rows_ref, query_ref, out_ref, [])


def first_own(ids, rows, query):
    count, half = rows.shape
    columns = query.shape[1] // 2
    return pl.pallas_call(
        first_own_kernel,
        out_shape=(
            jax.ShapeDtypeStruct((count, columns), F32),
            jax.ShapeDtypeStruct((half, columns), BF16),
        ),
        in_specs=[whole(pltpu.SMEM), whole(), whole(pltpu.HBM)],
        out_specs=(whole(), whole()),
        scratch_shapes=[pltpu.SemaphoreType.DMA((columns // BLOCK,))],
        compiler_params=pltpu.CompilerParams(vmem_limit_bytes=16 << 20),
        name="first_own",
    )(ids, rows, query)


def next_own(rows, query):
    return pl.pallas_call(
        next_own_kernel,
        out_shape=jax.ShapeDtypeStruct((rows.shape[0], query.shape[1]), F32),
        in_specs=[whole(), whole()],
        out_specs=whole(),
        compiler_params=pltpu.CompilerParams(vmem_limit_bytes=16 << 20),
        name="next_own",
    )(rows, query)


def slabs(refs, starts, count, at=slice(None)):
    return [ref[start:start + count, at].astype(F32) for ref, start in zip(refs, starts)]


def by_pack(parts, pack):
    count = parts[0].shape[0] // 2
    return jnp.concatenate([part[pack * count:(pack + 1) * count] for part in parts], axis=0)


def keyval_kernel(ids_ref, *refs, starts, recv_starts):
    chips = len(starts)
    owns, recvs = refs[:chips], refs[chips:2 * chips]
    keep_ref, first_ref, second_ref = refs[2 * chips:]
    tp = ids_ref[3]
    count = keep_ref.shape[0] // chips
    mine = slabs(owns, starts, count)
    theirs = [slabs((ref,), (start,), count, slice(ref.shape[1] - 2 * HEAD, ref.shape[1]))[0]
              for ref, start in zip(recvs, recv_starts)]
    sums = [own + recv for own, recv in zip(mine, theirs)]
    both = jnp.concatenate([by_pack(sums, pack) for pack in range(2)], axis=0)
    low, high = both[:, :HEAD], both[:, HEAD:]
    keep_ref[...] = jnp.where(tp == 3, high, low).astype(BF16)
    first_ref[...] = jnp.where(tp < 2, high, low).astype(BF16)
    second_ref[...] = jnp.where(tp == 2, high, low).astype(BF16)


def sum_keyval(ids, owns, starts, recvs, recv_starts, count):
    shape = jax.ShapeDtypeStruct((len(owns) * count, HEAD), BF16)
    return pl.pallas_call(
        functools.partial(keyval_kernel, starts=starts, recv_starts=recv_starts),
        out_shape=(shape, shape, shape),
        in_specs=[whole(pltpu.SMEM)] + [whole()] * (2 * len(owns)),
        out_specs=(whole(),) * 3,
        compiler_params=pltpu.CompilerParams(vmem_limit_bytes=8 << 20),
        name="sum_keyval",
    )(ids, *owns, *recvs)


def owner_of(row, pack, ids_ref, piece_rows):
    index = jnp.zeros_like(row)
    for step in range(1, 8):
        index = index + (row >= step * piece_rows).astype(jnp.int32)
    slot, low = index >> 1, index & 1
    chip = slot ^ (slot >> 1)
    shard = (((chip >> 1) ^ ids_ref[2]) * 2 + (low ^ pack)) * 2 + ((chip & 1) ^ ids_ref[1])
    return shard, row - index * piece_rows


def attention_kernel(ids_ref, lengths_ref, tail_ref, *refs, slot, starts, recv_starts, more):
    chips = len(starts)
    owns, recvs, directs = (refs[index * chips:(index + 1) * chips] for index in range(3))
    refs = refs[3 * chips:]
    firsts, lates, gain_ref = refs[0:3], refs[3:6], refs[6]
    before_ref = refs[7] if more else None
    out_ref, bias_ref = refs[7 + more:]
    segment, tp = ids_ref[1], ids_ref[3]
    rows = bias_ref.shape[1]
    slab = rows // 2
    queries = bias_ref.shape[0]
    base = slot * (slab // 2)
    piece_rows = rows // 8
    heads = owns[0].shape[1] // HEAD
    devices = out_ref.shape[0]
    wide = out_ref.shape[1] // 2
    scale = math.log2(math.e) / math.sqrt(HEAD)
    tail = tail_ref[:1, :].astype(jnp.int32)
    lane = iota((queries, wide), 1)

    def chosen_keys(refs):
        keep, first, second = (ref[...].astype(F32) for ref in refs)
        return (jnp.where(tp == 0, keep, jnp.where(tp == 2, second, first)),
                jnp.where(tp == 3, keep, jnp.where(tp == 1, second, first)))

    early, late = chosen_keys(firsts), chosen_keys(lates)
    through = jnp.zeros((devices, wide), F32)
    direct = jnp.zeros((devices, wide), F32)
    for pack in range(2):
        def place(row):
            shard, inner = owner_of(row, pack, ids_ref, piece_rows)
            position = shard * piece_rows + inner
            end = jnp.zeros((1, 1), jnp.int32)
            doc = jnp.zeros_like(position)
            for index in range(lengths_ref.shape[1]):
                at = LENGTHS_AT + index
                end = end + jnp.where(segment == pack, lengths_ref[0, index], tail[:, at:at + 1])
                doc = doc + (position >= end).astype(jnp.int32)
            return position, doc

        row_position, row_doc = place(iota((queries, 1), 0) + base)
        col_position, col_doc = place(iota((1, rows), 1))
        visible = jnp.logical_and(row_doc == col_doc, col_position <= row_position)
        bias_ref[...] = jnp.where(visible, 0.0, -1e30)
        keys, values = (
            jnp.concatenate([part[pack * (part.shape[0] // 2):(pack + 1) * (part.shape[0] // 2)]
                             for part in parts], axis=0).astype(BF16)
            for parts in zip(early, late))
        values = jnp.concatenate([values, jnp.ones((rows, HEAD), BF16)], axis=1)
        total = jnp.zeros((queries, HEAD), F32)
        for head in range(heads):
            at = slice(head * HEAD, (head + 1) * HEAD)
            parts = [own + recv for own, recv in zip(
                slabs(owns, starts, slab, at), slabs(recvs, recv_starts, slab, at))]
            query = (by_pack(parts, pack) * scale).astype(BF16)
            logits = lax.dot_general(query, keys, (((1,), (1,)), ((), ())), preferred_element_type=F32)
            logits = logits + bias_ref[...]
            expo = jnp.exp2(logits - jnp.max(logits, axis=1, keepdims=True)).astype(BF16)
            both = jnp.dot(expo, values, preferred_element_type=F32)
            offset = pl.multiple_of(segment * heads * HEAD + head * HEAD, HEAD)
            total = total + both[:, :HEAD] / both[:, HEAD:] * gain_ref[:, pl.ds(offset, HEAD)].astype(F32)

        _, inner = owner_of(iota((queries, 1), 0) + base, pack, ids_ref, piece_rows)
        shard_row, _ = owner_of(iota((1, queries), 1) + base, pack, ids_ref, piece_rows)
        chosen = ((iota((devices, 1), 0) >> 2) == shard_row).astype(F32)
        hit = lane == inner + pack * piece_rows

        def send(column):
            return jnp.dot(chosen, jnp.where(hit, column, 0.0), precision=HIGHEST, preferred_element_type=F32)

        through = through + send(jnp.sum(total, axis=1, keepdims=True))
        direct = direct + send(jnp.sum(by_pack(slabs(directs, starts, slab), pack), axis=1, keepdims=True))
    if more:
        through = through + before_ref[:, :wide]
        direct = direct + before_ref[:, wide:]
    out_ref[:, :wide] = through
    out_ref[:, wide:] = direct


def attention(ids, lengths, tail, owns, starts, recvs, recv_starts, directs, firsts, lates, gain, devices,
              slot, before):
    rows = firsts[0].shape[0] // 2 + lates[0].shape[0] // 2
    queries = len(owns) * (rows // 4)
    return pl.pallas_call(
        functools.partial(
            attention_kernel, slot=slot, starts=starts, recv_starts=recv_starts, more=len(before)),
        out_shape=jax.ShapeDtypeStruct((devices, 2 * LANES), F32),
        in_specs=[whole(pltpu.SMEM), whole(pltpu.SMEM)] + [whole()] * (8 + 3 * len(owns) + len(before)),
        out_specs=whole(),
        scratch_shapes=[pltpu.VMEM((queries, rows), F32)],
        compiler_params=pltpu.CompilerParams(vmem_limit_bytes=24 << 20),
        name="attend",
    )(ids, lengths, tail, *owns, *recvs, *directs, *firsts, *lates, gain, *before)


def finish_kernel(recv_ref, send_ref, out_ref):
    models, count = out_ref.shape
    devices, width = recv_ref.shape
    model_of = iota((models, devices), 1) // (devices // models)
    chosen = (model_of == iota((models, devices), 0)).astype(F32)
    sums = jnp.dot(chosen, recv_ref[...], precision=HIGHEST, preferred_element_type=F32)
    pick = (iota((count, count), 0) == send_ref[...]).astype(F32)
    half = width // 2
    both = sums[:, :count] + sums[:, half:half + count]
    out_ref[...] = lax.dot_general(
        both, pick, (((1,), (1,)), ((), ())), precision=HIGHEST, preferred_element_type=F32)


def finish(recv, send, models):
    count = send.shape[1]
    return pl.pallas_call(
        finish_kernel,
        out_shape=jax.ShapeDtypeStruct((models, count), F32),
        in_specs=[whole()] * 2,
        out_specs=whole(),
        compiler_params=pltpu.CompilerParams(vmem_limit_bytes=8 << 20),
        name="finish",
    )(recv, send)


def paired(rollout, send_rows, seq_lengths, attn_gain, w_query, w_keyval, head_weight, head_attn):
    n_branch = lax.axis_size("branch")
    branch = lax.axis_index("branch")
    segment = lax.axis_index("segment")
    tp = lax.axis_index("tp")
    send = send_rows.reshape(1, -1)
    ids = jnp.stack([branch & 1, segment, branch >> 1, tp]).astype(jnp.int32)

    core_pairs = [(i, i ^ 1) for i in range(n_branch)]
    y_pairs = [(i, i ^ 2) for i in range(n_branch)]
    x_pairs = [(0, 1), (1, 0)]

    def swap(piece):
        return lax.ppermute(piece, "branch", core_pairs)

    def across(part):
        return lax.ppermute(part, "segment", x_pairs)

    def in_hbm(array):
        return pltpu.with_memory_space_constraint(array, pltpu.HBM)

    packing = send
    rollout, send, attn_gain, head_weight, seq_lengths = map(
        in_hbm, (rollout, send, attn_gain, head_weight, seq_lengths))
    wq, wkv = in_hbm(w_query[0]), in_hbm(w_keyval[0])
    mine, theirs = prepare(ids, seq_lengths, rollout, send)
    from_x = across(theirs)
    from_y = lax.ppermute(mine, "branch", y_pairs)
    from_d = lax.ppermute(from_x, "branch", y_pairs)

    slab = 2 * mine.shape[0]
    local, direct, query, received = {}, {}, {}, {}
    for name, pieces in (("own", (mine,)), ("xy", (from_x, from_y)), ("d", (from_d,))):
        pieces = [part for piece in pieces for part in (piece, swap(piece))]
        if name == "own":
            out, weights = first_chunk(ids, *pieces, attn_gain, head_weight, wkv, wq)
        else:
            out = next_chunk(ids, pieces, weights)
        rows, local[name], direct[name], lengths, *sends = out
        if name == "xy":
            tail = lengths
        for index, part in reversed(list(enumerate(sends))):
            sends[index] = across(part)
        received[name] = sends
        if name == "own":
            query[name], own_weights = first_own(ids, rows, wq)
        else:
            query[name] = next_own(rows, own_weights)

    keep, first, second = sum_keyval(
        ids, [local["own"], local["xy"], local["d"]], (0, 0, 0),
        [received["xy"][1], received["own"][0], received["xy"][1]], (0, 0, slab), slab)
    hand_first, hand_second = [(0, 1), (2, 0), (1, 3), (3, 2)], [(2, 1), (1, 2)]
    first = lax.ppermute(first, "tp", hand_first)
    second = lax.ppermute(second, "tp", hand_second)
    early = (keep, first, second)
    keep, first, second = sum_keyval(
        ids, [local["xy"]], (slab,), [received["d"][1]], (0,), slab)
    first = lax.ppermute(first, "tp", hand_first)
    second = lax.ppermute(second, "tp", hand_second)
    late = (keep, first, second)
    devices = n_branch * 2 * lax.axis_size("tp")
    outgoing = attention(
        ids, seq_lengths, tail,
        [query["own"], query["xy"], query["d"], query["xy"]], (0, 0, 0, slab),
        [received["xy"][0], received["own"][0], received["xy"][0], received["d"][0]], (0, 0, slab, 0),
        [direct["own"], direct["xy"], direct["d"], direct["xy"]],
        early, late, head_attn, devices, 0, [])
    incoming = lax.all_to_all(outgoing, ALL_AXES, split_axis=0, concat_axis=0, tiled=True)
    return finish(incoming, packing, n_branch)


def general(rollout, send_rows, seq_lengths, attn_gain, w_query, w_keyval, head_weight, head_attn):
    n_branch = lax.axis_size("branch")
    n_segment = lax.axis_size("segment")
    gen_rows = rollout.shape[0]
    piece_rows = gen_rows // n_segment
    row_width = rollout.shape[1]
    ordered = jnp.take(rollout, send_rows, axis=0).reshape(n_segment, piece_rows, row_width)
    copies = jnp.broadcast_to(ordered[None], (n_branch, n_segment, piece_rows, row_width))
    copies = copies.reshape(n_branch * n_segment, piece_rows, row_width)
    arrived = lax.all_to_all(copies, ("branch", "segment"), split_axis=0, concat_axis=0, tiled=True)
    packed = arrived.reshape(-1, row_width)
    pack_rows = packed.shape[0]
    rows_float = packed.astype(jnp.float32)
    mean_square = jnp.mean(rows_float * rows_float, axis=-1, keepdims=True)
    normed = (
        rows_float * lax.rsqrt(mean_square + epsilon) * attn_gain[0].astype(jnp.float32)
    ).astype(jnp.bfloat16)
    query_acc = jnp.dot(
        normed,
        lax.all_gather(w_query, "segment", axis=1, tiled=True)[0],
        preferred_element_type=jnp.float32,
    )
    keyval_acc = jnp.dot(
        normed,
        lax.all_gather(w_keyval, "segment", axis=1, tiled=True)[0],
        preferred_element_type=jnp.float32,
    )
    queries = query_acc.astype(jnp.bfloat16)
    keyval_part = keyval_acc.astype(jnp.bfloat16)
    keyval = lax.all_gather(keyval_part, "tp", axis=1, tiled=True)
    tp_index = lax.axis_index("tp")
    heads_here = queries.shape[1] // HEAD
    group_size = HEADS // KV_HEADS
    per_group = min(heads_here, group_size)
    group_span = heads_here // per_group
    kv_first = tp_index * heads_here // group_size
    key_rows = lax.dynamic_slice_in_dim(keyval, kv_first * HEAD, group_span * HEAD, 1)
    value_rows = lax.dynamic_slice_in_dim(
        keyval, KV_HEADS * HEAD + kv_first * HEAD, group_span * HEAD, 1
    )
    key_rows = key_rows.reshape(pack_rows, group_span, HEAD)
    value_rows = value_rows.reshape(pack_rows, group_span, HEAD)
    queries = queries.reshape(pack_rows, group_span, per_group, HEAD)
    positions = jnp.arange(pack_rows, dtype=jnp.int32)
    doc_ends = jnp.cumsum(seq_lengths[0])
    doc_ids = jnp.sum((positions[:, None] >= doc_ends[None, :]).astype(jnp.int32), axis=-1)
    visible = (doc_ids[:, None] == doc_ids[None, :]) & (positions[None, :] <= positions[:, None])
    logits = jnp.einsum(
        "qgpc,kgc->gpqk", queries, key_rows, preferred_element_type=jnp.float32
    ) / math.sqrt(HEAD)
    logits = jnp.where(visible[None, None], logits, -1e30)
    row_max = jnp.max(logits, axis=-1, keepdims=True)
    expo = jnp.exp(logits - row_max)
    probabilities = (expo / jnp.sum(expo, axis=-1, keepdims=True)).astype(jnp.bfloat16)
    attended = jnp.einsum(
        "gpqk,kgc->qgpc", probabilities, value_rows, preferred_element_type=jnp.float32
    )
    attended = attended.reshape(pack_rows, heads_here * HEAD)
    slice_width = head_weight.shape[1]
    own_columns = lax.dynamic_slice_in_dim(packed, tp_index * slice_width, slice_width, 1)
    direct = jnp.dot(own_columns, head_weight[0], preferred_element_type=jnp.float32)
    through = jnp.dot(attended, head_attn[0].astype(jnp.float32), precision=lax.Precision.HIGHEST)
    totals = lax.psum(direct + through, "tp")
    outgoing = totals.reshape(n_branch * n_segment, piece_rows)
    incoming = lax.all_to_all(
        outgoing, ("branch", "segment"), split_axis=0, concat_axis=0, tiled=True
    )
    incoming = incoming.reshape(n_branch, n_segment * piece_rows)
    scores = jnp.zeros((n_branch, gen_rows), jnp.float32).at[:, send_rows].set(incoming)
    return scores


def solution(mesh):
    sizes = tuple(mesh.shape[axis] for axis in ALL_AXES)
    pairwise = sizes == (4, 2, 4)
    local = paired if pairwise else general
    return jax.shard_map(
        local,
        mesh=mesh,
        in_specs=(
            P(("branch", "segment"), None),
            P(("branch", "segment")),
            P("segment", None),
            P("branch", None),
            P("branch", "segment", "tp"),
            P("branch", "segment", "tp"),
            P("branch", "tp"),
            P("branch", "tp"),
        ),
        out_specs=P(None, ("branch", "segment")),
        check_vma=False,
    )
```

```python
import functools
import math

import jax
import jax.numpy as jnp
from jax import lax
from jax.experimental import pallas as pl
from jax.experimental.pallas import tpu as pltpu
from jax.sharding import PartitionSpec as P


HEAD = 128
HEADS = 64
KV_HEADS = 8
LANES = 128
LENGTHS_AT = 8

epsilon = 1e-05

ALL_AXES = ("branch", "segment", "tp")
HIGHEST = lax.Precision.HIGHEST
F32 = jnp.float32
BF16 = jnp.bfloat16


def whole(memory_space=pltpu.VMEM):
    return pl.BlockSpec(memory_space=memory_space)


def iota(shape, dimension):
    return lax.broadcasted_iota(jnp.int32, shape, dimension)


def prepare_kernel(ids_ref, lengths_ref, rows_hbm, send_hbm, mine_ref, theirs_ref, rows_ref, send_ref, sems):
    count, width = rows_ref.shape
    half = width // 2
    parts = sems.shape[0] - 1
    step = width // parts
    core, segment = ids_ref[0], ids_ref[1]
    copies = [pltpu.make_async_copy(send_hbm, send_ref, sems.at[parts])]
    for part in range(parts):
        at = pl.ds(part * step, step)
        copies.append(pltpu.make_async_copy(rows_hbm.at[:, at], rows_ref.at[:, at], sems.at[part]))
    for copy in copies:
        copy.start()
    copies[0].wait()
    send = send_ref[...]
    rolled = jnp.concatenate([send[:, count // 2:], send[:, :count // 2]], axis=1)
    order = jnp.where(core == 1, rolled, send)
    pick = (iota((count, count), 0) == order).astype(BF16)

    def ordered(part):
        out = lax.dot_general(pick, part, (((0,), (0,)), ((), ())), preferred_element_type=F32)
        return out.astype(BF16)

    lanes = jnp.zeros((count, LANES), F32)
    for part in range(parts):
        copies[1 + part].wait()
        square = rows_ref[:, part * step:(part + 1) * step].astype(F32)
        square = square * square
        for lane in range(0, step, LANES):
            lanes = lanes + square[:, lane:lane + LANES]
    chunk = 1024
    for start in range(0, half, chunk):
        for out_ref, which in ((theirs_ref, 1 - segment), (mine_ref, segment)):
            at = pl.multiple_of(which * half + start, chunk)
            out_ref[:, start:start + chunk] = ordered(rows_ref[:, pl.ds(at, chunk)])
    scale = lax.rsqrt(jnp.sum(lanes, axis=1, keepdims=True) * (1.0 / width) + epsilon)
    high = scale.astype(BF16).astype(F32)
    middle = (scale - high).astype(BF16).astype(F32)
    low = scale - high - middle
    lane = iota((count, LANES), 1)
    tail = jnp.where(lane == 0, high, jnp.where(lane == 1, middle, jnp.where(lane == 2, low, 0.0)))
    tail = ordered(tail.astype(BF16))
    for index in range(lengths_ref.shape[1]):
        length = lengths_ref[0, index].astype(F32).astype(BF16)
        tail = jnp.where(lane == LENGTHS_AT + index, length, tail)
    theirs_ref[:, half:] = tail
    mine_ref[:, half:] = tail


def prepare(ids, lengths, rows, send):
    count, width = rows.shape
    shape = jax.ShapeDtypeStruct((count, width // 2 + LANES), BF16)
    return pl.pallas_call(
        prepare_kernel,
        out_shape=(shape, shape),
        in_specs=[whole(pltpu.SMEM), whole(pltpu.SMEM), whole(pltpu.HBM), whole(pltpu.HBM)],
        out_specs=(whole(), whole()),
        scratch_shapes=[
            pltpu.VMEM((count, width), BF16),
            pltpu.VMEM((1, count), jnp.int32),
            pltpu.SemaphoreType.DMA((5,)),
        ],
        compiler_params=pltpu.CompilerParams(vmem_limit_bytes=12 << 20),
        name="prepare",
    )(ids, lengths, rows, send)


BLOCK = 256


def column_copies(source, first, target, sems):
    blocks = target.shape[1] // BLOCK
    return [
        pltpu.make_async_copy(
            source.at[:, pl.ds(pl.multiple_of(first + index * BLOCK, BLOCK), BLOCK)],
            target.at[:, pl.ds(index * BLOCK, BLOCK)], sems.at[index])
        for index in range(blocks)]


def split_slots(values):
    return values[:, :HEAD], values[:, HEAD:]


def chunk_body(ids_ref, pieces, gain_ref, head_ref, keyval_ref, query_ref, outs, waits, recv=None):
    rows_ref, direct_ref, tail_ref = outs[:3]
    count = pieces[0].shape[0]
    half = rows_ref.shape[1]
    core, segment, tp = ids_ref[0], ids_ref[1], ids_ref[3]
    columns = query_ref.shape[1]
    top = (iota((count, 1), 0) < count // 2).astype(jnp.int32)
    mask = (top ^ core) == 1

    def sorted_rows(values):
        near, far = values[0::2], values[1::2]
        return jnp.concatenate(
            [part for n, f in zip(near, far) for part in (jnp.where(mask, n, f), jnp.where(mask, f, n))], axis=0)

    first_lanes = iota((count, LANES), 1) < 3
    scale = sorted_rows([
        jnp.sum(jnp.where(first_lanes, ref[:, half:].astype(F32), 0.0), axis=1, keepdims=True) for ref in pieces])
    chunk = 512
    direct = jnp.zeros((direct_ref.shape[0], LANES), F32)
    for start in range(0, half, chunk):
        at = slice(start, start + chunk)
        rows = sorted_rows([ref[:, at].astype(F32) for ref in pieces])
        weight = head_ref[:, at].astype(F32)
        for lane in range(0, chunk, LANES):
            direct = direct + rows[:, lane:lane + LANES] * weight[:, lane:lane + LANES]
        rows_ref[:, at] = (rows * scale * gain_ref[:, at].astype(F32)).astype(BF16)
    direct_ref[...] = direct
    tail_ref[...] = pieces[0][:, half:].astype(F32)[:8]

    for wait in waits[:keyval_ref.shape[1] // BLOCK]:
        wait()
    keyval = jnp.dot(rows_ref[...], keyval_ref[...], preferred_element_type=F32)
    even = jnp.concatenate([keyval[:, :HEAD], keyval[:, 2 * HEAD:3 * HEAD]], axis=1)
    odd = jnp.concatenate([keyval[:, HEAD:2 * HEAD], keyval[:, 3 * HEAD:]], axis=1)
    own = jnp.where(segment == 0, even, odd)
    other = jnp.where(segment == 0, odd, even)
    if recv is None:
        own_ref, send_ref = outs[3:5]
        own_ref[...] = own
        if len(outs) > 5:
            outs[5][...] = other.astype(BF16)
        else:
            send_ref[:, columns:] = other.astype(BF16)
    else:
        send_ref, keep_ref, first_ref, second_ref, far_first_ref, far_second_ref = outs[3:]
        low, high = split_slots(own + recv)
        keep_ref[...] = jnp.where(tp == 3, high, low).astype(BF16)
        first_ref[...] = jnp.where(tp < 2, high, low).astype(BF16)
        second_ref[...] = jnp.where(tp == 2, high, low).astype(BF16)
        low, high = split_slots(other)
        far_first_ref[...] = jnp.where(tp < 2, high, low).astype(BF16)
        far_second_ref[...] = jnp.where(tp < 2, low, high).astype(BF16)
    waits = waits[keyval_ref.shape[1] // BLOCK:]
    for index in range(columns // BLOCK):
        if waits:
            waits[index]()
        at = slice(index * BLOCK, (index + 1) * BLOCK)
        send_ref[:, at] = jnp.dot(rows_ref[...], query_ref[:, at], preferred_element_type=F32).astype(BF16)


def first_chunk_kernel(ids_ref, near_ref, far_ref, gain_hbm, head_hbm, keyval_hbm, query_hbm, *refs):
    outs, (gain_ref, head_ref, keyval_ref, query_ref) = refs[:4], refs[4:8]
    own_query_ref, own_out_ref, rows_ref, part_ref, small_sems, sems, own_sems = refs[8:]
    outs = (rows_ref, *outs)
    half = rows_ref.shape[1]
    segment, tp = ids_ref[1], ids_ref[3]
    small = [
        pltpu.make_async_copy(
            gain_hbm.at[:, pl.ds(pl.multiple_of(segment * half, half), half)], gain_ref, small_sems.at[0]),
        pltpu.make_async_copy(head_hbm, part_ref, small_sems.at[1]),
    ]
    blocks = keyval_ref.shape[1] // BLOCK
    large = column_copies(keyval_hbm, 0, keyval_ref, sems)
    large += column_copies(query_hbm, (1 - segment) * query_ref.shape[1], query_ref, sems.at[pl.ds(blocks, query_ref.shape[1] // BLOCK)])
    owns = column_copies(query_hbm, segment * query_ref.shape[1], own_query_ref, own_sems)
    for copy in small + large + owns:
        copy.start()
    for copy in small:
        copy.wait()
    width = part_ref.shape[1]
    head_ref[...] = jnp.zeros_like(head_ref)

    @pl.when((tp * width) // half == segment)
    def _():
        head_ref[:, pl.ds(pl.multiple_of((tp * width) % half, width), width)] = part_ref[...]

    chunk_body(ids_ref, (near_ref, far_ref), gain_ref, head_ref, keyval_ref, query_ref, outs,
               [copy.wait for copy in large])
    own_body(rows_ref, own_query_ref, own_out_ref, [copy.wait for copy in owns])


def next_chunk_kernel(ids_ref, *refs, chips):
    pieces, refs = refs[:2 * chips], refs[2 * chips:]
    chunk_body(ids_ref, pieces, *refs[:4], refs[4:], [])


def last_chunk_kernel(ids_ref, *refs, start):
    pieces, refs = refs[:2], refs[2:]
    count = pieces[0].shape[0] * 2
    chunk_body(ids_ref, pieces, *refs[:4], refs[5:], [], refs[4][start:start + count, :].astype(F32))


def shape_of(*shape, kind=BF16):
    return jax.ShapeDtypeStruct(shape, kind)


def chunk_shapes(rows, half):
    return (shape_of(rows, half), shape_of(rows, LANES, kind=F32), shape_of(8, LANES, kind=F32))


def first_chunk(ids, near, far, gain, head, keyval, query):
    count, wide = near.shape
    half = wide - LANES
    columns = query.shape[1] // 2
    rows = 2 * count
    shapes = chunk_shapes(rows, half)[1:] + (
        shape_of(rows, 2 * HEAD, kind=F32), shape_of(rows, columns + 2 * HEAD),
        shape_of(1, half), shape_of(1, half), shape_of(*keyval.shape), shape_of(half, columns),
        shape_of(half, columns), shape_of(rows, columns, kind=F32))
    out = pl.pallas_call(
        first_chunk_kernel,
        out_shape=shapes,
        in_specs=[whole(pltpu.SMEM), whole(), whole()] + [whole(pltpu.HBM)] * 4,
        out_specs=(whole(),) * len(shapes),
        scratch_shapes=[
            pltpu.VMEM((rows, half), BF16),
            pltpu.VMEM(head.shape, BF16),
            pltpu.SemaphoreType.DMA((2,)),
            pltpu.SemaphoreType.DMA(((columns + keyval.shape[1]) // BLOCK,)),
            pltpu.SemaphoreType.DMA((columns // BLOCK,)),
        ],
        compiler_params=pltpu.CompilerParams(vmem_limit_bytes=14 << 20),
        name="first_chunk",
    )(ids, near, far, gain, head, keyval, query)
    return out[:4], out[4:8], out[8], out[9]


def next_chunk(ids, pieces, weights):
    count, wide = pieces[0].shape
    chips = len(pieces) // 2
    rows = 2 * chips * count
    shapes = chunk_shapes(rows, wide - LANES) + (
        shape_of(rows, 2 * HEAD, kind=F32), shape_of(rows, weights[3].shape[1]), shape_of(rows, 2 * HEAD))
    return pl.pallas_call(
        functools.partial(next_chunk_kernel, chips=chips),
        out_shape=shapes,
        in_specs=[whole(pltpu.SMEM)] + [whole()] * (len(pieces) + 4),
        out_specs=(whole(),) * len(shapes),
        compiler_params=pltpu.CompilerParams(vmem_limit_bytes=14 << 20),
        name="next_chunk",
    )(ids, *pieces, *weights)


def last_chunk(ids, pieces, weights, recv, start):
    count, wide = pieces[0].shape
    rows = 2 * count
    shapes = chunk_shapes(rows, wide - LANES) + (shape_of(rows, weights[3].shape[1]),) + (shape_of(rows, HEAD),) * 5
    return pl.pallas_call(
        functools.partial(last_chunk_kernel, start=start),
        out_shape=shapes,
        in_specs=[whole(pltpu.SMEM)] + [whole()] * (len(pieces) + 5),
        out_specs=(whole(),) * len(shapes),
        compiler_params=pltpu.CompilerParams(vmem_limit_bytes=14 << 20),
        name="last_chunk",
    )(ids, *pieces, *weights, recv)


def own_body(rows_ref, query_ref, out_ref, waits=()):
    for index in range(query_ref.shape[1] // BLOCK):
        if waits:
            waits[index]()
        at = slice(index * BLOCK, (index + 1) * BLOCK)
        out_ref[:, at] = jnp.dot(rows_ref[...], query_ref[:, at], preferred_element_type=F32)


def own_queries(rows, query):
    return pl.pallas_call(
        own_body,
        out_shape=shape_of(rows.shape[0], query.shape[1], kind=F32),
        in_specs=[whole(), whole()],
        out_specs=whole(),
        compiler_params=pltpu.CompilerParams(vmem_limit_bytes=10 << 20),
        name="own_queries",
    )(rows, query)


def slabs(refs, starts, count, at=slice(None)):
    return [ref[start:start + count, at].astype(F32) for ref, start in zip(refs, starts)]


def by_pack(parts, pack):
    count = parts[0].shape[0] // 2
    return jnp.concatenate([part[pack * count:(pack + 1) * count] for part in parts], axis=0)


def keyval_kernel(ids_ref, own_ref, next_ref, recv_own_ref, recv_next_ref, keep_ref, first_ref, second_ref):
    tp = ids_ref[3]
    count = own_ref.shape[0]
    mine, x_part, y_part = slabs((own_ref, next_ref, next_ref), (0, 0, count), count)
    width = recv_next_ref.shape[1]
    at = slice(width - 2 * HEAD, width)
    sums = [mine + recv_own_ref[:count, :].astype(F32), x_part + recv_next_ref[:, at].astype(F32), y_part]
    low, high = split_slots(jnp.concatenate([by_pack(sums, pack) for pack in range(2)], axis=0))
    keep_ref[...] = jnp.where(tp == 3, high, low).astype(BF16)
    first_ref[...] = jnp.where(tp < 2, high, low).astype(BF16)
    second_ref[...] = jnp.where(tp == 2, high, low).astype(BF16)


def sum_keyval(ids, own, pair, recv_own, recv_next):
    shape = shape_of(own.shape[0] + pair.shape[0], HEAD)
    return pl.pallas_call(
        keyval_kernel,
        out_shape=(shape, shape, shape),
        in_specs=[whole(pltpu.SMEM)] + [whole()] * 4,
        out_specs=(whole(),) * 3,
        compiler_params=pltpu.CompilerParams(vmem_limit_bytes=8 << 20),
        name="sum_keyval",
    )(ids, own, pair, recv_own, recv_next)


def owner_of(row, pack, ids_ref, piece_rows):
    index = jnp.zeros_like(row)
    for step in range(1, 8):
        index = index + (row >= step * piece_rows).astype(jnp.int32)
    chip, low = index >> 1, index & 1
    shard = (((chip >> 1) ^ ids_ref[2]) * 2 + (low ^ pack)) * 2 + ((chip & 1) ^ ids_ref[1])
    return shard, row - index * piece_rows


def attention_kernel(ids_ref, lengths_ref, tail_ref, *refs, starts, recv_starts):
    chips = len(starts)
    owns, recvs, directs = (refs[index * chips:(index + 1) * chips] for index in range(3))
    refs = refs[3 * chips:]
    earlies, lates, fars, gain_ref = refs[0:3], refs[3:6], refs[6:8], refs[8]
    out_ref, bias_ref = refs[9:]
    segment, tp = ids_ref[1], ids_ref[3]
    rows = bias_ref.shape[1]
    slab = rows // 2
    queries = bias_ref.shape[0]
    piece_rows = rows // 8
    heads = owns[0].shape[1] // HEAD
    devices = out_ref.shape[0]
    wide = out_ref.shape[1] // 2
    scale = math.log2(math.e) / math.sqrt(HEAD)
    tail = tail_ref[:1, :].astype(jnp.int32)
    lane = iota((queries, wide), 1)

    def chosen_keys(refs):
        keep, first, second = (ref[...].astype(F32) for ref in refs)
        return (jnp.where(tp == 0, keep, jnp.where(tp == 2, second, first)),
                jnp.where(tp == 3, keep, jnp.where(tp == 1, second, first)))

    def pack_part(part, pack):
        count = part.shape[0] // 2
        return part[pack * count:(pack + 1) * count]

    far_first, far_second = (ref[...].astype(F32) for ref in fars)
    odd = (tp & 1) == 1
    far = (jnp.where(odd, far_first, far_second), jnp.where(odd, far_second, far_first))
    early, late = chosen_keys(earlies), chosen_keys(lates)
    through = jnp.zeros((devices, wide), F32)
    direct = jnp.zeros((devices, wide), F32)
    for pack in range(2):
        def place(row):
            shard, inner = owner_of(row, pack, ids_ref, piece_rows)
            position = shard * piece_rows + inner
            end = jnp.zeros((1, 1), jnp.int32)
            doc = jnp.zeros_like(position)
            for index in range(lengths_ref.shape[1]):
                at = LENGTHS_AT + index
                end = end + jnp.where(segment == pack, lengths_ref[0, index], tail[:, at:at + 1])
                doc = doc + (position >= end).astype(jnp.int32)
            return position, doc

        row_position, row_doc = place(iota((queries, 1), 0))
        col_position, col_doc = place(iota((1, rows), 1))
        visible = jnp.logical_and(row_doc == col_doc, col_position <= row_position)
        bias_ref[...] = jnp.where(visible, 0.0, -1e30)
        keys, values = (
            jnp.concatenate([
                pack_part(at_once, pack)[:slab],
                pack_part(at_once, pack)[slab:] + pack_part(far_part, pack),
                pack_part(late_part, pack)], axis=0).astype(BF16)
            for at_once, far_part, late_part in zip(early, far, late))
        values = jnp.concatenate([values, jnp.ones((rows, HEAD), BF16)], axis=1)
        total = jnp.zeros((queries, HEAD), F32)
        for head in range(heads):
            at = slice(head * HEAD, (head + 1) * HEAD)
            parts = [own + recv for own, recv in zip(
                slabs(owns, starts, slab, at), slabs(recvs, recv_starts, slab, at))]
            query = (by_pack(parts, pack) * scale).astype(BF16)
            logits = lax.dot_general(query, keys, (((1,), (1,)), ((), ())), preferred_element_type=F32)
            logits = logits + bias_ref[...]
            expo = jnp.exp2(logits - jnp.max(logits, axis=1, keepdims=True)).astype(BF16)
            both = jnp.dot(expo, values, preferred_element_type=F32)
            offset = pl.multiple_of(segment * heads * HEAD + head * HEAD, HEAD)
            total = total + both[:, :HEAD] / both[:, HEAD:] * gain_ref[:, pl.ds(offset, HEAD)].astype(F32)

        _, inner = owner_of(iota((queries, 1), 0), pack, ids_ref, piece_rows)
        shard_row, _ = owner_of(iota((1, queries), 1), pack, ids_ref, piece_rows)
        chosen = ((iota((devices, 1), 0) >> 2) == shard_row).astype(F32)
        hit = lane == inner + pack * piece_rows

        def send(column):
            return jnp.dot(chosen, jnp.where(hit, column, 0.0), precision=HIGHEST, preferred_element_type=F32)

        through = through + send(jnp.sum(total, axis=1, keepdims=True))
        direct = direct + send(jnp.sum(by_pack(slabs(directs, starts, slab), pack), axis=1, keepdims=True))
    out_ref[:, :wide] = through
    out_ref[:, wide:] = direct


def attention(ids, lengths, tail, owns, starts, recvs, recv_starts, directs, early, late, far, gain, devices):
    rows = early[0].shape[0] // 2 + late[0].shape[0] // 2
    return pl.pallas_call(
        functools.partial(attention_kernel, starts=starts, recv_starts=recv_starts),
        out_shape=shape_of(devices, 2 * LANES, kind=F32),
        in_specs=[whole(pltpu.SMEM), whole(pltpu.SMEM)] + [whole()] * (10 + 3 * len(owns)),
        out_specs=whole(),
        scratch_shapes=[pltpu.VMEM((rows, rows), F32)],
        compiler_params=pltpu.CompilerParams(vmem_limit_bytes=14 << 20),
        name="attend",
    )(ids, lengths, tail, *owns, *recvs, *directs, *early, *late, *far, gain)


def finish_kernel(recv_ref, send_ref, out_ref):
    models, count = out_ref.shape
    devices, width = recv_ref.shape
    model_of = iota((models, devices), 1) // (devices // models)
    chosen = (model_of == iota((models, devices), 0)).astype(F32)
    sums = jnp.dot(chosen, recv_ref[...], precision=HIGHEST, preferred_element_type=F32)
    pick = (iota((count, count), 0) == send_ref[...]).astype(F32)
    half = width // 2
    both = sums[:, :count] + sums[:, half:half + count]
    out_ref[...] = lax.dot_general(
        both, pick, (((1,), (1,)), ((), ())), precision=HIGHEST, preferred_element_type=F32)


def finish(recv, send, models):
    count = send.shape[1]
    return pl.pallas_call(
        finish_kernel,
        out_shape=jax.ShapeDtypeStruct((models, count), F32),
        in_specs=[whole()] * 2,
        out_specs=whole(),
        compiler_params=pltpu.CompilerParams(vmem_limit_bytes=8 << 20),
        name="finish",
    )(recv, send)


def paired(rollout, send_rows, seq_lengths, attn_gain, w_query, w_keyval, head_weight, head_attn):
    n_branch = lax.axis_size("branch")
    branch = lax.axis_index("branch")
    segment = lax.axis_index("segment")
    tp = lax.axis_index("tp")
    send = send_rows.reshape(1, -1)
    ids = jnp.stack([branch & 1, segment, branch >> 1, tp]).astype(jnp.int32)

    core_pairs = [(i, i ^ 1) for i in range(n_branch)]
    y_pairs = [(i, i ^ 2) for i in range(n_branch)]
    x_pairs = [(0, 1), (1, 0)]

    def swap(piece):
        return lax.ppermute(piece, "branch", core_pairs)

    def across(part):
        return lax.ppermute(part, "segment", x_pairs)

    def in_hbm(array):
        return pltpu.with_memory_space_constraint(array, pltpu.HBM)

    packing = send
    rollout, send, attn_gain, head_weight, seq_lengths = map(
        in_hbm, (rollout, send, attn_gain, head_weight, seq_lengths))
    wq, wkv = in_hbm(w_query[0]), in_hbm(w_keyval[0])
    mine, theirs = prepare(ids, seq_lengths, rollout, send)
    from_x = across(theirs)
    from_y = lax.ppermute(mine, "branch", y_pairs)
    from_d = lax.ppermute(from_x, "branch", y_pairs)

    slab = 2 * mine.shape[0]

    def with_swapped(*pieces):
        return [part for piece in pieces for part in (piece, swap(piece))]

    pieces = with_swapped(mine)
    (direct_own, _, local_own, part), weights, own_weights, query_own = first_chunk(
        ids, *pieces, attn_gain, head_weight, wkv, wq)
    received_own = across(part)

    pieces = with_swapped(from_x, from_y)
    rows, direct_xy, tail, local_xy, part, keyval = next_chunk(ids, pieces, weights)
    keyval_xy = across(keyval)
    received_xy = across(part)
    query_xy = own_queries(rows, own_weights)

    keep, first, second = sum_keyval(ids, local_own, local_xy, keyval_xy, received_own)
    hand_first, hand_second = (1, 3, 0, 2), (0, 2, 1, 3)
    n_tp = len(hand_first)

    def hand(array, targets):
        return lax.ppermute(array, "tp", [(i, to) for i, to in enumerate(targets) if i != to])

    def hand_across(array, targets):
        return lax.ppermute(array, ("segment", "tp"), [
            (side * n_tp + i, (1 - side) * n_tp + to) for side in range(2) for i, to in enumerate(targets)])

    first = hand(first, hand_first)
    second = hand(second, hand_second)
    early = (keep, first, second)

    pieces = with_swapped(from_d)
    rows, direct_d, _, part, keep, first, second, far_first, far_second = last_chunk(
        ids, pieces, weights, keyval_xy, slab)
    far_first = hand_across(far_first, hand_first)
    far_second = hand_across(far_second, hand_second)
    received_d = across(part)
    first = hand(first, hand_first)
    second = hand(second, hand_second)
    late = (keep, first, second)
    query_d = own_queries(rows, own_weights)
    devices = n_branch * 2 * n_tp
    outgoing = attention(
        ids, seq_lengths, tail,
        [query_own, query_xy, query_xy, query_d], (0, 0, slab, 0),
        [received_xy, received_own, received_d, received_xy], (0, 0, 0, slab),
        [direct_own, direct_xy, direct_xy, direct_d],
        early, late, (far_first, far_second), head_attn, devices)
    incoming = lax.all_to_all(outgoing, ALL_AXES, split_axis=0, concat_axis=0, tiled=True)
    return finish(incoming, packing, n_branch)


def general(rollout, send_rows, seq_lengths, attn_gain, w_query, w_keyval, head_weight, head_attn):
    n_branch = lax.axis_size("branch")
    n_segment = lax.axis_size("segment")
    gen_rows = rollout.shape[0]
    piece_rows = gen_rows // n_segment
    row_width = rollout.shape[1]
    ordered = jnp.take(rollout, send_rows, axis=0).reshape(n_segment, piece_rows, row_width)
    copies = jnp.broadcast_to(ordered[None], (n_branch, n_segment, piece_rows, row_width))
    copies = copies.reshape(n_branch * n_segment, piece_rows, row_width)
    arrived = lax.all_to_all(copies, ("branch", "segment"), split_axis=0, concat_axis=0, tiled=True)
    packed = arrived.reshape(-1, row_width)
    pack_rows = packed.shape[0]
    rows_float = packed.astype(jnp.float32)
    mean_square = jnp.mean(rows_float * rows_float, axis=-1, keepdims=True)
    normed = (
        rows_float * lax.rsqrt(mean_square + epsilon) * attn_gain[0].astype(jnp.float32)
    ).astype(jnp.bfloat16)
    query_acc = jnp.dot(
        normed,
        lax.all_gather(w_query, "segment", axis=1, tiled=True)[0],
        preferred_element_type=jnp.float32,
    )
    keyval_acc = jnp.dot(
        normed,
        lax.all_gather(w_keyval, "segment", axis=1, tiled=True)[0],
        preferred_element_type=jnp.float32,
    )
    queries = query_acc.astype(jnp.bfloat16)
    keyval_part = keyval_acc.astype(jnp.bfloat16)
    keyval = lax.all_gather(keyval_part, "tp", axis=1, tiled=True)
    tp_index = lax.axis_index("tp")
    heads_here = queries.shape[1] // HEAD
    group_size = HEADS // KV_HEADS
    per_group = min(heads_here, group_size)
    group_span = heads_here // per_group
    kv_first = tp_index * heads_here // group_size
    key_rows = lax.dynamic_slice_in_dim(keyval, kv_first * HEAD, group_span * HEAD, 1)
    value_rows = lax.dynamic_slice_in_dim(
        keyval, KV_HEADS * HEAD + kv_first * HEAD, group_span * HEAD, 1
    )
    key_rows = key_rows.reshape(pack_rows, group_span, HEAD)
    value_rows = value_rows.reshape(pack_rows, group_span, HEAD)
    queries = queries.reshape(pack_rows, group_span, per_group, HEAD)
    positions = jnp.arange(pack_rows, dtype=jnp.int32)
    doc_ends = jnp.cumsum(seq_lengths[0])
    doc_ids = jnp.sum((positions[:, None] >= doc_ends[None, :]).astype(jnp.int32), axis=-1)
    visible = (doc_ids[:, None] == doc_ids[None, :]) & (positions[None, :] <= positions[:, None])
    logits = jnp.einsum(
        "qgpc,kgc->gpqk", queries, key_rows, preferred_element_type=jnp.float32
    ) / math.sqrt(HEAD)
    logits = jnp.where(visible[None, None], logits, -1e30)
    row_max = jnp.max(logits, axis=-1, keepdims=True)
    expo = jnp.exp(logits - row_max)
    probabilities = (expo / jnp.sum(expo, axis=-1, keepdims=True)).astype(jnp.bfloat16)
    attended = jnp.einsum(
        "gpqk,kgc->qgpc", probabilities, value_rows, preferred_element_type=jnp.float32
    )
    attended = attended.reshape(pack_rows, heads_here * HEAD)
    slice_width = head_weight.shape[1]
    own_columns = lax.dynamic_slice_in_dim(packed, tp_index * slice_width, slice_width, 1)
    direct = jnp.dot(own_columns, head_weight[0], preferred_element_type=jnp.float32)
    through = jnp.dot(attended, head_attn[0].astype(jnp.float32), precision=lax.Precision.HIGHEST)
    totals = lax.psum(direct + through, "tp")
    outgoing = totals.reshape(n_branch * n_segment, piece_rows)
    incoming = lax.all_to_all(
        outgoing, ("branch", "segment"), split_axis=0, concat_axis=0, tiled=True
    )
    incoming = incoming.reshape(n_branch, n_segment * piece_rows)
    scores = jnp.zeros((n_branch, gen_rows), jnp.float32).at[:, send_rows].set(incoming)
    return scores


def solution(mesh):
    sizes = tuple(mesh.shape[axis] for axis in ALL_AXES)
    pairwise = sizes == (4, 2, 4)
    local = paired if pairwise else general
    return jax.shard_map(
        local,
        mesh=mesh,
        in_specs=(
            P(("branch", "segment"), None),
            P(("branch", "segment")),
            P("segment", None),
            P("branch", None),
            P("branch", "segment", "tp"),
            P("branch", "segment", "tp"),
            P("branch", "tp"),
            P("branch", "tp"),
        ),
        out_specs=P(None, ("branch", "segment")),
        check_vma=False,
    )
```

```python
import functools
import math

import jax
import jax.numpy as jnp
from jax import lax
from jax.experimental import pallas as pl
from jax.experimental.pallas import tpu as pltpu
from jax.sharding import PartitionSpec as P


HEAD = 128
HEADS = 64
KV_HEADS = 8
LANES = 128
LENGTHS_AT = 8

epsilon = 1e-05

ALL_AXES = ("branch", "segment", "tp")
HIGHEST = lax.Precision.HIGHEST
F32 = jnp.float32
BF16 = jnp.bfloat16


def whole(memory_space=pltpu.VMEM):
    return pl.BlockSpec(memory_space=memory_space)


def iota(shape, dimension):
    return lax.broadcasted_iota(jnp.int32, shape, dimension)


def prepare_kernel(ids_ref, lengths_ref, rows_hbm, send_hbm, mine_ref, theirs_ref, rows_ref, send_ref, sems):
    count, width = rows_ref.shape
    half = width // 2
    parts = sems.shape[0] - 1
    step = width // parts
    core, segment = ids_ref[0], ids_ref[1]
    copies = [pltpu.make_async_copy(send_hbm, send_ref, sems.at[parts])]
    for part in range(parts):
        at = pl.ds(part * step, step)
        copies.append(pltpu.make_async_copy(rows_hbm.at[:, at], rows_ref.at[:, at], sems.at[part]))
    for copy in copies:
        copy.start()
    copies[0].wait()
    send = send_ref[...]
    rolled = jnp.concatenate([send[:, count // 2:], send[:, :count // 2]], axis=1)
    order = jnp.where(core == 1, rolled, send)
    pick = (iota((count, count), 0) == order).astype(BF16)

    def ordered(part):
        out = lax.dot_general(pick, part, (((0,), (0,)), ((), ())), preferred_element_type=F32)
        return out.astype(BF16)

    lanes = jnp.zeros((count, LANES), F32)
    for part in range(parts):
        copies[1 + part].wait()
        square = rows_ref[:, part * step:(part + 1) * step].astype(F32)
        square = square * square
        for lane in range(0, step, LANES):
            lanes = lanes + square[:, lane:lane + LANES]
    chunk = 1024
    for start in range(0, half, chunk):
        for out_ref, which in ((theirs_ref, 1 - segment), (mine_ref, segment)):
            at = pl.multiple_of(which * half + start, chunk)
            out_ref[:, start:start + chunk] = ordered(rows_ref[:, pl.ds(at, chunk)])
    scale = lax.rsqrt(jnp.sum(lanes, axis=1, keepdims=True) * (1.0 / width) + epsilon)
    high = scale.astype(BF16).astype(F32)
    middle = (scale - high).astype(BF16).astype(F32)
    low = scale - high - middle
    lane = iota((count, LANES), 1)
    tail = jnp.where(lane == 0, high, jnp.where(lane == 1, middle, jnp.where(lane == 2, low, 0.0)))
    tail = ordered(tail.astype(BF16))
    for index in range(lengths_ref.shape[1]):
        length = lengths_ref[0, index].astype(F32).astype(BF16)
        tail = jnp.where(lane == LENGTHS_AT + index, length, tail)
    theirs_ref[:, half:] = tail
    mine_ref[:, half:] = tail


def prepare(ids, lengths, rows, send):
    count, width = rows.shape
    shape = jax.ShapeDtypeStruct((count, width // 2 + LANES), BF16)
    return pl.pallas_call(
        prepare_kernel,
        out_shape=(shape, shape),
        in_specs=[whole(pltpu.SMEM), whole(pltpu.SMEM), whole(pltpu.HBM), whole(pltpu.HBM)],
        out_specs=(whole(), whole()),
        scratch_shapes=[
            pltpu.VMEM((count, width), BF16),
            pltpu.VMEM((1, count), jnp.int32),
            pltpu.SemaphoreType.DMA((5,)),
        ],
        compiler_params=pltpu.CompilerParams(vmem_limit_bytes=12 << 20),
        name="prepare",
    )(ids, lengths, rows, send)


BLOCK = 256
IN_FLIGHT = 4


def column_copies(source, first, target, sems):
    blocks = target.shape[1] // BLOCK
    return [
        pltpu.make_async_copy(
            source.at[:, pl.ds(pl.multiple_of(first + index * BLOCK, BLOCK), BLOCK)],
            target.at[:, pl.ds(index * BLOCK, BLOCK)], sems.at[index])
        for index in range(blocks)]


def split_slots(values):
    return values[:, :HEAD], values[:, HEAD:]


def chunk_body(ids_ref, pieces, gain_ref, head_ref, keyval_ref, query_ref, outs, waits, recv=None):
    rows_ref, direct_ref, tail_ref = outs[:3]
    count = pieces[0].shape[0]
    half = rows_ref.shape[1]
    core, segment, tp = ids_ref[0], ids_ref[1], ids_ref[3]
    columns = query_ref.shape[1]
    top = (iota((count, 1), 0) < count // 2).astype(jnp.int32)
    mask = (top ^ core) == 1

    def sorted_rows(values):
        near, far = values[0::2], values[1::2]
        return jnp.concatenate(
            [part for n, f in zip(near, far) for part in (jnp.where(mask, n, f), jnp.where(mask, f, n))], axis=0)

    first_lanes = iota((count, LANES), 1) < 3
    scale = sorted_rows([
        jnp.sum(jnp.where(first_lanes, ref[:, half:].astype(F32), 0.0), axis=1, keepdims=True) for ref in pieces])
    chunk = 512
    direct = jnp.zeros((direct_ref.shape[0], LANES), F32)
    for start in range(0, half, chunk):
        at = slice(start, start + chunk)
        rows = sorted_rows([ref[:, at].astype(F32) for ref in pieces])
        weight = head_ref[:, at].astype(F32)
        for lane in range(0, chunk, LANES):
            direct = direct + rows[:, lane:lane + LANES] * weight[:, lane:lane + LANES]
        rows_ref[:, at] = (rows * scale * gain_ref[:, at].astype(F32)).astype(BF16)
    direct_ref[...] = direct
    tail_ref[...] = pieces[0][:, half:].astype(F32)[:8]

    for wait in waits[:keyval_ref.shape[1] // BLOCK]:
        wait()
    keyval = jnp.dot(rows_ref[...], keyval_ref[...], preferred_element_type=F32)
    even = jnp.concatenate([keyval[:, :HEAD], keyval[:, 2 * HEAD:3 * HEAD]], axis=1)
    odd = jnp.concatenate([keyval[:, HEAD:2 * HEAD], keyval[:, 3 * HEAD:]], axis=1)
    own = jnp.where(segment == 0, even, odd)
    other = jnp.where(segment == 0, odd, even)
    if recv is None:
        own_ref, send_ref = outs[3:5]
        own_ref[...] = own
        if len(outs) > 5:
            outs[5][...] = other.astype(BF16)
        else:
            send_ref[:, columns:] = other.astype(BF16)
    else:
        send_ref, keep_ref, first_ref, second_ref, far_first_ref, far_second_ref = outs[3:]
        low, high = split_slots(own + recv)
        keep_ref[...] = jnp.where(tp == 3, high, low).astype(BF16)
        first_ref[...] = jnp.where(tp < 2, high, low).astype(BF16)
        second_ref[...] = jnp.where(tp == 2, high, low).astype(BF16)
        low, high = split_slots(other)
        far_first_ref[...] = jnp.where(tp < 2, high, low).astype(BF16)
        far_second_ref[...] = jnp.where(tp < 2, low, high).astype(BF16)
    waits = waits[keyval_ref.shape[1] // BLOCK:]
    for index in range(columns // BLOCK):
        if waits:
            waits[index]()
        at = slice(index * BLOCK, (index + 1) * BLOCK)
        send_ref[:, at] = jnp.dot(rows_ref[...], query_ref[:, at], preferred_element_type=F32).astype(BF16)


def first_chunk_kernel(ids_ref, near_ref, far_ref, gain_hbm, head_hbm, keyval_hbm, query_hbm, *refs):
    outs, (gain_ref, head_ref, keyval_ref, query_ref) = refs[:4], refs[4:8]
    own_query_ref, own_out_ref, rows_ref, part_ref, small_sems, sems, own_sems = refs[8:]
    outs = (rows_ref, *outs)
    half = rows_ref.shape[1]
    segment, tp = ids_ref[1], ids_ref[3]
    small = [
        pltpu.make_async_copy(
            gain_hbm.at[:, pl.ds(pl.multiple_of(segment * half, half), half)], gain_ref, small_sems.at[0]),
        pltpu.make_async_copy(head_hbm, part_ref, small_sems.at[1]),
    ]
    blocks = keyval_ref.shape[1] // BLOCK
    large = column_copies(keyval_hbm, 0, keyval_ref, sems)
    large += column_copies(query_hbm, (1 - segment) * query_ref.shape[1], query_ref, sems.at[pl.ds(blocks, query_ref.shape[1] // BLOCK)])
    owns = column_copies(query_hbm, segment * query_ref.shape[1], own_query_ref, own_sems)
    copies = large + owns
    for copy in small + copies[:IN_FLIGHT]:
        copy.start()

    def waiter(index):
        def wait():
            copies[index].wait()
            if index + IN_FLIGHT < len(copies):
                copies[index + IN_FLIGHT].start()

        return wait

    waits = [waiter(index) for index in range(len(copies))]
    for copy in small:
        copy.wait()
    width = part_ref.shape[1]
    head_ref[...] = jnp.zeros_like(head_ref)

    @pl.when((tp * width) // half == segment)
    def _():
        head_ref[:, pl.ds(pl.multiple_of((tp * width) % half, width), width)] = part_ref[...]

    chunk_body(ids_ref, (near_ref, far_ref), gain_ref, head_ref, keyval_ref, query_ref, outs,
               waits[:len(large)])
    own_body(rows_ref, own_query_ref, own_out_ref, waits[len(large):])


def next_chunk_kernel(ids_ref, *refs, chips):
    pieces, refs = refs[:2 * chips], refs[2 * chips:]
    chunk_body(ids_ref, pieces, *refs[:4], refs[4:], [])


def last_chunk_kernel(ids_ref, *refs, start):
    pieces, refs = refs[:2], refs[2:]
    count = pieces[0].shape[0] * 2
    chunk_body(ids_ref, pieces, *refs[:4], refs[5:], [], refs[4][start:start + count, :].astype(F32))


def shape_of(*shape, kind=BF16):
    return jax.ShapeDtypeStruct(shape, kind)


def chunk_shapes(rows, half):
    return (shape_of(rows, half), shape_of(rows, LANES, kind=F32), shape_of(8, LANES, kind=F32))


def first_chunk(ids, near, far, gain, head, keyval, query):
    count, wide = near.shape
    half = wide - LANES
    columns = query.shape[1] // 2
    rows = 2 * count
    shapes = chunk_shapes(rows, half)[1:] + (
        shape_of(rows, 2 * HEAD, kind=F32), shape_of(rows, columns + 2 * HEAD),
        shape_of(1, half), shape_of(1, half), shape_of(*keyval.shape), shape_of(half, columns),
        shape_of(half, columns), shape_of(rows, columns, kind=F32))
    out = pl.pallas_call(
        first_chunk_kernel,
        out_shape=shapes,
        in_specs=[whole(pltpu.SMEM), whole(), whole()] + [whole(pltpu.HBM)] * 4,
        out_specs=(whole(),) * len(shapes),
        scratch_shapes=[
            pltpu.VMEM((rows, half), BF16),
            pltpu.VMEM(head.shape, BF16),
            pltpu.SemaphoreType.DMA((2,)),
            pltpu.SemaphoreType.DMA(((columns + keyval.shape[1]) // BLOCK,)),
            pltpu.SemaphoreType.DMA((columns // BLOCK,)),
        ],
        compiler_params=pltpu.CompilerParams(vmem_limit_bytes=14 << 20),
        name="first_chunk",
    )(ids, near, far, gain, head, keyval, query)
    return out[:4], out[4:8], out[8], out[9]


def next_chunk(ids, pieces, weights):
    count, wide = pieces[0].shape
    chips = len(pieces) // 2
    rows = 2 * chips * count
    shapes = chunk_shapes(rows, wide - LANES) + (
        shape_of(rows, 2 * HEAD, kind=F32), shape_of(rows, weights[3].shape[1]), shape_of(rows, 2 * HEAD))
    return pl.pallas_call(
        functools.partial(next_chunk_kernel, chips=chips),
        out_shape=shapes,
        in_specs=[whole(pltpu.SMEM)] + [whole()] * (len(pieces) + 4),
        out_specs=(whole(),) * len(shapes),
        compiler_params=pltpu.CompilerParams(vmem_limit_bytes=14 << 20),
        name="next_chunk",
    )(ids, *pieces, *weights)


def last_chunk(ids, pieces, weights, recv, start):
    count, wide = pieces[0].shape
    rows = 2 * count
    shapes = chunk_shapes(rows, wide - LANES) + (shape_of(rows, weights[3].shape[1]),) + (shape_of(rows, HEAD),) * 5
    return pl.pallas_call(
        functools.partial(last_chunk_kernel, start=start),
        out_shape=shapes,
        in_specs=[whole(pltpu.SMEM)] + [whole()] * (len(pieces) + 5),
        out_specs=(whole(),) * len(shapes),
        compiler_params=pltpu.CompilerParams(vmem_limit_bytes=14 << 20),
        name="last_chunk",
    )(ids, *pieces, *weights, recv)


def own_body(rows_ref, query_ref, out_ref, waits=()):
    for index in range(query_ref.shape[1] // BLOCK):
        if waits:
            waits[index]()
        at = slice(index * BLOCK, (index + 1) * BLOCK)
        out_ref[:, at] = jnp.dot(rows_ref[...], query_ref[:, at], preferred_element_type=F32)


def own_queries(rows, query):
    return pl.pallas_call(
        own_body,
        out_shape=shape_of(rows.shape[0], query.shape[1], kind=F32),
        in_specs=[whole(), whole()],
        out_specs=whole(),
        compiler_params=pltpu.CompilerParams(vmem_limit_bytes=10 << 20),
        name="own_queries",
    )(rows, query)


def slabs(refs, starts, count, at=slice(None)):
    return [ref[start:start + count, at].astype(F32) for ref, start in zip(refs, starts)]


def by_pack(parts, pack):
    count = parts[0].shape[0] // 2
    return jnp.concatenate([part[pack * count:(pack + 1) * count] for part in parts], axis=0)


def keyval_kernel(ids_ref, own_ref, next_ref, recv_own_ref, recv_next_ref, keep_ref, first_ref, second_ref):
    tp = ids_ref[3]
    count = own_ref.shape[0]
    mine, x_part, y_part = slabs((own_ref, next_ref, next_ref), (0, 0, count), count)
    width = recv_next_ref.shape[1]
    at = slice(width - 2 * HEAD, width)
    sums = [mine + recv_own_ref[:count, :].astype(F32), x_part + recv_next_ref[:, at].astype(F32), y_part]
    low, high = split_slots(jnp.concatenate([by_pack(sums, pack) for pack in range(2)], axis=0))
    keep_ref[...] = jnp.where(tp == 3, high, low).astype(BF16)
    first_ref[...] = jnp.where(tp < 2, high, low).astype(BF16)
    second_ref[...] = jnp.where(tp == 2, high, low).astype(BF16)


def sum_keyval(ids, own, pair, recv_own, recv_next):
    shape = shape_of(own.shape[0] + pair.shape[0], HEAD)
    return pl.pallas_call(
        keyval_kernel,
        out_shape=(shape, shape, shape),
        in_specs=[whole(pltpu.SMEM)] + [whole()] * 4,
        out_specs=(whole(),) * 3,
        compiler_params=pltpu.CompilerParams(vmem_limit_bytes=8 << 20),
        name="sum_keyval",
    )(ids, own, pair, recv_own, recv_next)


def owner_of(row, pack, ids_ref, piece_rows):
    index = jnp.zeros_like(row)
    for step in range(1, 8):
        index = index + (row >= step * piece_rows).astype(jnp.int32)
    chip, low = index >> 1, index & 1
    shard = (((chip >> 1) ^ ids_ref[2]) * 2 + (low ^ pack)) * 2 + ((chip & 1) ^ ids_ref[1])
    return shard, row - index * piece_rows


def attention_kernel(ids_ref, lengths_ref, tail_ref, *refs, starts, recv_starts):
    chips = len(starts)
    owns, recvs, directs = (refs[index * chips:(index + 1) * chips] for index in range(3))
    refs = refs[3 * chips:]
    earlies, lates, fars, gain_ref = refs[0:3], refs[3:6], refs[6:8], refs[8]
    out_ref, bias_ref = refs[9:]
    segment, tp = ids_ref[1], ids_ref[3]
    rows = bias_ref.shape[1]
    slab = rows // 2
    queries = bias_ref.shape[0]
    piece_rows = rows // 8
    heads = owns[0].shape[1] // HEAD
    devices = out_ref.shape[0]
    wide = out_ref.shape[1] // 2
    scale = math.log2(math.e) / math.sqrt(HEAD)
    tail = tail_ref[:1, :].astype(jnp.int32)
    lane = iota((queries, wide), 1)

    def chosen_keys(refs):
        keep, first, second = (ref[...].astype(F32) for ref in refs)
        return (jnp.where(tp == 0, keep, jnp.where(tp == 2, second, first)),
                jnp.where(tp == 3, keep, jnp.where(tp == 1, second, first)))

    def pack_part(part, pack):
        count = part.shape[0] // 2
        return part[pack * count:(pack + 1) * count]

    far_first, far_second = (ref[...].astype(F32) for ref in fars)
    odd = (tp & 1) == 1
    far = (jnp.where(odd, far_first, far_second), jnp.where(odd, far_second, far_first))
    early, late = chosen_keys(earlies), chosen_keys(lates)
    through = jnp.zeros((devices, wide), F32)
    direct = jnp.zeros((devices, wide), F32)
    for pack in range(2):
        def place(row):
            shard, inner = owner_of(row, pack, ids_ref, piece_rows)
            position = shard * piece_rows + inner
            end = jnp.zeros((1, 1), jnp.int32)
            doc = jnp.zeros_like(position)
            for index in range(lengths_ref.shape[1]):
                at = LENGTHS_AT + index
                end = end + jnp.where(segment == pack, lengths_ref[0, index], tail[:, at:at + 1])
                doc = doc + (position >= end).astype(jnp.int32)
            return position, doc

        row_position, row_doc = place(iota((queries, 1), 0))
        col_position, col_doc = place(iota((1, rows), 1))
        visible = jnp.logical_and(row_doc == col_doc, col_position <= row_position)
        bias_ref[...] = jnp.where(visible, 0.0, -1e30)
        keys, values = (
            jnp.concatenate([
                pack_part(at_once, pack)[:slab],
                pack_part(at_once, pack)[slab:] + pack_part(far_part, pack),
                pack_part(late_part, pack)], axis=0).astype(BF16)
            for at_once, far_part, late_part in zip(early, far, late))
        values = jnp.concatenate([values, jnp.ones((rows, HEAD), BF16)], axis=1)
        total = jnp.zeros((queries, HEAD), F32)
        for head in range(heads):
            at = slice(head * HEAD, (head + 1) * HEAD)
            parts = [own + recv for own, recv in zip(
                slabs(owns, starts, slab, at), slabs(recvs, recv_starts, slab, at))]
            query = (by_pack(parts, pack) * scale).astype(BF16)
            logits = lax.dot_general(query, keys, (((1,), (1,)), ((), ())), preferred_element_type=F32)
            logits = logits + bias_ref[...]
            expo = jnp.exp2(logits - jnp.max(logits, axis=1, keepdims=True)).astype(BF16)
            both = jnp.dot(expo, values, preferred_element_type=F32)
            offset = pl.multiple_of(segment * heads * HEAD + head * HEAD, HEAD)
            total = total + both[:, :HEAD] / both[:, HEAD:] * gain_ref[:, pl.ds(offset, HEAD)].astype(F32)

        _, inner = owner_of(iota((queries, 1), 0), pack, ids_ref, piece_rows)
        shard_row, _ = owner_of(iota((1, queries), 1), pack, ids_ref, piece_rows)
        chosen = ((iota((devices, 1), 0) >> 2) == shard_row).astype(F32)
        hit = lane == inner + pack * piece_rows

        def send(column):
            return jnp.dot(chosen, jnp.where(hit, column, 0.0), precision=HIGHEST, preferred_element_type=F32)

        through = through + send(jnp.sum(total, axis=1, keepdims=True))
        direct = direct + send(jnp.sum(by_pack(slabs(directs, starts, slab), pack), axis=1, keepdims=True))
    out_ref[:, :wide] = through
    out_ref[:, wide:] = direct


def attention(ids, lengths, tail, owns, starts, recvs, recv_starts, directs, early, late, far, gain, devices):
    rows = early[0].shape[0] // 2 + late[0].shape[0] // 2
    return pl.pallas_call(
        functools.partial(attention_kernel, starts=starts, recv_starts=recv_starts),
        out_shape=shape_of(devices, 2 * LANES, kind=F32),
        in_specs=[whole(pltpu.SMEM), whole(pltpu.SMEM)] + [whole()] * (10 + 3 * len(owns)),
        out_specs=whole(),
        scratch_shapes=[pltpu.VMEM((rows, rows), F32)],
        compiler_params=pltpu.CompilerParams(vmem_limit_bytes=14 << 20),
        name="attend",
    )(ids, lengths, tail, *owns, *recvs, *directs, *early, *late, *far, gain)


def finish_kernel(recv_ref, send_ref, out_ref):
    models, count = out_ref.shape
    devices, width = recv_ref.shape
    model_of = iota((models, devices), 1) // (devices // models)
    chosen = (model_of == iota((models, devices), 0)).astype(F32)
    sums = jnp.dot(chosen, recv_ref[...], precision=HIGHEST, preferred_element_type=F32)
    pick = (iota((count, count), 0) == send_ref[...]).astype(F32)
    half = width // 2
    both = sums[:, :count] + sums[:, half:half + count]
    out_ref[...] = lax.dot_general(
        both, pick, (((1,), (1,)), ((), ())), precision=HIGHEST, preferred_element_type=F32)


def finish(recv, send, models):
    count = send.shape[1]
    return pl.pallas_call(
        finish_kernel,
        out_shape=jax.ShapeDtypeStruct((models, count), F32),
        in_specs=[whole()] * 2,
        out_specs=whole(),
        compiler_params=pltpu.CompilerParams(vmem_limit_bytes=8 << 20),
        name="finish",
    )(recv, send)


def paired(rollout, send_rows, seq_lengths, attn_gain, w_query, w_keyval, head_weight, head_attn):
    n_branch = lax.axis_size("branch")
    branch = lax.axis_index("branch")
    segment = lax.axis_index("segment")
    tp = lax.axis_index("tp")
    send = send_rows.reshape(1, -1)
    ids = jnp.stack([branch & 1, segment, branch >> 1, tp]).astype(jnp.int32)

    core_pairs = [(i, i ^ 1) for i in range(n_branch)]
    y_pairs = [(i, i ^ 2) for i in range(n_branch)]
    x_pairs = [(0, 1), (1, 0)]

    def swap(piece):
        return lax.ppermute(piece, "branch", core_pairs)

    def across(part):
        return lax.ppermute(part, "segment", x_pairs)

    def in_hbm(array):
        return pltpu.with_memory_space_constraint(array, pltpu.HBM)

    packing = send
    rollout, send, attn_gain, head_weight, seq_lengths = map(
        in_hbm, (rollout, send, attn_gain, head_weight, seq_lengths))
    wq, wkv = in_hbm(w_query[0]), in_hbm(w_keyval[0])
    mine, theirs = prepare(ids, seq_lengths, rollout, send)
    from_x = across(theirs)
    from_y = lax.ppermute(mine, "branch", y_pairs)
    from_d = lax.ppermute(from_x, "branch", y_pairs)

    slab = 2 * mine.shape[0]

    def with_swapped(*pieces):
        return [part for piece in pieces for part in (piece, swap(piece))]

    pieces = with_swapped(mine)
    (direct_own, _, local_own, part), weights, own_weights, query_own = first_chunk(
        ids, *pieces, attn_gain, head_weight, wkv, wq)
    received_own = across(part)

    pieces = with_swapped(from_x, from_y)
    rows, direct_xy, tail, local_xy, part, keyval = next_chunk(ids, pieces, weights)
    keyval_xy = across(keyval)
    received_xy = across(part)
    query_xy = own_queries(rows, own_weights)

    keep, first, second = sum_keyval(ids, local_own, local_xy, keyval_xy, received_own)
    hand_first, hand_second = (1, 3, 0, 2), (0, 2, 1, 3)
    n_tp = len(hand_first)

    def hand(array, targets):
        return lax.ppermute(array, "tp", [(i, to) for i, to in enumerate(targets) if i != to])

    def hand_across(array, targets):
        return lax.ppermute(array, ("segment", "tp"), [
            (side * n_tp + i, (1 - side) * n_tp + to) for side in range(2) for i, to in enumerate(targets)])

    first = hand(first, hand_first)
    second = hand(second, hand_second)
    early = (keep, first, second)

    pieces = with_swapped(from_d)
    rows, direct_d, _, part, keep, first, second, far_first, far_second = last_chunk(
        ids, pieces, weights, keyval_xy, slab)
    far_first = hand_across(far_first, hand_first)
    far_second = hand_across(far_second, hand_second)
    received_d = across(part)
    first = hand(first, hand_first)
    second = hand(second, hand_second)
    late = (keep, first, second)
    query_d = own_queries(rows, own_weights)
    devices = n_branch * 2 * n_tp
    outgoing = attention(
        ids, seq_lengths, tail,
        [query_own, query_xy, query_xy, query_d], (0, 0, slab, 0),
        [received_xy, received_own, received_d, received_xy], (0, 0, 0, slab),
        [direct_own, direct_xy, direct_xy, direct_d],
        early, late, (far_first, far_second), head_attn, devices)
    incoming = lax.all_to_all(outgoing, ALL_AXES, split_axis=0, concat_axis=0, tiled=True)
    return finish(incoming, packing, n_branch)


def general(rollout, send_rows, seq_lengths, attn_gain, w_query, w_keyval, head_weight, head_attn):
    n_branch = lax.axis_size("branch")
    n_segment = lax.axis_size("segment")
    gen_rows = rollout.shape[0]
    piece_rows = gen_rows // n_segment
    row_width = rollout.shape[1]
    ordered = jnp.take(rollout, send_rows, axis=0).reshape(n_segment, piece_rows, row_width)
    copies = jnp.broadcast_to(ordered[None], (n_branch, n_segment, piece_rows, row_width))
    copies = copies.reshape(n_branch * n_segment, piece_rows, row_width)
    arrived = lax.all_to_all(copies, ("branch", "segment"), split_axis=0, concat_axis=0, tiled=True)
    packed = arrived.reshape(-1, row_width)
    pack_rows = packed.shape[0]
    rows_float = packed.astype(jnp.float32)
    mean_square = jnp.mean(rows_float * rows_float, axis=-1, keepdims=True)
    normed = (
        rows_float * lax.rsqrt(mean_square + epsilon) * attn_gain[0].astype(jnp.float32)
    ).astype(jnp.bfloat16)
    query_acc = jnp.dot(
        normed,
        lax.all_gather(w_query, "segment", axis=1, tiled=True)[0],
        preferred_element_type=jnp.float32,
    )
    keyval_acc = jnp.dot(
        normed,
        lax.all_gather(w_keyval, "segment", axis=1, tiled=True)[0],
        preferred_element_type=jnp.float32,
    )
    queries = query_acc.astype(jnp.bfloat16)
    keyval_part = keyval_acc.astype(jnp.bfloat16)
    keyval = lax.all_gather(keyval_part, "tp", axis=1, tiled=True)
    tp_index = lax.axis_index("tp")
    heads_here = queries.shape[1] // HEAD
    group_size = HEADS // KV_HEADS
    per_group = min(heads_here, group_size)
    group_span = heads_here // per_group
    kv_first = tp_index * heads_here // group_size
    key_rows = lax.dynamic_slice_in_dim(keyval, kv_first * HEAD, group_span * HEAD, 1)
    value_rows = lax.dynamic_slice_in_dim(
        keyval, KV_HEADS * HEAD + kv_first * HEAD, group_span * HEAD, 1
    )
    key_rows = key_rows.reshape(pack_rows, group_span, HEAD)
    value_rows = value_rows.reshape(pack_rows, group_span, HEAD)
    queries = queries.reshape(pack_rows, group_span, per_group, HEAD)
    positions = jnp.arange(pack_rows, dtype=jnp.int32)
    doc_ends = jnp.cumsum(seq_lengths[0])
    doc_ids = jnp.sum((positions[:, None] >= doc_ends[None, :]).astype(jnp.int32), axis=-1)
    visible = (doc_ids[:, None] == doc_ids[None, :]) & (positions[None, :] <= positions[:, None])
    logits = jnp.einsum(
        "qgpc,kgc->gpqk", queries, key_rows, preferred_element_type=jnp.float32
    ) / math.sqrt(HEAD)
    logits = jnp.where(visible[None, None], logits, -1e30)
    row_max = jnp.max(logits, axis=-1, keepdims=True)
    expo = jnp.exp(logits - row_max)
    probabilities = (expo / jnp.sum(expo, axis=-1, keepdims=True)).astype(jnp.bfloat16)
    attended = jnp.einsum(
        "gpqk,kgc->qgpc", probabilities, value_rows, preferred_element_type=jnp.float32
    )
    attended = attended.reshape(pack_rows, heads_here * HEAD)
    slice_width = head_weight.shape[1]
    own_columns = lax.dynamic_slice_in_dim(packed, tp_index * slice_width, slice_width, 1)
    direct = jnp.dot(own_columns, head_weight[0], preferred_element_type=jnp.float32)
    through = jnp.dot(attended, head_attn[0].astype(jnp.float32), precision=lax.Precision.HIGHEST)
    totals = lax.psum(direct + through, "tp")
    outgoing = totals.reshape(n_branch * n_segment, piece_rows)
    incoming = lax.all_to_all(
        outgoing, ("branch", "segment"), split_axis=0, concat_axis=0, tiled=True
    )
    incoming = incoming.reshape(n_branch, n_segment * piece_rows)
    scores = jnp.zeros((n_branch, gen_rows), jnp.float32).at[:, send_rows].set(incoming)
    return scores


def solution(mesh):
    sizes = tuple(mesh.shape[axis] for axis in ALL_AXES)
    pairwise = sizes == (4, 2, 4)
    local = paired if pairwise else general
    return jax.shard_map(
        local,
        mesh=mesh,
        in_specs=(
            P(("branch", "segment"), None),
            P(("branch", "segment")),
            P("segment", None),
            P("branch", None),
            P("branch", "segment", "tp"),
            P("branch", "segment", "tp"),
            P("branch", "tp"),
            P("branch", "tp"),
        ),
        out_specs=P(None, ("branch", "segment")),
        check_vma=False,
    )
```

```python
import functools
import math

import jax
import jax.numpy as jnp
from jax import lax
from jax.experimental import pallas as pl
from jax.experimental.pallas import tpu as pltpu
from jax.sharding import PartitionSpec as P


HEAD = 128
HEADS = 64
KV_HEADS = 8
LANES = 128
LENGTHS_AT = 8

epsilon = 1e-05

ALL_AXES = ("branch", "segment", "tp")
HIGHEST = lax.Precision.HIGHEST
F32 = jnp.float32
BF16 = jnp.bfloat16


def whole(memory_space=pltpu.VMEM):
    return pl.BlockSpec(memory_space=memory_space)


def iota(shape, dimension):
    return lax.broadcasted_iota(jnp.int32, shape, dimension)


def prepare_kernel(ids_ref, lengths_ref, rows_hbm, send_hbm, mine_ref, theirs_ref, rows_ref, send_ref, sems):
    count, width = rows_ref.shape
    half = width // 2
    parts = sems.shape[0] - 1
    step = width // parts
    core, segment = ids_ref[0], ids_ref[1]
    copies = [pltpu.make_async_copy(send_hbm, send_ref, sems.at[parts])]
    for part in range(parts):
        at = pl.ds(part * step, step)
        copies.append(pltpu.make_async_copy(rows_hbm.at[:, at], rows_ref.at[:, at], sems.at[part]))
    for copy in copies:
        copy.start()
    copies[0].wait()
    send = send_ref[...]
    rolled = jnp.concatenate([send[:, count // 2:], send[:, :count // 2]], axis=1)
    order = jnp.where(core == 1, rolled, send)
    pick = (iota((count, count), 0) == order).astype(BF16)

    def ordered(part):
        out = lax.dot_general(pick, part, (((0,), (0,)), ((), ())), preferred_element_type=F32)
        return out.astype(BF16)

    lanes = jnp.zeros((count, LANES), F32)
    for part in range(parts):
        copies[1 + part].wait()
        square = rows_ref[:, part * step:(part + 1) * step].astype(F32)
        square = square * square
        for lane in range(0, step, LANES):
            lanes = lanes + square[:, lane:lane + LANES]
    chunk = 1024
    for start in range(0, half, chunk):
        for out_ref, which in ((theirs_ref, 1 - segment), (mine_ref, segment)):
            at = pl.multiple_of(which * half + start, chunk)
            out_ref[:, start:start + chunk] = ordered(rows_ref[:, pl.ds(at, chunk)])
    scale = lax.rsqrt(jnp.sum(lanes, axis=1, keepdims=True) * (1.0 / width) + epsilon)
    high = scale.astype(BF16).astype(F32)
    middle = (scale - high).astype(BF16).astype(F32)
    low = scale - high - middle
    lane = iota((count, LANES), 1)
    tail = jnp.where(lane == 0, high, jnp.where(lane == 1, middle, jnp.where(lane == 2, low, 0.0)))
    tail = ordered(tail.astype(BF16))
    for index in range(lengths_ref.shape[1]):
        length = lengths_ref[0, index].astype(F32).astype(BF16)
        tail = jnp.where(lane == LENGTHS_AT + index, length, tail)
    theirs_ref[:, half:] = tail
    mine_ref[:, half:] = tail


def prepare(ids, lengths, rows, send):
    count, width = rows.shape
    shape = jax.ShapeDtypeStruct((count, width // 2 + LANES), BF16)
    return pl.pallas_call(
        prepare_kernel,
        out_shape=(shape, shape),
        in_specs=[whole(pltpu.SMEM), whole(pltpu.SMEM), whole(pltpu.HBM), whole(pltpu.HBM)],
        out_specs=(whole(), whole()),
        scratch_shapes=[
            pltpu.VMEM((count, width), BF16),
            pltpu.VMEM((1, count), jnp.int32),
            pltpu.SemaphoreType.DMA((5,)),
        ],
        compiler_params=pltpu.CompilerParams(vmem_limit_bytes=12 << 20),
        name="prepare",
    )(ids, lengths, rows, send)


BLOCK = 256
IN_FLIGHT = 4


def column_copies(source, first, target, sems):
    blocks = target.shape[1] // BLOCK
    return [
        pltpu.make_async_copy(
            source.at[:, pl.ds(pl.multiple_of(first + index * BLOCK, BLOCK), BLOCK)],
            target.at[:, pl.ds(index * BLOCK, BLOCK)], sems.at[index])
        for index in range(blocks)]


def split_slots(values):
    return values[:, :HEAD], values[:, HEAD:]


def chunk_body(ids_ref, pieces, gain_ref, head_ref, keyval_ref, query_ref, outs, waits, recv=None):
    rows_ref, direct_ref = outs[:2]
    count = pieces[0].shape[0]
    half = rows_ref.shape[1]
    core, segment, tp = ids_ref[0], ids_ref[1], ids_ref[3]
    columns = query_ref.shape[1]
    top = (iota((count, 1), 0) < count // 2).astype(jnp.int32)
    mask = (top ^ core) == 1

    def sorted_rows(values):
        near, far = values[0::2], values[1::2]
        return jnp.concatenate(
            [part for n, f in zip(near, far) for part in (jnp.where(mask, n, f), jnp.where(mask, f, n))], axis=0)

    first_lanes = iota((count, LANES), 1) < 3
    scale = sorted_rows([
        jnp.sum(jnp.where(first_lanes, ref[:, half:].astype(F32), 0.0), axis=1, keepdims=True) for ref in pieces])
    chunk = 512
    direct = jnp.zeros((direct_ref.shape[0], LANES), F32)
    for start in range(0, half, chunk):
        at = slice(start, start + chunk)
        rows = sorted_rows([ref[:, at].astype(F32) for ref in pieces])
        weight = head_ref[:, at].astype(F32)
        for lane in range(0, chunk, LANES):
            direct = direct + rows[:, lane:lane + LANES] * weight[:, lane:lane + LANES]
        rows_ref[:, at] = (rows * scale * gain_ref[:, at].astype(F32)).astype(BF16)
    direct_ref[...] = direct

    for wait in waits[:keyval_ref.shape[1] // BLOCK]:
        wait()
    keyval = jnp.dot(rows_ref[...], keyval_ref[...], preferred_element_type=F32)
    even = jnp.concatenate([keyval[:, :HEAD], keyval[:, 2 * HEAD:3 * HEAD]], axis=1)
    odd = jnp.concatenate([keyval[:, HEAD:2 * HEAD], keyval[:, 3 * HEAD:]], axis=1)
    own = jnp.where(segment == 0, even, odd)
    other = jnp.where(segment == 0, odd, even)
    if recv is None:
        own_ref, send_ref = outs[2:4]
        own_ref[...] = own
        if len(outs) > 4:
            outs[4][...] = other.astype(BF16)
        else:
            send_ref[:, columns:] = other.astype(BF16)
    else:
        send_ref, keep_ref, first_ref, second_ref, far_first_ref, far_second_ref = outs[2:]
        own_part_ref, pair_part_ref, recv_own_ref, recv_next_ref = recv
        slab = 2 * count
        mine, x_part, y_part = slabs((own_part_ref, pair_part_ref, pair_part_ref), (0, 0, slab), slab)
        at = slice(columns, columns + 2 * HEAD)
        sums = [mine + recv_own_ref[:slab, :].astype(F32), x_part + recv_next_ref[:, at].astype(F32), y_part,
                own + recv_own_ref[slab:, :].astype(F32)]
        low, high = split_slots(jnp.concatenate([by_pack(sums, pack) for pack in range(2)], axis=0))
        keep_ref[...] = jnp.where(tp == 3, high, low).astype(BF16)
        first_ref[...] = jnp.where(tp < 2, high, low).astype(BF16)
        second_ref[...] = jnp.where(tp == 2, high, low).astype(BF16)
        low, high = split_slots(other)
        far_first_ref[...] = jnp.where(tp < 2, high, low).astype(BF16)
        far_second_ref[...] = jnp.where(tp < 2, low, high).astype(BF16)
    waits = waits[keyval_ref.shape[1] // BLOCK:]
    for index in range(columns // BLOCK):
        if waits:
            waits[index]()
        at = slice(index * BLOCK, (index + 1) * BLOCK)
        send_ref[:, at] = jnp.dot(rows_ref[...], query_ref[:, at], preferred_element_type=F32).astype(BF16)


def first_chunk_kernel(ids_ref, near_ref, far_ref, gain_hbm, head_hbm, keyval_hbm, query_hbm, *refs):
    outs, (gain_ref, head_ref, keyval_ref, query_ref) = refs[:4], refs[4:8]
    own_query_ref, part_ref, small_sems, sems, own_sems = refs[8:]
    rows_ref = outs[0]
    half = rows_ref.shape[1]
    segment, tp = ids_ref[1], ids_ref[3]
    small = [
        pltpu.make_async_copy(
            gain_hbm.at[:, pl.ds(pl.multiple_of(segment * half, half), half)], gain_ref, small_sems.at[0]),
        pltpu.make_async_copy(head_hbm, part_ref, small_sems.at[1]),
    ]
    blocks = keyval_ref.shape[1] // BLOCK
    large = column_copies(keyval_hbm, 0, keyval_ref, sems)
    large += column_copies(query_hbm, (1 - segment) * query_ref.shape[1], query_ref, sems.at[pl.ds(blocks, query_ref.shape[1] // BLOCK)])
    owns = column_copies(query_hbm, segment * query_ref.shape[1], own_query_ref, own_sems)
    copies = large + owns
    for copy in small + copies[:IN_FLIGHT]:
        copy.start()

    def waiter(index):
        def wait():
            copies[index].wait()
            if index + IN_FLIGHT < len(copies):
                copies[index + IN_FLIGHT].start()

        return wait

    waits = [waiter(index) for index in range(len(copies))]
    for copy in small:
        copy.wait()
    width = part_ref.shape[1]
    head_ref[...] = jnp.zeros_like(head_ref)

    @pl.when((tp * width) // half == segment)
    def _():
        head_ref[:, pl.ds(pl.multiple_of((tp * width) % half, width), width)] = part_ref[...]

    chunk_body(ids_ref, (near_ref, far_ref), gain_ref, head_ref, keyval_ref, query_ref, outs,
               waits[:len(large)])
    for wait in waits[len(large):]:
        wait()


def next_chunk_kernel(ids_ref, *refs, chips):
    pieces, refs = refs[:2 * chips], refs[2 * chips:]
    chunk_body(ids_ref, pieces, *refs[:4], refs[4:], [])


def last_chunk_kernel(ids_ref, *refs):
    chunk_body(ids_ref, refs[:2], *refs[2:6], refs[10:], [], refs[6:10])


def shape_of(*shape, kind=BF16):
    return jax.ShapeDtypeStruct(shape, kind)


def chunk_shapes(rows, half):
    return (shape_of(rows, half), shape_of(rows, LANES, kind=F32))


def first_chunk(ids, near, far, gain, head, keyval, query):
    count, wide = near.shape
    half = wide - LANES
    columns = query.shape[1] // 2
    rows = 2 * count
    shapes = chunk_shapes(rows, half) + (
        shape_of(rows, 2 * HEAD, kind=F32), shape_of(rows, columns + 2 * HEAD),
        shape_of(1, half), shape_of(1, half), shape_of(*keyval.shape), shape_of(half, columns),
        shape_of(half, columns))
    out = pl.pallas_call(
        first_chunk_kernel,
        out_shape=shapes,
        in_specs=[whole(pltpu.SMEM), whole(), whole()] + [whole(pltpu.HBM)] * 4,
        out_specs=(whole(),) * len(shapes),
        scratch_shapes=[
            pltpu.VMEM(head.shape, BF16),
            pltpu.SemaphoreType.DMA((2,)),
            pltpu.SemaphoreType.DMA(((columns + keyval.shape[1]) // BLOCK,)),
            pltpu.SemaphoreType.DMA((columns // BLOCK,)),
        ],
        compiler_params=pltpu.CompilerParams(vmem_limit_bytes=14 << 20),
        name="first_chunk",
    )(ids, near, far, gain, head, keyval, query)
    return out[:4], out[4:8], out[8]


def next_chunk(ids, pieces, weights):
    count, wide = pieces[0].shape
    chips = len(pieces) // 2
    rows = 2 * chips * count
    shapes = chunk_shapes(rows, wide - LANES) + (
        shape_of(rows, 2 * HEAD, kind=F32), shape_of(rows, weights[3].shape[1]), shape_of(rows, 2 * HEAD))
    return pl.pallas_call(
        functools.partial(next_chunk_kernel, chips=chips),
        out_shape=shapes,
        in_specs=[whole(pltpu.SMEM)] + [whole()] * (len(pieces) + 4),
        out_specs=(whole(),) * len(shapes),
        compiler_params=pltpu.CompilerParams(vmem_limit_bytes=14 << 20),
        name="next_chunk",
    )(ids, *pieces, *weights)


def last_chunk(ids, pieces, weights, parts):
    count, wide = pieces[0].shape
    rows = 2 * count
    shapes = chunk_shapes(rows, wide - LANES) + (
        shape_of(rows, weights[3].shape[1]),) + (shape_of(4 * rows, HEAD),) * 3 + (shape_of(rows, HEAD),) * 2
    return pl.pallas_call(
        last_chunk_kernel,
        out_shape=shapes,
        in_specs=[whole(pltpu.SMEM)] + [whole()] * (len(pieces) + 8),
        out_specs=(whole(),) * len(shapes),
        compiler_params=pltpu.CompilerParams(vmem_limit_bytes=14 << 20),
        name="last_chunk",
    )(ids, *pieces, *weights, *parts)


def own_body(rows_ref, query_ref, out_ref, waits=()):
    for index in range(query_ref.shape[1] // BLOCK):
        if waits:
            waits[index]()
        at = slice(index * BLOCK, (index + 1) * BLOCK)
        out_ref[:, at] = jnp.dot(rows_ref[...], query_ref[:, at], preferred_element_type=F32)


def own_queries(rows, query):
    return pl.pallas_call(
        own_body,
        out_shape=shape_of(rows.shape[0], query.shape[1], kind=F32),
        in_specs=[whole(), whole()],
        out_specs=whole(),
        compiler_params=pltpu.CompilerParams(vmem_limit_bytes=10 << 20),
        name="own_queries",
    )(rows, query)


def slabs(refs, starts, count, at=slice(None)):
    return [ref[start:start + count, at].astype(F32) for ref, start in zip(refs, starts)]


def by_pack(parts, pack):
    count = parts[0].shape[0] // 2
    return jnp.concatenate([part[pack * count:(pack + 1) * count] for part in parts], axis=0)


def owner_of(row, pack, ids_ref, piece_rows):
    index = jnp.zeros_like(row)
    for step in range(1, 8):
        index = index + (row >= step * piece_rows).astype(jnp.int32)
    chip, low = index >> 1, index & 1
    shard = (((chip >> 1) ^ ids_ref[2]) * 2 + (low ^ pack)) * 2 + ((chip & 1) ^ ids_ref[1])
    return shard, row - index * piece_rows


def mask_kernel(ids_ref, lengths_ref, near_ref, out_ref):
    segment = ids_ref[1]
    rows = out_ref.shape[1]
    piece_rows = rows // 8
    tail = near_ref[:, near_ref.shape[1] - LANES:].astype(F32)[:1].astype(jnp.int32)
    for pack in range(2):
        def place(row):
            shard, inner = owner_of(row, pack, ids_ref, piece_rows)
            position = shard * piece_rows + inner
            end = jnp.zeros((1, 1), jnp.int32)
            doc = jnp.zeros_like(position)
            for index in range(lengths_ref.shape[1]):
                at = LENGTHS_AT + index
                end = end + jnp.where(segment == pack, lengths_ref[0, index], tail[:, at:at + 1])
                doc = doc + (position >= end).astype(jnp.int32)
            return position, doc

        row_position, row_doc = place(iota((rows, 1), 0))
        col_position, col_doc = place(iota((1, rows), 1))
        visible = jnp.logical_and(row_doc == col_doc, col_position <= row_position)
        out_ref[pack * rows:(pack + 1) * rows, :] = jnp.where(visible, 0.0, -1e30)


def masks(ids, lengths, near, rows):
    return pl.pallas_call(
        mask_kernel,
        out_shape=shape_of(2 * rows, rows, kind=F32),
        in_specs=[whole(pltpu.SMEM), whole(pltpu.SMEM), whole()],
        out_specs=whole(),
        compiler_params=pltpu.CompilerParams(vmem_limit_bytes=4 << 20),
        name="masks",
    )(ids, lengths, near)


def attention_kernel(ids_ref, bias_ref, *refs, starts, recv_starts):
    chips = len(starts)
    owns, recvs, directs = (refs[index * chips:(index + 1) * chips] for index in range(3))
    refs = refs[3 * chips:]
    nears, fars, gain_ref, out_ref = refs[0:3], refs[3:5], refs[5], refs[6]
    segment, tp = ids_ref[1], ids_ref[3]
    rows = bias_ref.shape[1]
    slab = rows // 2
    queries = rows
    piece_rows = rows // 8
    heads = owns[0].shape[1] // HEAD
    devices = out_ref.shape[0]
    wide = out_ref.shape[1] // 2
    scale = math.log2(math.e) / math.sqrt(HEAD)
    lane = iota((queries, wide), 1)

    def chosen_keys(refs):
        keep, first, second = (ref[...].astype(F32) for ref in refs)
        return (jnp.where(tp == 0, keep, jnp.where(tp == 2, second, first)),
                jnp.where(tp == 3, keep, jnp.where(tp == 1, second, first)))

    def pack_part(part, pack):
        count = part.shape[0] // 2
        return part[pack * count:(pack + 1) * count]

    far_first, far_second = (ref[...].astype(F32) for ref in fars)
    odd = (tp & 1) == 1
    far = (jnp.where(odd, far_first, far_second), jnp.where(odd, far_second, far_first))
    near = chosen_keys(nears)
    through = jnp.zeros((devices, wide), F32)
    direct = jnp.zeros((devices, wide), F32)
    for pack in range(2):
        keys, values = (
            jnp.concatenate([
                pack_part(near_part, pack)[:slab],
                pack_part(near_part, pack)[slab:slab + slab // 2] + pack_part(far_part, pack),
                pack_part(near_part, pack)[slab + slab // 2:]], axis=0).astype(BF16)
            for near_part, far_part in zip(near, far))
        values = jnp.concatenate([values, jnp.ones((rows, HEAD), BF16)], axis=1)
        total = jnp.zeros((queries, HEAD), F32)
        for head in range(heads):
            at = slice(head * HEAD, (head + 1) * HEAD)
            parts = [own + recv for own, recv in zip(
                slabs(owns, starts, slab, at), slabs(recvs, recv_starts, slab, at))]
            query = (by_pack(parts, pack) * scale).astype(BF16)
            logits = lax.dot_general(query, keys, (((1,), (1,)), ((), ())), preferred_element_type=F32)
            logits = logits + bias_ref[pack * rows:(pack + 1) * rows, :]
            expo = jnp.exp2(logits - jnp.max(logits, axis=1, keepdims=True)).astype(BF16)
            both = jnp.dot(expo, values, preferred_element_type=F32)
            offset = pl.multiple_of(segment * heads * HEAD + head * HEAD, HEAD)
            total = total + both[:, :HEAD] / both[:, HEAD:] * gain_ref[:, pl.ds(offset, HEAD)].astype(F32)

        _, inner = owner_of(iota((queries, 1), 0), pack, ids_ref, piece_rows)
        shard_row, _ = owner_of(iota((1, queries), 1), pack, ids_ref, piece_rows)
        chosen = ((iota((devices, 1), 0) >> 2) == shard_row).astype(F32)
        hit = lane == inner + pack * piece_rows

        def send(column):
            return jnp.dot(chosen, jnp.where(hit, column, 0.0), precision=HIGHEST, preferred_element_type=F32)

        through = through + send(jnp.sum(total, axis=1, keepdims=True))
        direct = direct + send(jnp.sum(by_pack(slabs(directs, starts, slab), pack), axis=1, keepdims=True))
    out_ref[:, :wide] = through
    out_ref[:, wide:] = direct


def attention(ids, bias, owns, starts, recvs, recv_starts, directs, near, far, gain, devices):
    return pl.pallas_call(
        functools.partial(attention_kernel, starts=starts, recv_starts=recv_starts),
        out_shape=shape_of(devices, 2 * LANES, kind=F32),
        in_specs=[whole(pltpu.SMEM)] + [whole()] * (7 + 3 * len(owns)),
        out_specs=whole(),
        compiler_params=pltpu.CompilerParams(vmem_limit_bytes=14 << 20),
        name="attend",
    )(ids, bias, *owns, *recvs, *directs, *near, *far, gain)


def finish_kernel(recv_ref, send_ref, out_ref):
    models, count = out_ref.shape
    devices, width = recv_ref.shape
    model_of = iota((models, devices), 1) // (devices // models)
    chosen = (model_of == iota((models, devices), 0)).astype(F32)
    sums = jnp.dot(chosen, recv_ref[...], precision=HIGHEST, preferred_element_type=F32)
    pick = (iota((count, count), 0) == send_ref[...]).astype(F32)
    half = width // 2
    both = sums[:, :count] + sums[:, half:half + count]
    out_ref[...] = lax.dot_general(
        both, pick, (((1,), (1,)), ((), ())), precision=HIGHEST, preferred_element_type=F32)


def finish(recv, send, models):
    count = send.shape[1]
    return pl.pallas_call(
        finish_kernel,
        out_shape=jax.ShapeDtypeStruct((models, count), F32),
        in_specs=[whole()] * 2,
        out_specs=whole(),
        compiler_params=pltpu.CompilerParams(vmem_limit_bytes=8 << 20),
        name="finish",
    )(recv, send)


def paired(rollout, send_rows, seq_lengths, attn_gain, w_query, w_keyval, head_weight, head_attn):
    n_branch = lax.axis_size("branch")
    branch = lax.axis_index("branch")
    segment = lax.axis_index("segment")
    tp = lax.axis_index("tp")
    send = send_rows.reshape(1, -1)
    ids = jnp.stack([branch & 1, segment, branch >> 1, tp]).astype(jnp.int32)

    core_pairs = [(i, i ^ 1) for i in range(n_branch)]
    y_pairs = [(i, i ^ 2) for i in range(n_branch)]
    x_pairs = [(0, 1), (1, 0)]

    def swap(piece):
        return lax.ppermute(piece, "branch", core_pairs)

    def across(part):
        return lax.ppermute(part, "segment", x_pairs)

    def in_hbm(array):
        return pltpu.with_memory_space_constraint(array, pltpu.HBM)

    packing = send
    rollout, send, attn_gain, head_weight, seq_lengths = map(
        in_hbm, (rollout, send, attn_gain, head_weight, seq_lengths))
    wq, wkv = in_hbm(w_query[0]), in_hbm(w_keyval[0])
    mine, theirs = prepare(ids, seq_lengths, rollout, send)
    from_x = across(theirs)
    from_y = lax.ppermute(mine, "branch", y_pairs)
    from_d = lax.ppermute(from_x, "branch", y_pairs)

    slab = 2 * mine.shape[0]

    def with_swapped(*pieces):
        return [part for piece in pieces for part in (piece, swap(piece))]

    pieces = with_swapped(mine)
    (rows, direct_own, local_own, part), weights, own_weights = first_chunk(
        ids, *pieces, attn_gain, head_weight, wkv, wq)
    received_own = across(part)
    query_own = own_queries(rows, own_weights)
    bias = masks(ids, seq_lengths, from_x, 2 * slab)

    pieces = with_swapped(from_x, from_y)
    rows, direct_xy, local_xy, part, keyval = next_chunk(ids, pieces, weights)
    keyval_xy = across(keyval)
    received_xy = across(part)
    query_xy = own_queries(rows, own_weights)

    hand_first, hand_second = (1, 3, 0, 2), (0, 2, 1, 3)
    n_tp = len(hand_first)

    def hand(array, targets):
        return lax.ppermute(array, "tp", [(i, to) for i, to in enumerate(targets) if i != to])

    def hand_across(array, targets):
        return lax.ppermute(array, ("segment", "tp"), [
            (side * n_tp + i, (1 - side) * n_tp + to) for side in range(2) for i, to in enumerate(targets)])

    pieces = with_swapped(from_d)
    rows, direct_d, part, keep, first, second, far_first, far_second = last_chunk(
        ids, pieces, weights, (local_own, local_xy, keyval_xy, received_own))
    received_d = across(part)
    first = hand(first, hand_first)
    second = hand(second, hand_second)
    far_first = hand_across(far_first, hand_first)
    far_second = hand_across(far_second, hand_second)
    query_d = own_queries(rows, own_weights)
    devices = n_branch * 2 * n_tp
    outgoing = attention(
        ids, bias, [query_own, query_xy, query_xy, query_d], (0, 0, slab, 0),
        [received_xy, received_own, received_d, received_xy], (0, 0, 0, slab),
        [direct_own, direct_xy, direct_xy, direct_d],
        (keep, first, second), (far_first, far_second), head_attn, devices)
    incoming = lax.all_to_all(outgoing, ALL_AXES, split_axis=0, concat_axis=0, tiled=True)
    return finish(incoming, packing, n_branch)


def general(rollout, send_rows, seq_lengths, attn_gain, w_query, w_keyval, head_weight, head_attn):
    n_branch = lax.axis_size("branch")
    n_segment = lax.axis_size("segment")
    gen_rows = rollout.shape[0]
    piece_rows = gen_rows // n_segment
    row_width = rollout.shape[1]
    ordered = jnp.take(rollout, send_rows, axis=0).reshape(n_segment, piece_rows, row_width)
    copies = jnp.broadcast_to(ordered[None], (n_branch, n_segment, piece_rows, row_width))
    copies = copies.reshape(n_branch * n_segment, piece_rows, row_width)
    arrived = lax.all_to_all(copies, ("branch", "segment"), split_axis=0, concat_axis=0, tiled=True)
    packed = arrived.reshape(-1, row_width)
    pack_rows = packed.shape[0]
    rows_float = packed.astype(jnp.float32)
    mean_square = jnp.mean(rows_float * rows_float, axis=-1, keepdims=True)
    normed = (
        rows_float * lax.rsqrt(mean_square + epsilon) * attn_gain[0].astype(jnp.float32)
    ).astype(jnp.bfloat16)
    query_acc = jnp.dot(
        normed,
        lax.all_gather(w_query, "segment", axis=1, tiled=True)[0],
        preferred_element_type=jnp.float32,
    )
    keyval_acc = jnp.dot(
        normed,
        lax.all_gather(w_keyval, "segment", axis=1, tiled=True)[0],
        preferred_element_type=jnp.float32,
    )
    queries = query_acc.astype(jnp.bfloat16)
    keyval_part = keyval_acc.astype(jnp.bfloat16)
    keyval = lax.all_gather(keyval_part, "tp", axis=1, tiled=True)
    tp_index = lax.axis_index("tp")
    heads_here = queries.shape[1] // HEAD
    group_size = HEADS // KV_HEADS
    per_group = min(heads_here, group_size)
    group_span = heads_here // per_group
    kv_first = tp_index * heads_here // group_size
    key_rows = lax.dynamic_slice_in_dim(keyval, kv_first * HEAD, group_span * HEAD, 1)
    value_rows = lax.dynamic_slice_in_dim(
        keyval, KV_HEADS * HEAD + kv_first * HEAD, group_span * HEAD, 1
    )
    key_rows = key_rows.reshape(pack_rows, group_span, HEAD)
    value_rows = value_rows.reshape(pack_rows, group_span, HEAD)
    queries = queries.reshape(pack_rows, group_span, per_group, HEAD)
    positions = jnp.arange(pack_rows, dtype=jnp.int32)
    doc_ends = jnp.cumsum(seq_lengths[0])
    doc_ids = jnp.sum((positions[:, None] >= doc_ends[None, :]).astype(jnp.int32), axis=-1)
    visible = (doc_ids[:, None] == doc_ids[None, :]) & (positions[None, :] <= positions[:, None])
    logits = jnp.einsum(
        "qgpc,kgc->gpqk", queries, key_rows, preferred_element_type=jnp.float32
    ) / math.sqrt(HEAD)
    logits = jnp.where(visible[None, None], logits, -1e30)
    row_max = jnp.max(logits, axis=-1, keepdims=True)
    expo = jnp.exp(logits - row_max)
    probabilities = (expo / jnp.sum(expo, axis=-1, keepdims=True)).astype(jnp.bfloat16)
    attended = jnp.einsum(
        "gpqk,kgc->qgpc", probabilities, value_rows, preferred_element_type=jnp.float32
    )
    attended = attended.reshape(pack_rows, heads_here * HEAD)
    slice_width = head_weight.shape[1]
    own_columns = lax.dynamic_slice_in_dim(packed, tp_index * slice_width, slice_width, 1)
    direct = jnp.dot(own_columns, head_weight[0], preferred_element_type=jnp.float32)
    through = jnp.dot(attended, head_attn[0].astype(jnp.float32), precision=lax.Precision.HIGHEST)
    totals = lax.psum(direct + through, "tp")
    outgoing = totals.reshape(n_branch * n_segment, piece_rows)
    incoming = lax.all_to_all(
        outgoing, ("branch", "segment"), split_axis=0, concat_axis=0, tiled=True
    )
    incoming = incoming.reshape(n_branch, n_segment * piece_rows)
    scores = jnp.zeros((n_branch, gen_rows), jnp.float32).at[:, send_rows].set(incoming)
    return scores


def solution(mesh):
    sizes = tuple(mesh.shape[axis] for axis in ALL_AXES)
    pairwise = sizes == (4, 2, 4)
    local = paired if pairwise else general
    return jax.shard_map(
        local,
        mesh=mesh,
        in_specs=(
            P(("branch", "segment"), None),
            P(("branch", "segment")),
            P("segment", None),
            P("branch", None),
            P("branch", "segment", "tp"),
            P("branch", "segment", "tp"),
            P("branch", "tp"),
            P("branch", "tp"),
        ),
        out_specs=P(None, ("branch", "segment")),
        check_vma=False,
    )
```

```python
import functools
import math

import jax
import jax.numpy as jnp
from jax import lax
from jax.experimental import pallas as pl
from jax.experimental.pallas import tpu as pltpu
from jax.sharding import PartitionSpec as P


HEAD = 128
HEADS = 64
KV_HEADS = 8
LANES = 128
LENGTHS_AT = 8

epsilon = 1e-05

ALL_AXES = ("branch", "segment", "tp")
HIGHEST = lax.Precision.HIGHEST
F32 = jnp.float32
BF16 = jnp.bfloat16


def whole(memory_space=pltpu.VMEM):
    return pl.BlockSpec(memory_space=memory_space)


def position():
    branch = lax.axis_index("branch")
    return branch & 1, lax.axis_index("segment"), branch >> 1, lax.axis_index("tp")


def iota(shape, dimension):
    return lax.broadcasted_iota(jnp.int32, shape, dimension)


def prepare_kernel(lengths_ref, rows_hbm, send_hbm, mine_ref, theirs_ref, rows_ref, send_ref, sems):
    ids = position()
    count, width = rows_ref.shape
    half = width // 2
    parts = sems.shape[0] - 1
    step = width // parts
    core, segment = ids[0], ids[1]
    copies = [pltpu.make_async_copy(send_hbm, send_ref, sems.at[parts])]
    for part in range(parts):
        at = pl.ds(part * step, step)
        copies.append(pltpu.make_async_copy(rows_hbm.at[:, at], rows_ref.at[:, at], sems.at[part]))
    for copy in copies:
        copy.start()
    copies[0].wait()
    send = send_ref[...]
    rolled = jnp.concatenate([send[:, count // 2:], send[:, :count // 2]], axis=1)
    order = jnp.where(core == 1, rolled, send)
    pick = (iota((count, count), 0) == order).astype(BF16)

    def ordered(part):
        out = lax.dot_general(pick, part, (((0,), (0,)), ((), ())), preferred_element_type=F32)
        return out.astype(BF16)

    lanes = jnp.zeros((count, LANES), F32)
    for part in range(parts):
        copies[1 + part].wait()
        square = rows_ref[:, part * step:(part + 1) * step].astype(F32)
        square = square * square
        for lane in range(0, step, LANES):
            lanes = lanes + square[:, lane:lane + LANES]
    chunk = 1024
    for start in range(0, half, chunk):
        for out_ref, which in ((theirs_ref, 1 - segment), (mine_ref, segment)):
            at = pl.multiple_of(which * half + start, chunk)
            out_ref[:, start:start + chunk] = ordered(rows_ref[:, pl.ds(at, chunk)])
    scale = lax.rsqrt(jnp.sum(lanes, axis=1, keepdims=True) * (1.0 / width) + epsilon)
    high = scale.astype(BF16).astype(F32)
    middle = (scale - high).astype(BF16).astype(F32)
    low = scale - high - middle
    lane = iota((count, LANES), 1)
    tail = jnp.where(lane == 0, high, jnp.where(lane == 1, middle, jnp.where(lane == 2, low, 0.0)))
    tail = ordered(tail.astype(BF16))
    for index in range(lengths_ref.shape[1]):
        length = lengths_ref[0, index].astype(F32).astype(BF16)
        tail = jnp.where(lane == LENGTHS_AT + index, length, tail)
    theirs_ref[:, half:] = tail
    mine_ref[:, half:] = tail


def prepare(lengths, rows, send):
    count, width = rows.shape
    shape = jax.ShapeDtypeStruct((count, width // 2 + LANES), BF16)
    return pl.pallas_call(
        prepare_kernel,
        out_shape=(shape, shape),
        in_specs=[whole(pltpu.SMEM), whole(pltpu.HBM), whole(pltpu.HBM)],
        out_specs=(whole(), whole()),
        scratch_shapes=[
            pltpu.VMEM((count, width), BF16),
            pltpu.VMEM((1, count), jnp.int32),
            pltpu.SemaphoreType.DMA((5,)),
        ],
        compiler_params=pltpu.CompilerParams(vmem_limit_bytes=12 << 20),
        name="prepare",
    )(lengths, rows, send)


BLOCK = 256
IN_FLIGHT = 4


def column_copies(source, first, target, sems):
    blocks = target.shape[1] // BLOCK
    return [
        pltpu.make_async_copy(
            source.at[:, pl.ds(pl.multiple_of(first + index * BLOCK, BLOCK), BLOCK)],
            target.at[:, pl.ds(index * BLOCK, BLOCK)], sems.at[index])
        for index in range(blocks)]


def split_slots(values):
    return values[:, :HEAD], values[:, HEAD:]


def chunk_body(pieces, gain_ref, head_ref, keyval_ref, query_ref, outs, waits, recv=None):
    rows_ref, direct_ref = outs[:2]
    count = pieces[0].shape[0]
    half = rows_ref.shape[1]
    core, segment, _, tp = position()
    columns = query_ref.shape[1]
    top = (iota((count, 1), 0) < count // 2).astype(jnp.int32)
    mask = (top ^ core) == 1

    def sorted_rows(values):
        near, far = values[0::2], values[1::2]
        return jnp.concatenate(
            [part for n, f in zip(near, far) for part in (jnp.where(mask, n, f), jnp.where(mask, f, n))], axis=0)

    first_lanes = iota((count, LANES), 1) < 3
    scale = sorted_rows([
        jnp.sum(jnp.where(first_lanes, ref[:, half:].astype(F32), 0.0), axis=1, keepdims=True) for ref in pieces])
    chunk = 512
    direct = jnp.zeros((direct_ref.shape[0], LANES), F32)
    for start in range(0, half, chunk):
        at = slice(start, start + chunk)
        rows = sorted_rows([ref[:, at].astype(F32) for ref in pieces])
        weight = head_ref[:, at].astype(F32)
        for lane in range(0, chunk, LANES):
            direct = direct + rows[:, lane:lane + LANES] * weight[:, lane:lane + LANES]
        rows_ref[:, at] = (rows * scale * gain_ref[:, at].astype(F32)).astype(BF16)
    direct_ref[...] = direct

    for wait in waits[:keyval_ref.shape[1] // BLOCK]:
        wait()
    keyval = jnp.dot(rows_ref[...], keyval_ref[...], preferred_element_type=F32)
    even = jnp.concatenate([keyval[:, :HEAD], keyval[:, 2 * HEAD:3 * HEAD]], axis=1)
    odd = jnp.concatenate([keyval[:, HEAD:2 * HEAD], keyval[:, 3 * HEAD:]], axis=1)
    own = jnp.where(segment == 0, even, odd)
    other = jnp.where(segment == 0, odd, even)
    if recv is None:
        own_ref, send_ref = outs[2:4]
        own_ref[...] = own
        if len(outs) > 4:
            outs[4][...] = other.astype(BF16)
        else:
            send_ref[:, columns:] = other.astype(BF16)
    else:
        send_ref, keep_ref, first_ref, second_ref, far_first_ref, far_second_ref = outs[2:]
        own_part_ref, pair_part_ref, recv_own_ref, recv_next_ref = recv
        slab = 2 * count
        mine, x_part, y_part = slabs((own_part_ref, pair_part_ref, pair_part_ref), (0, 0, slab), slab)
        at = slice(columns, columns + 2 * HEAD)
        sums = [mine + recv_own_ref[:slab, :].astype(F32), x_part + recv_next_ref[:, at].astype(F32), y_part,
                own + recv_own_ref[slab:, :].astype(F32)]
        low, high = split_slots(jnp.concatenate([by_pack(sums, pack) for pack in range(2)], axis=0))
        keep_ref[...] = jnp.where(tp == 3, high, low).astype(BF16)
        first_ref[...] = jnp.where(tp < 2, high, low).astype(BF16)
        second_ref[...] = jnp.where(tp == 2, high, low).astype(BF16)
        low, high = split_slots(other)
        far_first_ref[...] = jnp.where(tp < 2, high, low).astype(BF16)
        far_second_ref[...] = jnp.where(tp < 2, low, high).astype(BF16)
    waits = waits[keyval_ref.shape[1] // BLOCK:]
    for index in range(columns // BLOCK):
        if waits:
            waits[index]()
        at = slice(index * BLOCK, (index + 1) * BLOCK)
        send_ref[:, at] = jnp.dot(rows_ref[...], query_ref[:, at], preferred_element_type=F32).astype(BF16)


def first_chunk_kernel(near_ref, far_ref, gain_hbm, head_hbm, keyval_hbm, query_hbm, *refs):
    outs, (gain_ref, head_ref, keyval_ref, query_ref) = refs[:4], refs[4:8]
    own_query_ref, part_ref, small_sems, sems, own_sems = refs[8:]
    rows_ref = outs[0]
    half = rows_ref.shape[1]
    _, segment, _, tp = position()
    small = [
        pltpu.make_async_copy(
            gain_hbm.at[:, pl.ds(pl.multiple_of(segment * half, half), half)], gain_ref, small_sems.at[0]),
        pltpu.make_async_copy(head_hbm, part_ref, small_sems.at[1]),
    ]
    blocks = keyval_ref.shape[1] // BLOCK
    large = column_copies(keyval_hbm, 0, keyval_ref, sems)
    large += column_copies(query_hbm, (1 - segment) * query_ref.shape[1], query_ref, sems.at[pl.ds(blocks, query_ref.shape[1] // BLOCK)])
    owns = column_copies(query_hbm, segment * query_ref.shape[1], own_query_ref, own_sems)
    copies = large + owns
    for copy in small + copies[:IN_FLIGHT]:
        copy.start()

    def waiter(index):
        def wait():
            copies[index].wait()
            if index + IN_FLIGHT < len(copies):
                copies[index + IN_FLIGHT].start()

        return wait

    waits = [waiter(index) for index in range(len(copies))]
    for copy in small:
        copy.wait()
    width = part_ref.shape[1]
    head_ref[...] = jnp.zeros_like(head_ref)

    @pl.when((tp * width) // half == segment)
    def _():
        head_ref[:, pl.ds(pl.multiple_of((tp * width) % half, width), width)] = part_ref[...]

    chunk_body((near_ref, far_ref), gain_ref, head_ref, keyval_ref, query_ref, outs,
               waits[:len(large)])
    for wait in waits[len(large):]:
        wait()


def next_chunk_kernel(*refs, chips):
    pieces, refs = refs[:2 * chips], refs[2 * chips:]
    chunk_body(pieces, *refs[:4], refs[4:], [])


def last_chunk_kernel(*refs):
    chunk_body(refs[:2], *refs[2:6], refs[10:], [], refs[6:10])


def shape_of(*shape, kind=BF16):
    return jax.ShapeDtypeStruct(shape, kind)


def chunk_shapes(rows, half):
    return (shape_of(rows, half), shape_of(rows, LANES, kind=F32))


def first_chunk(near, far, gain, head, keyval, query):
    count, wide = near.shape
    half = wide - LANES
    columns = query.shape[1] // 2
    rows = 2 * count
    shapes = chunk_shapes(rows, half) + (
        shape_of(rows, 2 * HEAD, kind=F32), shape_of(rows, columns + 2 * HEAD),
        shape_of(1, half), shape_of(1, half), shape_of(*keyval.shape), shape_of(half, columns),
        shape_of(half, columns))
    out = pl.pallas_call(
        first_chunk_kernel,
        out_shape=shapes,
        in_specs=[whole(), whole()] + [whole(pltpu.HBM)] * 4,
        out_specs=(whole(),) * len(shapes),
        scratch_shapes=[
            pltpu.VMEM(head.shape, BF16),
            pltpu.SemaphoreType.DMA((2,)),
            pltpu.SemaphoreType.DMA(((columns + keyval.shape[1]) // BLOCK,)),
            pltpu.SemaphoreType.DMA((columns // BLOCK,)),
        ],
        compiler_params=pltpu.CompilerParams(vmem_limit_bytes=14 << 20),
        name="first_chunk",
    )(near, far, gain, head, keyval, query)
    return out[:4], out[4:8], out[8]


def next_chunk(pieces, weights):
    count, wide = pieces[0].shape
    chips = len(pieces) // 2
    rows = 2 * chips * count
    shapes = chunk_shapes(rows, wide - LANES) + (
        shape_of(rows, 2 * HEAD, kind=F32), shape_of(rows, weights[3].shape[1]), shape_of(rows, 2 * HEAD))
    return pl.pallas_call(
        functools.partial(next_chunk_kernel, chips=chips),
        out_shape=shapes,
        in_specs=[whole()] * (len(pieces) + 4),
        out_specs=(whole(),) * len(shapes),
        compiler_params=pltpu.CompilerParams(vmem_limit_bytes=14 << 20),
        name="next_chunk",
    )(*pieces, *weights)


def last_chunk(pieces, weights, parts):
    count, wide = pieces[0].shape
    rows = 2 * count
    shapes = chunk_shapes(rows, wide - LANES) + (
        shape_of(rows, weights[3].shape[1]),) + (shape_of(4 * rows, HEAD),) * 3 + (shape_of(rows, HEAD),) * 2
    return pl.pallas_call(
        last_chunk_kernel,
        out_shape=shapes,
        in_specs=[whole()] * (len(pieces) + 8),
        out_specs=(whole(),) * len(shapes),
        compiler_params=pltpu.CompilerParams(vmem_limit_bytes=14 << 20),
        name="last_chunk",
    )(*pieces, *weights, *parts)


def own_body(rows_ref, query_ref, out_ref, waits=()):
    for index in range(query_ref.shape[1] // BLOCK):
        if waits:
            waits[index]()
        at = slice(index * BLOCK, (index + 1) * BLOCK)
        out_ref[:, at] = jnp.dot(rows_ref[...], query_ref[:, at], preferred_element_type=F32)


def own_queries(rows, query):
    return pl.pallas_call(
        own_body,
        out_shape=shape_of(rows.shape[0], query.shape[1], kind=F32),
        in_specs=[whole(), whole()],
        out_specs=whole(),
        compiler_params=pltpu.CompilerParams(vmem_limit_bytes=10 << 20),
        name="own_queries",
    )(rows, query)


def slabs(refs, starts, count, at=slice(None)):
    return [ref[start:start + count, at].astype(F32) for ref, start in zip(refs, starts)]


def by_pack(parts, pack):
    count = parts[0].shape[0] // 2
    return jnp.concatenate([part[pack * count:(pack + 1) * count] for part in parts], axis=0)


def owner_of(row, pack, ids, piece_rows):
    index = jnp.zeros_like(row)
    for step in range(1, 8):
        index = index + (row >= step * piece_rows).astype(jnp.int32)
    chip, low = index >> 1, index & 1
    shard = (((chip >> 1) ^ ids[2]) * 2 + (low ^ pack)) * 2 + ((chip & 1) ^ ids[1])
    return shard, row - index * piece_rows


def mask_kernel(lengths_ref, near_ref, out_ref):
    ids = position()
    segment = ids[1]
    rows = out_ref.shape[1]
    piece_rows = rows // 8
    tail = near_ref[:, near_ref.shape[1] - LANES:].astype(F32)[:1].astype(jnp.int32)
    for pack in range(2):
        def place(row):
            shard, inner = owner_of(row, pack, ids, piece_rows)
            place_in_pack = shard * piece_rows + inner
            end = jnp.zeros((1, 1), jnp.int32)
            doc = jnp.zeros_like(place_in_pack)
            for index in range(lengths_ref.shape[1]):
                at = LENGTHS_AT + index
                end = end + jnp.where(segment == pack, lengths_ref[0, index], tail[:, at:at + 1])
                doc = doc + (place_in_pack >= end).astype(jnp.int32)
            return place_in_pack, doc

        row_position, row_doc = place(iota((rows, 1), 0))
        col_position, col_doc = place(iota((1, rows), 1))
        visible = jnp.logical_and(row_doc == col_doc, col_position <= row_position)
        out_ref[pack * rows:(pack + 1) * rows, :] = jnp.where(visible, 0.0, -1e30)


def masks(lengths, near, rows):
    return pl.pallas_call(
        mask_kernel,
        out_shape=shape_of(2 * rows, rows, kind=F32),
        in_specs=[whole(pltpu.SMEM), whole()],
        out_specs=whole(),
        compiler_params=pltpu.CompilerParams(vmem_limit_bytes=4 << 20),
        name="masks",
    )(lengths, near)


def attention_kernel(bias_ref, *refs, starts, recv_starts):
    chips = len(starts)
    owns, recvs, directs = (refs[index * chips:(index + 1) * chips] for index in range(3))
    refs = refs[3 * chips:]
    nears, fars, gain_ref, out_ref = refs[0:3], refs[3:5], refs[5], refs[6]
    ids = position()
    segment, tp = ids[1], ids[3]
    rows = bias_ref.shape[1]
    slab = rows // 2
    queries = rows
    piece_rows = rows // 8
    heads = owns[0].shape[1] // HEAD
    devices = out_ref.shape[0]
    wide = out_ref.shape[1] // 2
    scale = math.log2(math.e) / math.sqrt(HEAD)
    lane = iota((queries, wide), 1)

    def chosen_keys(refs):
        keep, first, second = (ref[...].astype(F32) for ref in refs)
        return (jnp.where(tp == 0, keep, jnp.where(tp == 2, second, first)),
                jnp.where(tp == 3, keep, jnp.where(tp == 1, second, first)))

    def pack_part(part, pack):
        count = part.shape[0] // 2
        return part[pack * count:(pack + 1) * count]

    far_first, far_second = (ref[...].astype(F32) for ref in fars)
    odd = (tp & 1) == 1
    far = (jnp.where(odd, far_first, far_second), jnp.where(odd, far_second, far_first))
    near = chosen_keys(nears)
    through = jnp.zeros((devices, wide), F32)
    direct = jnp.zeros((devices, wide), F32)
    for pack in range(2):
        keys, values = (
            jnp.concatenate([
                pack_part(near_part, pack)[:slab],
                pack_part(near_part, pack)[slab:slab + slab // 2] + pack_part(far_part, pack),
                pack_part(near_part, pack)[slab + slab // 2:]], axis=0).astype(BF16)
            for near_part, far_part in zip(near, far))
        values = jnp.concatenate([values, jnp.ones((rows, HEAD), BF16)], axis=1)
        total = jnp.zeros((queries, HEAD), F32)
        for head in range(heads):
            at = slice(head * HEAD, (head + 1) * HEAD)
            parts = [own + recv for own, recv in zip(
                slabs(owns, starts, slab, at), slabs(recvs, recv_starts, slab, at))]
            query = (by_pack(parts, pack) * scale).astype(BF16)
            logits = lax.dot_general(query, keys, (((1,), (1,)), ((), ())), preferred_element_type=F32)
            logits = logits + bias_ref[pack * rows:(pack + 1) * rows, :]
            expo = jnp.exp2(logits - jnp.max(logits, axis=1, keepdims=True)).astype(BF16)
            both = jnp.dot(expo, values, preferred_element_type=F32)
            offset = pl.multiple_of(segment * heads * HEAD + head * HEAD, HEAD)
            total = total + both[:, :HEAD] / both[:, HEAD:] * gain_ref[:, pl.ds(offset, HEAD)].astype(F32)

        _, inner = owner_of(iota((queries, 1), 0), pack, ids, piece_rows)
        shard_row, _ = owner_of(iota((1, queries), 1), pack, ids, piece_rows)
        chosen = ((iota((devices, 1), 0) >> 2) == shard_row).astype(F32)
        hit = lane == inner + pack * piece_rows

        def send(column):
            return jnp.dot(chosen, jnp.where(hit, column, 0.0), precision=HIGHEST, preferred_element_type=F32)

        through = through + send(jnp.sum(total, axis=1, keepdims=True))
        direct = direct + send(jnp.sum(by_pack(slabs(directs, starts, slab), pack), axis=1, keepdims=True))
    out_ref[:, :wide] = through
    out_ref[:, wide:] = direct


def attention(bias, owns, starts, recvs, recv_starts, directs, near, far, gain, devices):
    return pl.pallas_call(
        functools.partial(attention_kernel, starts=starts, recv_starts=recv_starts),
        out_shape=shape_of(devices, 2 * LANES, kind=F32),
        in_specs=[whole()] * (7 + 3 * len(owns)),
        out_specs=whole(),
        compiler_params=pltpu.CompilerParams(vmem_limit_bytes=14 << 20),
        name="attend",
    )(bias, *owns, *recvs, *directs, *near, *far, gain)


def finish_kernel(recv_ref, send_ref, out_ref):
    models, count = out_ref.shape
    devices, width = recv_ref.shape
    model_of = iota((models, devices), 1) // (devices // models)
    chosen = (model_of == iota((models, devices), 0)).astype(F32)
    sums = jnp.dot(chosen, recv_ref[...], precision=HIGHEST, preferred_element_type=F32)
    pick = (iota((count, count), 0) == send_ref[...]).astype(F32)
    half = width // 2
    both = sums[:, :count] + sums[:, half:half + count]
    out_ref[...] = lax.dot_general(
        both, pick, (((1,), (1,)), ((), ())), precision=HIGHEST, preferred_element_type=F32)


def finish(recv, send, models):
    count = send.shape[1]
    return pl.pallas_call(
        finish_kernel,
        out_shape=jax.ShapeDtypeStruct((models, count), F32),
        in_specs=[whole()] * 2,
        out_specs=whole(),
        compiler_params=pltpu.CompilerParams(vmem_limit_bytes=8 << 20),
        name="finish",
    )(recv, send)


def paired(rollout, send_rows, seq_lengths, attn_gain, w_query, w_keyval, head_weight, head_attn):
    n_branch = lax.axis_size("branch")
    send = send_rows.reshape(1, -1)

    core_pairs = [(i, i ^ 1) for i in range(n_branch)]
    y_pairs = [(i, i ^ 2) for i in range(n_branch)]
    x_pairs = [(0, 1), (1, 0)]

    def swap(piece):
        return lax.ppermute(piece, "branch", core_pairs)

    def across(part):
        return lax.ppermute(part, "segment", x_pairs)

    def in_hbm(array):
        return pltpu.with_memory_space_constraint(array, pltpu.HBM)

    packing = send
    rollout, send, attn_gain, head_weight, seq_lengths = map(
        in_hbm, (rollout, send, attn_gain, head_weight, seq_lengths))
    wq, wkv = in_hbm(w_query[0]), in_hbm(w_keyval[0])
    mine, theirs = prepare(seq_lengths, rollout, send)
    from_x = across(theirs)
    from_y = lax.ppermute(mine, "branch", y_pairs)
    from_d = lax.ppermute(from_x, "branch", y_pairs)

    slab = 2 * mine.shape[0]

    def with_swapped(*pieces):
        return [part for piece in pieces for part in (piece, swap(piece))]

    pieces = with_swapped(mine)
    (rows, direct_own, local_own, part), weights, own_weights = first_chunk(
        *pieces, attn_gain, head_weight, wkv, wq)
    received_own = across(part)
    query_own = own_queries(rows, own_weights)
    bias = masks(seq_lengths, from_x, 2 * slab)

    pieces = with_swapped(from_x) + with_swapped(from_y)
    rows, direct_xy, local_xy, part, keyval = next_chunk(pieces, weights)
    keyval_xy = across(keyval)
    received_xy = across(part)
    query_xy = own_queries(rows, own_weights)

    hand_first, hand_second = (1, 3, 0, 2), (0, 2, 1, 3)
    n_tp = len(hand_first)

    def hand(array, targets):
        return lax.ppermute(array, "tp", [(i, to) for i, to in enumerate(targets) if i != to])

    def hand_across(array, targets):
        return lax.ppermute(array, ("segment", "tp"), [
            (side * n_tp + i, (1 - side) * n_tp + to) for side in range(2) for i, to in enumerate(targets)])

    pieces = with_swapped(from_d)
    rows, direct_d, part, keep, first, second, far_first, far_second = last_chunk(
        pieces, weights, (local_own, local_xy, keyval_xy, received_own))
    received_d = across(part)
    first = hand(first, hand_first)
    second = hand(second, hand_second)
    far_first = hand_across(far_first, hand_first)
    far_second = hand_across(far_second, hand_second)
    query_d = own_queries(rows, own_weights)
    devices = n_branch * 2 * n_tp
    outgoing = attention(
        bias, [query_own, query_xy, query_xy, query_d], (0, 0, slab, 0),
        [received_xy, received_own, received_d, received_xy], (0, 0, 0, slab),
        [direct_own, direct_xy, direct_xy, direct_d],
        (keep, first, second), (far_first, far_second), head_attn, devices)
    incoming = lax.all_to_all(outgoing, ALL_AXES, split_axis=0, concat_axis=0, tiled=True)
    return finish(incoming, packing, n_branch)


def general(rollout, send_rows, seq_lengths, attn_gain, w_query, w_keyval, head_weight, head_attn):
    n_branch = lax.axis_size("branch")
    n_segment = lax.axis_size("segment")
    gen_rows = rollout.shape[0]
    piece_rows = gen_rows // n_segment
    row_width = rollout.shape[1]
    ordered = jnp.take(rollout, send_rows, axis=0).reshape(n_segment, piece_rows, row_width)
    copies = jnp.broadcast_to(ordered[None], (n_branch, n_segment, piece_rows, row_width))
    copies = copies.reshape(n_branch * n_segment, piece_rows, row_width)
    arrived = lax.all_to_all(copies, ("branch", "segment"), split_axis=0, concat_axis=0, tiled=True)
    packed = arrived.reshape(-1, row_width)
    pack_rows = packed.shape[0]
    rows_float = packed.astype(jnp.float32)
    mean_square = jnp.mean(rows_float * rows_float, axis=-1, keepdims=True)
    normed = (
        rows_float * lax.rsqrt(mean_square + epsilon) * attn_gain[0].astype(jnp.float32)
    ).astype(jnp.bfloat16)
    query_acc = jnp.dot(
        normed,
        lax.all_gather(w_query, "segment", axis=1, tiled=True)[0],
        preferred_element_type=jnp.float32,
    )
    keyval_acc = jnp.dot(
        normed,
        lax.all_gather(w_keyval, "segment", axis=1, tiled=True)[0],
        preferred_element_type=jnp.float32,
    )
    queries = query_acc.astype(jnp.bfloat16)
    keyval_part = keyval_acc.astype(jnp.bfloat16)
    keyval = lax.all_gather(keyval_part, "tp", axis=1, tiled=True)
    tp_index = lax.axis_index("tp")
    heads_here = queries.shape[1] // HEAD
    group_size = HEADS // KV_HEADS
    per_group = min(heads_here, group_size)
    group_span = heads_here // per_group
    kv_first = tp_index * heads_here // group_size
    key_rows = lax.dynamic_slice_in_dim(keyval, kv_first * HEAD, group_span * HEAD, 1)
    value_rows = lax.dynamic_slice_in_dim(
        keyval, KV_HEADS * HEAD + kv_first * HEAD, group_span * HEAD, 1
    )
    key_rows = key_rows.reshape(pack_rows, group_span, HEAD)
    value_rows = value_rows.reshape(pack_rows, group_span, HEAD)
    queries = queries.reshape(pack_rows, group_span, per_group, HEAD)
    positions = jnp.arange(pack_rows, dtype=jnp.int32)
    doc_ends = jnp.cumsum(seq_lengths[0])
    doc_ids = jnp.sum((positions[:, None] >= doc_ends[None, :]).astype(jnp.int32), axis=-1)
    visible = (doc_ids[:, None] == doc_ids[None, :]) & (positions[None, :] <= positions[:, None])
    logits = jnp.einsum(
        "qgpc,kgc->gpqk", queries, key_rows, preferred_element_type=jnp.float32
    ) / math.sqrt(HEAD)
    logits = jnp.where(visible[None, None], logits, -1e30)
    row_max = jnp.max(logits, axis=-1, keepdims=True)
    expo = jnp.exp(logits - row_max)
    probabilities = (expo / jnp.sum(expo, axis=-1, keepdims=True)).astype(jnp.bfloat16)
    attended = jnp.einsum(
        "gpqk,kgc->qgpc", probabilities, value_rows, preferred_element_type=jnp.float32
    )
    attended = attended.reshape(pack_rows, heads_here * HEAD)
    slice_width = head_weight.shape[1]
    own_columns = lax.dynamic_slice_in_dim(packed, tp_index * slice_width, slice_width, 1)
    direct = jnp.dot(own_columns, head_weight[0], preferred_element_type=jnp.float32)
    through = jnp.dot(attended, head_attn[0].astype(jnp.float32), precision=lax.Precision.HIGHEST)
    totals = lax.psum(direct + through, "tp")
    outgoing = totals.reshape(n_branch * n_segment, piece_rows)
    incoming = lax.all_to_all(
        outgoing, ("branch", "segment"), split_axis=0, concat_axis=0, tiled=True
    )
    incoming = incoming.reshape(n_branch, n_segment * piece_rows)
    scores = jnp.zeros((n_branch, gen_rows), jnp.float32).at[:, send_rows].set(incoming)
    return scores


def solution(mesh):
    sizes = tuple(mesh.shape[axis] for axis in ALL_AXES)
    pairwise = sizes == (4, 2, 4)
    local = paired if pairwise else general
    return jax.shard_map(
        local,
        mesh=mesh,
        in_specs=(
            P(("branch", "segment"), None),
            P(("branch", "segment")),
            P("segment", None),
            P("branch", None),
            P("branch", "segment", "tp"),
            P("branch", "segment", "tp"),
            P("branch", "tp"),
            P("branch", "tp"),
        ),
        out_specs=P(None, ("branch", "segment")),
        check_vma=False,
    )
```

```python
import functools
import math

import jax
import jax.numpy as jnp
from jax import lax
from jax.experimental import pallas as pl
from jax.experimental.pallas import tpu as pltpu
from jax.sharding import PartitionSpec as P


HEAD = 128
HEADS = 64
KV_HEADS = 8
LANES = 128
LENGTHS_AT = 8

epsilon = 1e-05

ALL_AXES = ("branch", "segment", "tp")
HIGHEST = lax.Precision.HIGHEST
F32 = jnp.float32
BF16 = jnp.bfloat16


def whole(memory_space=pltpu.VMEM):
    return pl.BlockSpec(memory_space=memory_space)


def position():
    branch = lax.axis_index("branch")
    return branch & 1, lax.axis_index("segment"), branch >> 1, lax.axis_index("tp")


def iota(shape, dimension):
    return lax.broadcasted_iota(jnp.int32, shape, dimension)


def prepare_kernel(lengths_hbm, rows_hbm, send_hbm, mine_ref, theirs_ref, rows_ref, send_ref, lengths_ref, sems):
    ids = position()
    count, width = rows_ref.shape
    half = width // 2
    parts = sems.shape[0] - 2
    step = width // parts
    core, segment = ids[0], ids[1]
    copies = [pltpu.make_async_copy(send_hbm, send_ref, sems.at[parts])]
    for part in range(parts):
        at = pl.ds(part * step, step)
        copies.append(pltpu.make_async_copy(rows_hbm.at[:, at], rows_ref.at[:, at], sems.at[part]))
    lengths_copy = pltpu.make_async_copy(lengths_hbm, lengths_ref, sems.at[parts + 1])
    for copy in copies + [lengths_copy]:
        copy.start()
    copies[0].wait()
    send = send_ref[...]
    rolled = jnp.concatenate([send[:, count // 2:], send[:, :count // 2]], axis=1)
    order = jnp.where(core == 1, rolled, send)
    pick = (iota((count, count), 0) == order).astype(BF16)

    def ordered(part):
        out = lax.dot_general(pick, part, (((0,), (0,)), ((), ())), preferred_element_type=F32)
        return out.astype(BF16)

    lanes = jnp.zeros((count, LANES), F32)
    for part in range(parts):
        copies[1 + part].wait()
        square = rows_ref[:, part * step:(part + 1) * step].astype(F32)
        square = square * square
        for lane in range(0, step, LANES):
            lanes = lanes + square[:, lane:lane + LANES]
    chunk = 1024
    for start in range(0, half, chunk):
        for out_ref, which in ((theirs_ref, 1 - segment), (mine_ref, segment)):
            at = pl.multiple_of(which * half + start, chunk)
            out_ref[:, start:start + chunk] = ordered(rows_ref[:, pl.ds(at, chunk)])
    scale = lax.rsqrt(jnp.sum(lanes, axis=1, keepdims=True) * (1.0 / width) + epsilon)
    high = scale.astype(BF16).astype(F32)
    middle = (scale - high).astype(BF16).astype(F32)
    low = scale - high - middle
    lane = iota((count, LANES), 1)
    tail = jnp.where(lane == 0, high, jnp.where(lane == 1, middle, jnp.where(lane == 2, low, 0.0)))
    tail = ordered(tail.astype(BF16))
    lengths_copy.wait()
    for index in range(lengths_ref.shape[1]):
        length = lengths_ref[0, index].astype(F32).astype(BF16)
        tail = jnp.where(lane == LENGTHS_AT + index, length, tail)
    theirs_ref[:, half:] = tail
    mine_ref[:, half:] = tail


def prepare(lengths, rows, send):
    count, width = rows.shape
    shape = jax.ShapeDtypeStruct((count, width // 2 + LANES), BF16)
    return pl.pallas_call(
        prepare_kernel,
        out_shape=(shape, shape),
        in_specs=[whole(pltpu.HBM)] * 3,
        out_specs=(whole(), whole()),
        scratch_shapes=[
            pltpu.VMEM((count, width), BF16),
            pltpu.VMEM((1, count), jnp.int32),
            pltpu.SMEM(lengths.shape, jnp.int32),
            pltpu.SemaphoreType.DMA((6,)),
        ],
        compiler_params=pltpu.CompilerParams(vmem_limit_bytes=12 << 20),
        name="prepare",
    )(lengths, rows, send)


BLOCK = 256
IN_FLIGHT = 4


def column_copies(source, first, target, sems):
    blocks = target.shape[1] // BLOCK
    return [
        pltpu.make_async_copy(
            source.at[:, pl.ds(pl.multiple_of(first + index * BLOCK, BLOCK), BLOCK)],
            target.at[:, pl.ds(index * BLOCK, BLOCK)], sems.at[index])
        for index in range(blocks)]


def split_slots(values):
    return values[:, :HEAD], values[:, HEAD:]


def chunk_body(pieces, gain_ref, head_ref, keyval_ref, query_ref, outs, waits, recv=None):
    rows_ref, direct_ref = outs[:2]
    count = pieces[0].shape[0]
    half = rows_ref.shape[1]
    core, segment, _, tp = position()
    columns = query_ref.shape[1]
    top = (iota((count, 1), 0) < count // 2).astype(jnp.int32)
    mask = (top ^ core) == 1

    def sorted_rows(values):
        near, far = values[0::2], values[1::2]
        return jnp.concatenate(
            [part for n, f in zip(near, far) for part in (jnp.where(mask, n, f), jnp.where(mask, f, n))], axis=0)

    first_lanes = iota((count, LANES), 1) < 3
    scale = sorted_rows([
        jnp.sum(jnp.where(first_lanes, ref[:, half:].astype(F32), 0.0), axis=1, keepdims=True) for ref in pieces])
    chunk = 512
    direct = jnp.zeros((direct_ref.shape[0], LANES), F32)
    for start in range(0, half, chunk):
        at = slice(start, start + chunk)
        rows = sorted_rows([ref[:, at].astype(F32) for ref in pieces])
        weight = head_ref[:, at].astype(F32)
        for lane in range(0, chunk, LANES):
            direct = direct + rows[:, lane:lane + LANES] * weight[:, lane:lane + LANES]
        rows_ref[:, at] = (rows * scale * gain_ref[:, at].astype(F32)).astype(BF16)
    direct_ref[...] = direct

    for wait in waits[:keyval_ref.shape[1] // BLOCK]:
        wait()
    keyval = jnp.dot(rows_ref[...], keyval_ref[...], preferred_element_type=F32)
    even = jnp.concatenate([keyval[:, :HEAD], keyval[:, 2 * HEAD:3 * HEAD]], axis=1)
    odd = jnp.concatenate([keyval[:, HEAD:2 * HEAD], keyval[:, 3 * HEAD:]], axis=1)
    own = jnp.where(segment == 0, even, odd)
    other = jnp.where(segment == 0, odd, even)
    if recv is None:
        own_ref, send_ref = outs[2:4]
        own_ref[...] = own
        if len(outs) > 4:
            outs[4][...] = other.astype(BF16)
        else:
            send_ref[:, columns:] = other.astype(BF16)
    else:
        send_ref, keep_ref, first_ref, second_ref, far_first_ref, far_second_ref = outs[2:]
        own_part_ref, pair_part_ref, recv_own_ref, recv_next_ref = recv
        slab = 2 * count
        mine, x_part, y_part = slabs((own_part_ref, pair_part_ref, pair_part_ref), (0, 0, slab), slab)
        at = slice(columns, columns + 2 * HEAD)
        sums = [mine + recv_own_ref[:slab, :].astype(F32), x_part + recv_next_ref[:, at].astype(F32), y_part,
                own + recv_own_ref[slab:, :].astype(F32)]
        low, high = split_slots(jnp.concatenate([by_pack(sums, pack) for pack in range(2)], axis=0))
        keep_ref[...] = jnp.where(tp == 3, high, low).astype(BF16)
        first_ref[...] = jnp.where(tp < 2, high, low).astype(BF16)
        second_ref[...] = jnp.where(tp == 2, high, low).astype(BF16)
        low, high = split_slots(other)
        far_first_ref[...] = jnp.where(tp < 2, high, low).astype(BF16)
        far_second_ref[...] = jnp.where(tp < 2, low, high).astype(BF16)
    waits = waits[keyval_ref.shape[1] // BLOCK:]
    for index in range(columns // BLOCK):
        if waits:
            waits[index]()
        at = slice(index * BLOCK, (index + 1) * BLOCK)
        send_ref[:, at] = jnp.dot(rows_ref[...], query_ref[:, at], preferred_element_type=F32).astype(BF16)


def first_chunk_kernel(near_ref, far_ref, gain_hbm, head_hbm, keyval_hbm, query_hbm, *refs):
    outs, (gain_ref, head_ref, keyval_ref, query_ref) = refs[:4], refs[4:8]
    own_query_ref, part_ref, small_sems, sems, own_sems = refs[8:]
    rows_ref = outs[0]
    half = rows_ref.shape[1]
    _, segment, _, tp = position()
    small = [
        pltpu.make_async_copy(
            gain_hbm.at[:, pl.ds(pl.multiple_of(segment * half, half), half)], gain_ref, small_sems.at[0]),
        pltpu.make_async_copy(head_hbm, part_ref, small_sems.at[1]),
    ]
    blocks = keyval_ref.shape[1] // BLOCK
    large = column_copies(keyval_hbm, 0, keyval_ref, sems)
    large += column_copies(query_hbm, (1 - segment) * query_ref.shape[1], query_ref, sems.at[pl.ds(blocks, query_ref.shape[1] // BLOCK)])
    owns = column_copies(query_hbm, segment * query_ref.shape[1], own_query_ref, own_sems)
    copies = large + owns
    for copy in small + copies[:IN_FLIGHT]:
        copy.start()

    def waiter(index):
        def wait():
            copies[index].wait()
            if index + IN_FLIGHT < len(copies):
                copies[index + IN_FLIGHT].start()

        return wait

    waits = [waiter(index) for index in range(len(copies))]
    for copy in small:
        copy.wait()
    width = part_ref.shape[1]
    head_ref[...] = jnp.zeros_like(head_ref)

    @pl.when((tp * width) // half == segment)
    def _():
        head_ref[:, pl.ds(pl.multiple_of((tp * width) % half, width), width)] = part_ref[...]

    chunk_body((near_ref, far_ref), gain_ref, head_ref, keyval_ref, query_ref, outs,
               waits[:len(large)])
    for wait in waits[len(large):]:
        wait()


def next_chunk_kernel(*refs, chips):
    pieces, refs = refs[:2 * chips], refs[2 * chips:]
    chunk_body(pieces, *refs[:4], refs[4:], [])


def last_chunk_kernel(*refs):
    chunk_body(refs[:2], *refs[2:6], refs[10:], [], refs[6:10])


def shape_of(*shape, kind=BF16):
    return jax.ShapeDtypeStruct(shape, kind)


def chunk_shapes(rows, half):
    return (shape_of(rows, half), shape_of(rows, LANES, kind=F32))


def first_chunk(near, far, gain, head, keyval, query):
    count, wide = near.shape
    half = wide - LANES
    columns = query.shape[1] // 2
    rows = 2 * count
    shapes = chunk_shapes(rows, half) + (
        shape_of(rows, 2 * HEAD, kind=F32), shape_of(rows, columns + 2 * HEAD),
        shape_of(1, half), shape_of(1, half), shape_of(*keyval.shape), shape_of(half, columns),
        shape_of(half, columns))
    out = pl.pallas_call(
        first_chunk_kernel,
        out_shape=shapes,
        in_specs=[whole(), whole()] + [whole(pltpu.HBM)] * 4,
        out_specs=(whole(),) * len(shapes),
        scratch_shapes=[
            pltpu.VMEM(head.shape, BF16),
            pltpu.SemaphoreType.DMA((2,)),
            pltpu.SemaphoreType.DMA(((columns + keyval.shape[1]) // BLOCK,)),
            pltpu.SemaphoreType.DMA((columns // BLOCK,)),
        ],
        compiler_params=pltpu.CompilerParams(vmem_limit_bytes=14 << 20),
        name="first_chunk",
    )(near, far, gain, head, keyval, query)
    return out[:4], out[4:8], out[8]


def next_chunk(pieces, weights):
    count, wide = pieces[0].shape
    chips = len(pieces) // 2
    rows = 2 * chips * count
    shapes = chunk_shapes(rows, wide - LANES) + (
        shape_of(rows, 2 * HEAD, kind=F32), shape_of(rows, weights[3].shape[1]), shape_of(rows, 2 * HEAD))
    return pl.pallas_call(
        functools.partial(next_chunk_kernel, chips=chips),
        out_shape=shapes,
        in_specs=[whole()] * (len(pieces) + 4),
        out_specs=(whole(),) * len(shapes),
        compiler_params=pltpu.CompilerParams(vmem_limit_bytes=14 << 20),
        name="next_chunk",
    )(*pieces, *weights)


def last_chunk(pieces, weights, parts):
    count, wide = pieces[0].shape
    rows = 2 * count
    shapes = chunk_shapes(rows, wide - LANES) + (
        shape_of(rows, weights[3].shape[1]),) + (shape_of(4 * rows, HEAD),) * 3 + (shape_of(rows, HEAD),) * 2
    return pl.pallas_call(
        last_chunk_kernel,
        out_shape=shapes,
        in_specs=[whole()] * (len(pieces) + 8),
        out_specs=(whole(),) * len(shapes),
        compiler_params=pltpu.CompilerParams(vmem_limit_bytes=14 << 20),
        name="last_chunk",
    )(*pieces, *weights, *parts)


def own_body(rows_ref, query_ref, out_ref, waits=()):
    for index in range(query_ref.shape[1] // BLOCK):
        if waits:
            waits[index]()
        at = slice(index * BLOCK, (index + 1) * BLOCK)
        out_ref[:, at] = jnp.dot(rows_ref[...], query_ref[:, at], preferred_element_type=F32)


def own_queries(rows, query):
    return pl.pallas_call(
        own_body,
        out_shape=shape_of(rows.shape[0], query.shape[1], kind=F32),
        in_specs=[whole(), whole()],
        out_specs=whole(),
        compiler_params=pltpu.CompilerParams(vmem_limit_bytes=10 << 20),
        name="own_queries",
    )(rows, query)


def slabs(refs, starts, count, at=slice(None)):
    return [ref[start:start + count, at].astype(F32) for ref, start in zip(refs, starts)]


def by_pack(parts, pack):
    count = parts[0].shape[0] // 2
    return jnp.concatenate([part[pack * count:(pack + 1) * count] for part in parts], axis=0)


def owner_of(row, pack, ids, piece_rows):
    index = jnp.zeros_like(row)
    for step in range(1, 8):
        index = index + (row >= step * piece_rows).astype(jnp.int32)
    chip, low = index >> 1, index & 1
    shard = (((chip >> 1) ^ ids[2]) * 2 + (low ^ pack)) * 2 + ((chip & 1) ^ ids[1])
    return shard, row - index * piece_rows


def padded(rows):
    return -(-rows // LANES) * LANES


def mask_kernel(lengths_ref, near_ref, out_ref):
    ids = position()
    segment = ids[1]
    rows = out_ref.shape[0] // 2
    piece_rows = rows // 8
    tail = near_ref[:, near_ref.shape[1] - LANES:].astype(F32)[:1].astype(jnp.int32)
    for pack in range(2):
        def place(row):
            shard, inner = owner_of(row, pack, ids, piece_rows)
            place_in_pack = shard * piece_rows + inner
            end = jnp.zeros((1, 1), jnp.int32)
            doc = jnp.zeros_like(place_in_pack)
            for index in range(lengths_ref.shape[1]):
                at = LENGTHS_AT + index
                end = end + jnp.where(segment == pack, lengths_ref[0, index], tail[:, at:at + 1])
                doc = doc + (place_in_pack >= end).astype(jnp.int32)
            return place_in_pack, doc

        row_position, row_doc = place(iota((rows, 1), 0))
        column = iota((1, out_ref.shape[1]), 1)
        col_position, col_doc = place(column)
        visible = jnp.logical_and(row_doc == col_doc, col_position <= row_position)
        visible = jnp.logical_and(visible, column < rows)
        out_ref[pack * rows:(pack + 1) * rows, :] = jnp.where(visible, 0.0, -1e30)


def masks(lengths, near, rows):
    return pl.pallas_call(
        mask_kernel,
        out_shape=shape_of(2 * rows, padded(rows), kind=F32),
        in_specs=[whole(pltpu.SMEM), whole()],
        out_specs=whole(),
        compiler_params=pltpu.CompilerParams(vmem_limit_bytes=4 << 20),
        name="masks",
    )(lengths, near)


def attention_kernel(bias_ref, *refs, starts, recv_starts):
    chips = len(starts)
    owns, recvs, directs = (refs[index * chips:(index + 1) * chips] for index in range(3))
    refs = refs[3 * chips:]
    nears, fars, gain_ref, out_ref = refs[0:3], refs[3:5], refs[5], refs[6]
    expo_ref, weight_ref = refs[7:]
    ids = position()
    segment, tp = ids[1], ids[3]
    rows = bias_ref.shape[0] // 2
    keys_wide = bias_ref.shape[1]
    slab = rows // 2
    piece_rows = rows // 8
    heads = owns[0].shape[1] // HEAD
    devices = out_ref.shape[0]
    wide = out_ref.shape[1] // 2
    scale = math.log2(math.e) / math.sqrt(HEAD)
    lane = iota((rows, wide), 1)
    used = lane < 2 * heads
    gains = [gain_ref[:, pl.ds(pl.multiple_of((segment * heads + head) * HEAD, HEAD), HEAD)].astype(F32)
             for head in range(heads)]
    gains = jnp.concatenate(gains * 2 + [jnp.zeros((LANES - 2 * heads, HEAD), F32)], axis=0).astype(BF16)

    def chosen_keys(refs):
        keep, first, second = (ref[...].astype(F32) for ref in refs)
        return (jnp.where(tp == 0, keep, jnp.where(tp == 2, second, first)),
                jnp.where(tp == 3, keep, jnp.where(tp == 1, second, first)))

    def pack_part(part, pack):
        count = part.shape[0] // 2
        return part[pack * count:(pack + 1) * count]

    far_first, far_second = (ref[...].astype(F32) for ref in fars)
    odd = (tp & 1) == 1
    far = (jnp.where(odd, far_first, far_second), jnp.where(odd, far_second, far_first))
    near = chosen_keys(nears)
    through = jnp.zeros((devices, wide), F32)
    direct = jnp.zeros((devices, wide), F32)
    for pack in range(2):
        keys, values = (
            jnp.concatenate([
                pack_part(near_part, pack)[:slab],
                pack_part(near_part, pack)[slab:slab + slab // 2] + pack_part(far_part, pack),
                pack_part(near_part, pack)[slab + slab // 2:]], axis=0)
            for near_part, far_part in zip(near, far))
        keys = jnp.concatenate([keys, jnp.zeros((keys_wide - rows, HEAD), F32)], axis=0).astype(BF16)
        high = values.astype(BF16)
        rest = (values - high.astype(F32)).astype(BF16)
        product = (((1,), (1,)), ((), ()))
        score = (lax.dot_general(high, gains, product, preferred_element_type=F32)
                 + lax.dot_general(rest, gains, product, preferred_element_type=F32))
        high = score.astype(BF16).astype(F32)
        score = jnp.where(lane < heads, high, score - high)
        for head in range(heads):
            here = jnp.logical_and(used, (lane & (heads - 1)) == head)
            block = jnp.concatenate([jnp.where(here, score, 0.0), jnp.where(here, 1.0, 0.0)], axis=1)
            block = jnp.concatenate([block, jnp.zeros((keys_wide - rows, 2 * LANES), F32)], axis=0)
            weight_ref[head * keys_wide:(head + 1) * keys_wide, :] = block.astype(BF16)

            at = slice(head * HEAD, (head + 1) * HEAD)
            parts = [own + recv for own, recv in zip(
                slabs(owns, starts, slab, at), slabs(recvs, recv_starts, slab, at))]
            query = (by_pack(parts, pack) * scale).astype(BF16)
            logits = lax.dot_general(query, keys, product, preferred_element_type=F32)
            logits = logits + bias_ref[pack * rows:(pack + 1) * rows, :]
            expo = jnp.exp2(logits - jnp.max(logits, axis=1, keepdims=True)).astype(BF16)
            expo_ref[:, head * keys_wide:(head + 1) * keys_wide] = expo
        both = jnp.dot(expo_ref[...], weight_ref[...], preferred_element_type=F32)
        total = both[:, :LANES] / jnp.where(used, both[:, LANES:], 1.0)

        _, inner = owner_of(iota((rows, 1), 0), pack, ids, piece_rows)
        shard_row, _ = owner_of(iota((1, rows), 1), pack, ids, piece_rows)
        chosen = ((iota((devices, 1), 0) >> 2) == shard_row).astype(F32)
        hit = lane == inner + pack * piece_rows

        def send(column):
            return jnp.dot(chosen, jnp.where(hit, column, 0.0), precision=HIGHEST, preferred_element_type=F32)

        through = through + send(jnp.sum(total, axis=1, keepdims=True))
        direct = direct + send(jnp.sum(by_pack(slabs(directs, starts, slab), pack), axis=1, keepdims=True))
    out_ref[:, :wide] = through
    out_ref[:, wide:] = direct


def attention(bias, owns, starts, recvs, recv_starts, directs, near, far, gain, devices):
    heads = owns[0].shape[1] // HEAD
    return pl.pallas_call(
        functools.partial(attention_kernel, starts=starts, recv_starts=recv_starts),
        out_shape=shape_of(devices, 2 * LANES, kind=F32),
        in_specs=[whole()] * (7 + 3 * len(owns)),
        out_specs=whole(),
        scratch_shapes=[
            pltpu.VMEM((bias.shape[0] // 2, heads * bias.shape[1]), BF16),
            pltpu.VMEM((heads * bias.shape[1], 2 * LANES), BF16),
        ],
        compiler_params=pltpu.CompilerParams(vmem_limit_bytes=14 << 20),
        name="attend",
    )(bias, *owns, *recvs, *directs, *near, *far, gain)


def finish_kernel(recv_ref, send_ref, out_ref):
    models, count = out_ref.shape
    devices, width = recv_ref.shape
    model_of = iota((models, devices), 1) // (devices // models)
    chosen = (model_of == iota((models, devices), 0)).astype(F32)
    sums = jnp.dot(chosen, recv_ref[...], precision=HIGHEST, preferred_element_type=F32)
    pick = (iota((count, count), 0) == send_ref[...]).astype(F32)
    half = width // 2
    both = sums[:, :count] + sums[:, half:half + count]
    out_ref[...] = lax.dot_general(
        both, pick, (((1,), (1,)), ((), ())), precision=HIGHEST, preferred_element_type=F32)


def finish(recv, send, models):
    count = send.shape[1]
    return pl.pallas_call(
        finish_kernel,
        out_shape=jax.ShapeDtypeStruct((models, count), F32),
        in_specs=[whole()] * 2,
        out_specs=whole(),
        compiler_params=pltpu.CompilerParams(vmem_limit_bytes=8 << 20),
        name="finish",
    )(recv, send)


def paired(rollout, send_rows, seq_lengths, attn_gain, w_query, w_keyval, head_weight, head_attn):
    n_branch = lax.axis_size("branch")
    send = send_rows.reshape(1, -1)

    core_pairs = [(i, i ^ 1) for i in range(n_branch)]
    y_pairs = [(i, i ^ 2) for i in range(n_branch)]
    x_pairs = [(0, 1), (1, 0)]

    def swap(piece):
        return lax.ppermute(piece, "branch", core_pairs)

    def across(part):
        return lax.ppermute(part, "segment", x_pairs)

    def in_hbm(array):
        return pltpu.with_memory_space_constraint(array, pltpu.HBM)

    packing = send
    rollout, send, attn_gain, head_weight, seq_lengths = map(
        in_hbm, (rollout, send, attn_gain, head_weight, seq_lengths))
    wq, wkv = in_hbm(w_query[0]), in_hbm(w_keyval[0])
    mine, theirs = prepare(seq_lengths, rollout, send)
    from_x = across(theirs)
    from_y = lax.ppermute(mine, "branch", y_pairs)
    from_d = lax.ppermute(from_x, "branch", y_pairs)

    slab = 2 * mine.shape[0]

    def with_swapped(*pieces):
        return [part for piece in pieces for part in (piece, swap(piece))]

    pieces = with_swapped(mine)
    (rows, direct_own, local_own, part), weights, own_weights = first_chunk(
        *pieces, attn_gain, head_weight, wkv, wq)
    received_own = across(part)
    query_own = own_queries(rows, own_weights)
    bias = masks(seq_lengths, from_x, 2 * slab)

    pieces = with_swapped(from_x) + with_swapped(from_y)
    rows, direct_xy, local_xy, part, keyval = next_chunk(pieces, weights)
    keyval_xy = across(keyval)
    received_xy = across(part)
    query_xy = own_queries(rows, own_weights)

    hand_first, hand_second = (1, 3, 0, 2), (0, 2, 1, 3)
    n_tp = len(hand_first)

    def hand(array, targets):
        return lax.ppermute(array, "tp", [(i, to) for i, to in enumerate(targets) if i != to])

    def hand_across(array, targets):
        return lax.ppermute(array, ("segment", "tp"), [
            (side * n_tp + i, (1 - side) * n_tp + to) for side in range(2) for i, to in enumerate(targets)])

    pieces = with_swapped(from_d)
    rows, direct_d, part, keep, first, second, far_first, far_second = last_chunk(
        pieces, weights, (local_own, local_xy, keyval_xy, received_own))
    received_d = across(part)
    first = hand(first, hand_first)
    second = hand(second, hand_second)
    far_first = hand_across(far_first, hand_first)
    far_second = hand_across(far_second, hand_second)
    query_d = own_queries(rows, own_weights)
    devices = n_branch * 2 * n_tp
    outgoing = attention(
        bias, [query_own, query_xy, query_xy, query_d], (0, 0, slab, 0),
        [received_xy, received_own, received_d, received_xy], (0, 0, 0, slab),
        [direct_own, direct_xy, direct_xy, direct_d],
        (keep, first, second), (far_first, far_second), head_attn, devices)
    incoming = lax.all_to_all(outgoing, ALL_AXES, split_axis=0, concat_axis=0, tiled=True)
    return finish(incoming, packing, n_branch)


def general(rollout, send_rows, seq_lengths, attn_gain, w_query, w_keyval, head_weight, head_attn):
    n_branch = lax.axis_size("branch")
    n_segment = lax.axis_size("segment")
    gen_rows = rollout.shape[0]
    piece_rows = gen_rows // n_segment
    row_width = rollout.shape[1]
    ordered = jnp.take(rollout, send_rows, axis=0).reshape(n_segment, piece_rows, row_width)
    copies = jnp.broadcast_to(ordered[None], (n_branch, n_segment, piece_rows, row_width))
    copies = copies.reshape(n_branch * n_segment, piece_rows, row_width)
    arrived = lax.all_to_all(copies, ("branch", "segment"), split_axis=0, concat_axis=0, tiled=True)
    packed = arrived.reshape(-1, row_width)
    pack_rows = packed.shape[0]
    rows_float = packed.astype(jnp.float32)
    mean_square = jnp.mean(rows_float * rows_float, axis=-1, keepdims=True)
    normed = (
        rows_float * lax.rsqrt(mean_square + epsilon) * attn_gain[0].astype(jnp.float32)
    ).astype(jnp.bfloat16)
    query_acc = jnp.dot(
        normed,
        lax.all_gather(w_query, "segment", axis=1, tiled=True)[0],
        preferred_element_type=jnp.float32,
    )
    keyval_acc = jnp.dot(
        normed,
        lax.all_gather(w_keyval, "segment", axis=1, tiled=True)[0],
        preferred_element_type=jnp.float32,
    )
    queries = query_acc.astype(jnp.bfloat16)
    keyval_part = keyval_acc.astype(jnp.bfloat16)
    keyval = lax.all_gather(keyval_part, "tp", axis=1, tiled=True)
    tp_index = lax.axis_index("tp")
    heads_here = queries.shape[1] // HEAD
    group_size = HEADS // KV_HEADS
    per_group = min(heads_here, group_size)
    group_span = heads_here // per_group
    kv_first = tp_index * heads_here // group_size
    key_rows = lax.dynamic_slice_in_dim(keyval, kv_first * HEAD, group_span * HEAD, 1)
    value_rows = lax.dynamic_slice_in_dim(
        keyval, KV_HEADS * HEAD + kv_first * HEAD, group_span * HEAD, 1
    )
    key_rows = key_rows.reshape(pack_rows, group_span, HEAD)
    value_rows = value_rows.reshape(pack_rows, group_span, HEAD)
    queries = queries.reshape(pack_rows, group_span, per_group, HEAD)
    positions = jnp.arange(pack_rows, dtype=jnp.int32)
    doc_ends = jnp.cumsum(seq_lengths[0])
    doc_ids = jnp.sum((positions[:, None] >= doc_ends[None, :]).astype(jnp.int32), axis=-1)
    visible = (doc_ids[:, None] == doc_ids[None, :]) & (positions[None, :] <= positions[:, None])
    logits = jnp.einsum(
        "qgpc,kgc->gpqk", queries, key_rows, preferred_element_type=jnp.float32
    ) / math.sqrt(HEAD)
    logits = jnp.where(visible[None, None], logits, -1e30)
    row_max = jnp.max(logits, axis=-1, keepdims=True)
    expo = jnp.exp(logits - row_max)
    probabilities = (expo / jnp.sum(expo, axis=-1, keepdims=True)).astype(jnp.bfloat16)
    attended = jnp.einsum(
        "gpqk,kgc->qgpc", probabilities, value_rows, preferred_element_type=jnp.float32
    )
    attended = attended.reshape(pack_rows, heads_here * HEAD)
    slice_width = head_weight.shape[1]
    own_columns = lax.dynamic_slice_in_dim(packed, tp_index * slice_width, slice_width, 1)
    direct = jnp.dot(own_columns, head_weight[0], preferred_element_type=jnp.float32)
    through = jnp.dot(attended, head_attn[0].astype(jnp.float32), precision=lax.Precision.HIGHEST)
    totals = lax.psum(direct + through, "tp")
    outgoing = totals.reshape(n_branch * n_segment, piece_rows)
    incoming = lax.all_to_all(
        outgoing, ("branch", "segment"), split_axis=0, concat_axis=0, tiled=True
    )
    incoming = incoming.reshape(n_branch, n_segment * piece_rows)
    scores = jnp.zeros((n_branch, gen_rows), jnp.float32).at[:, send_rows].set(incoming)
    return scores


def solution(mesh):
    sizes = tuple(mesh.shape[axis] for axis in ALL_AXES)
    pairwise = sizes == (4, 2, 4)
    local = paired if pairwise else general
    return jax.shard_map(
        local,
        mesh=mesh,
        in_specs=(
            P(("branch", "segment"), None),
            P(("branch", "segment")),
            P("segment", None),
            P("branch", None),
            P("branch", "segment", "tp"),
            P("branch", "segment", "tp"),
            P("branch", "tp"),
            P("branch", "tp"),
        ),
        out_specs=P(None, ("branch", "segment")),
        check_vma=False,
    )
```

```python
import functools
import math

import jax
import jax.numpy as jnp
from jax import lax
from jax.experimental import pallas as pl
from jax.experimental.pallas import tpu as pltpu
from jax.sharding import PartitionSpec as P


HEAD = 128
HEADS = 64
KV_HEADS = 8
LANES = 128
LENGTHS_AT = 8

epsilon = 1e-05

ALL_AXES = ("branch", "segment", "tp")
HIGHEST = lax.Precision.HIGHEST
F32 = jnp.float32
BF16 = jnp.bfloat16


def whole(memory_space=pltpu.VMEM):
    return pl.BlockSpec(memory_space=memory_space)


def position():
    branch = lax.axis_index("branch")
    return branch & 1, lax.axis_index("segment"), branch >> 1, lax.axis_index("tp")


def iota(shape, dimension):
    return lax.broadcasted_iota(jnp.int32, shape, dimension)


def prepare_kernel(lengths_hbm, rows_hbm, send_hbm, mine_ref, theirs_ref, rows_ref, send_ref, lengths_ref, sems):
    ids = position()
    count, width = rows_ref.shape
    half = width // 2
    parts = sems.shape[0] - 2
    step = width // parts
    core, segment = ids[0], ids[1]
    copies = [pltpu.make_async_copy(send_hbm, send_ref, sems.at[parts])]
    for part in range(parts):
        first = (1 - segment) * half if part < parts // 2 else segment * half
        source = pl.ds(pl.multiple_of(first + part % (parts // 2) * step, step), step)
        copies.append(pltpu.make_async_copy(
            rows_hbm.at[:, source], rows_ref.at[:, pl.ds(part * step, step)], sems.at[part]))
    lengths_copy = pltpu.make_async_copy(lengths_hbm, lengths_ref, sems.at[parts + 1])
    for copy in copies + [lengths_copy]:
        copy.start()
    copies[0].wait()
    send = send_ref[...]
    rolled = jnp.concatenate([send[:, count // 2:], send[:, :count // 2]], axis=1)
    order = jnp.where(core == 1, rolled, send)
    pick = (iota((count, count), 0) == order).astype(BF16)

    def ordered(part):
        out = lax.dot_general(pick, part, (((0,), (0,)), ((), ())), preferred_element_type=F32)
        return out.astype(BF16)

    lanes = jnp.zeros((count, LANES), F32)
    chunk = 512
    for part in range(parts):
        copies[1 + part].wait()
        out_ref = theirs_ref if part < parts // 2 else mine_ref
        for start in range(part * step, (part + 1) * step, chunk):
            rows = rows_ref[:, start:start + chunk]
            out_ref[:, start % half:start % half + chunk] = ordered(rows)
            for lane in range(0, chunk, LANES):
                square = rows[:, lane:lane + LANES].astype(F32)
                lanes = lanes + square * square
    scale = lax.rsqrt(jnp.sum(lanes, axis=1, keepdims=True) * (1.0 / width) + epsilon)
    high = scale.astype(BF16).astype(F32)
    middle = (scale - high).astype(BF16).astype(F32)
    low = scale - high - middle
    lane = iota((count, LANES), 1)
    tail = jnp.where(lane == 0, high, jnp.where(lane == 1, middle, jnp.where(lane == 2, low, 0.0)))
    tail = ordered(tail.astype(BF16))
    lengths_copy.wait()
    for index in range(lengths_ref.shape[1]):
        length = lengths_ref[0, index].astype(F32).astype(BF16)
        tail = jnp.where(lane == LENGTHS_AT + index, length, tail)
    theirs_ref[:, half:] = tail
    mine_ref[:, half:] = tail


def prepare(lengths, rows, send):
    count, width = rows.shape
    shape = jax.ShapeDtypeStruct((count, width // 2 + LANES), BF16)
    return pl.pallas_call(
        prepare_kernel,
        out_shape=(shape, shape),
        in_specs=[whole(pltpu.HBM)] * 3,
        out_specs=(whole(), whole()),
        scratch_shapes=[
            pltpu.VMEM((count, width), BF16),
            pltpu.VMEM((1, count), jnp.int32),
            pltpu.SMEM(lengths.shape, jnp.int32),
            pltpu.SemaphoreType.DMA((6,)),
        ],
        compiler_params=pltpu.CompilerParams(vmem_limit_bytes=12 << 20),
        name="prepare",
    )(lengths, rows, send)


BLOCK = 256
IN_FLIGHT = 4


def column_copies(source, first, target, sems):
    blocks = target.shape[1] // BLOCK
    return [
        pltpu.make_async_copy(
            source.at[:, pl.ds(pl.multiple_of(first + index * BLOCK, BLOCK), BLOCK)],
            target.at[:, pl.ds(index * BLOCK, BLOCK)], sems.at[index])
        for index in range(blocks)]


def split_slots(values):
    return values[:, :HEAD], values[:, HEAD:]


def chunk_body(pieces, gain_ref, head_ref, keyval_ref, query_ref, outs, waits, recv=None):
    rows_ref, direct_ref = outs[:2]
    count = pieces[0].shape[0]
    half = rows_ref.shape[1]
    core, segment, _, tp = position()
    columns = query_ref.shape[1]
    top = (iota((count, 1), 0) < count // 2).astype(jnp.int32)
    mask = (top ^ core) == 1

    def sorted_rows(values):
        near, far = values[0::2], values[1::2]
        return jnp.concatenate(
            [part for n, f in zip(near, far) for part in (jnp.where(mask, n, f), jnp.where(mask, f, n))], axis=0)

    first_lanes = iota((count, LANES), 1) < 3
    scale = sorted_rows([
        jnp.sum(jnp.where(first_lanes, ref[:, half:].astype(F32), 0.0), axis=1, keepdims=True) for ref in pieces])
    chunk = 512
    direct = jnp.zeros((direct_ref.shape[0], LANES), F32)
    for start in range(0, half, chunk):
        at = slice(start, start + chunk)
        rows = sorted_rows([ref[:, at].astype(F32) for ref in pieces])
        weight = head_ref[:, at].astype(F32)
        for lane in range(0, chunk, LANES):
            direct = direct + rows[:, lane:lane + LANES] * weight[:, lane:lane + LANES]
        rows_ref[:, at] = (rows * scale * gain_ref[:, at].astype(F32)).astype(BF16)
    direct_ref[...] = direct

    for wait in waits[:keyval_ref.shape[1] // BLOCK]:
        wait()
    keyval = jnp.dot(rows_ref[...], keyval_ref[...], preferred_element_type=F32)
    even = jnp.concatenate([keyval[:, :HEAD], keyval[:, 2 * HEAD:3 * HEAD]], axis=1)
    odd = jnp.concatenate([keyval[:, HEAD:2 * HEAD], keyval[:, 3 * HEAD:]], axis=1)
    own = jnp.where(segment == 0, even, odd)
    other = jnp.where(segment == 0, odd, even)
    if recv is None:
        own_ref, send_ref = outs[2:4]
        own_ref[...] = own
        if len(outs) > 4:
            outs[4][...] = other.astype(BF16)
        else:
            send_ref[:, columns:] = other.astype(BF16)
    else:
        send_ref, keep_ref, first_ref, second_ref, far_first_ref, far_second_ref = outs[2:]
        own_part_ref, pair_part_ref, recv_own_ref, recv_next_ref = recv
        slab = 2 * count
        mine, x_part, y_part = slabs((own_part_ref, pair_part_ref, pair_part_ref), (0, 0, slab), slab)
        at = slice(columns, columns + 2 * HEAD)
        sums = [mine + recv_own_ref[:slab, :].astype(F32), x_part + recv_next_ref[:, at].astype(F32), y_part,
                own + recv_own_ref[slab:, :].astype(F32)]
        low, high = split_slots(jnp.concatenate([by_pack(sums, pack) for pack in range(2)], axis=0))
        keep_ref[...] = jnp.where(tp == 3, high, low).astype(BF16)
        first_ref[...] = jnp.where(tp < 2, high, low).astype(BF16)
        second_ref[...] = jnp.where(tp == 2, high, low).astype(BF16)
        low, high = split_slots(other)
        far_first_ref[...] = jnp.where(tp < 2, high, low).astype(BF16)
        far_second_ref[...] = jnp.where(tp < 2, low, high).astype(BF16)
    waits = waits[keyval_ref.shape[1] // BLOCK:]
    for index in range(columns // BLOCK):
        if waits:
            waits[index]()
        at = slice(index * BLOCK, (index + 1) * BLOCK)
        send_ref[:, at] = jnp.dot(rows_ref[...], query_ref[:, at], preferred_element_type=F32).astype(BF16)


def first_chunk_kernel(near_ref, far_ref, gain_hbm, head_hbm, keyval_hbm, query_hbm, *refs):
    outs, (gain_ref, head_ref, keyval_ref, query_ref) = refs[:4], refs[4:8]
    own_query_ref, part_ref, small_sems, sems, own_sems = refs[8:]
    rows_ref = outs[0]
    half = rows_ref.shape[1]
    _, segment, _, tp = position()
    small = [
        pltpu.make_async_copy(
            gain_hbm.at[:, pl.ds(pl.multiple_of(segment * half, half), half)], gain_ref, small_sems.at[0]),
        pltpu.make_async_copy(head_hbm, part_ref, small_sems.at[1]),
    ]
    blocks = keyval_ref.shape[1] // BLOCK
    large = column_copies(keyval_hbm, 0, keyval_ref, sems)
    large += column_copies(query_hbm, (1 - segment) * query_ref.shape[1], query_ref, sems.at[pl.ds(blocks, query_ref.shape[1] // BLOCK)])
    owns = column_copies(query_hbm, segment * query_ref.shape[1], own_query_ref, own_sems)
    copies = large + owns
    for copy in small + copies[:IN_FLIGHT]:
        copy.start()

    def waiter(index):
        def wait():
            copies[index].wait()
            if index + IN_FLIGHT < len(copies):
                copies[index + IN_FLIGHT].start()

        return wait

    waits = [waiter(index) for index in range(len(copies))]
    for copy in small:
        copy.wait()
    width = part_ref.shape[1]
    head_ref[...] = jnp.zeros_like(head_ref)

    @pl.when((tp * width) // half == segment)
    def _():
        head_ref[:, pl.ds(pl.multiple_of((tp * width) % half, width), width)] = part_ref[...]

    chunk_body((near_ref, far_ref), gain_ref, head_ref, keyval_ref, query_ref, outs,
               waits[:len(large)])
    for wait in waits[len(large):]:
        wait()


def next_chunk_kernel(*refs, chips):
    pieces, refs = refs[:2 * chips], refs[2 * chips:]
    chunk_body(pieces, *refs[:4], refs[4:], [])


def last_chunk_kernel(*refs):
    chunk_body(refs[:2], *refs[2:6], refs[10:], [], refs[6:10])


def shape_of(*shape, kind=BF16):
    return jax.ShapeDtypeStruct(shape, kind)


def chunk_shapes(rows, half):
    return (shape_of(rows, half), shape_of(rows, LANES, kind=F32))


def first_chunk(near, far, gain, head, keyval, query):
    count, wide = near.shape
    half = wide - LANES
    columns = query.shape[1] // 2
    rows = 2 * count
    shapes = chunk_shapes(rows, half) + (
        shape_of(rows, 2 * HEAD, kind=F32), shape_of(rows, columns + 2 * HEAD),
        shape_of(1, half), shape_of(1, half), shape_of(*keyval.shape), shape_of(half, columns),
        shape_of(half, columns))
    out = pl.pallas_call(
        first_chunk_kernel,
        out_shape=shapes,
        in_specs=[whole(), whole()] + [whole(pltpu.HBM)] * 4,
        out_specs=(whole(),) * len(shapes),
        scratch_shapes=[
            pltpu.VMEM(head.shape, BF16),
            pltpu.SemaphoreType.DMA((2,)),
            pltpu.SemaphoreType.DMA(((columns + keyval.shape[1]) // BLOCK,)),
            pltpu.SemaphoreType.DMA((columns // BLOCK,)),
        ],
        compiler_params=pltpu.CompilerParams(vmem_limit_bytes=14 << 20),
        name="first_chunk",
    )(near, far, gain, head, keyval, query)
    return out[:4], out[4:8], out[8]


def next_chunk(pieces, weights):
    count, wide = pieces[0].shape
    chips = len(pieces) // 2
    rows = 2 * chips * count
    shapes = chunk_shapes(rows, wide - LANES) + (
        shape_of(rows, 2 * HEAD, kind=F32), shape_of(rows, weights[3].shape[1]), shape_of(rows, 2 * HEAD))
    return pl.pallas_call(
        functools.partial(next_chunk_kernel, chips=chips),
        out_shape=shapes,
        in_specs=[whole()] * (len(pieces) + 4),
        out_specs=(whole(),) * len(shapes),
        compiler_params=pltpu.CompilerParams(vmem_limit_bytes=14 << 20),
        name="next_chunk",
    )(*pieces, *weights)


def last_chunk(pieces, weights, parts):
    count, wide = pieces[0].shape
    rows = 2 * count
    shapes = chunk_shapes(rows, wide - LANES) + (
        shape_of(rows, weights[3].shape[1]),) + (shape_of(4 * rows, HEAD),) * 3 + (shape_of(rows, HEAD),) * 2
    return pl.pallas_call(
        last_chunk_kernel,
        out_shape=shapes,
        in_specs=[whole()] * (len(pieces) + 8),
        out_specs=(whole(),) * len(shapes),
        compiler_params=pltpu.CompilerParams(vmem_limit_bytes=14 << 20),
        name="last_chunk",
    )(*pieces, *weights, *parts)


def own_body(rows_ref, query_ref, out_ref, waits=()):
    for index in range(query_ref.shape[1] // BLOCK):
        if waits:
            waits[index]()
        at = slice(index * BLOCK, (index + 1) * BLOCK)
        out_ref[:, at] = jnp.dot(rows_ref[...], query_ref[:, at], preferred_element_type=F32)


def own_queries(rows, query):
    return pl.pallas_call(
        own_body,
        out_shape=shape_of(rows.shape[0], query.shape[1], kind=F32),
        in_specs=[whole(), whole()],
        out_specs=whole(),
        compiler_params=pltpu.CompilerParams(vmem_limit_bytes=10 << 20),
        name="own_queries",
    )(rows, query)


def slabs(refs, starts, count, at=slice(None)):
    return [ref[start:start + count, at].astype(F32) for ref, start in zip(refs, starts)]


def by_pack(parts, pack):
    count = parts[0].shape[0] // 2
    return jnp.concatenate([part[pack * count:(pack + 1) * count] for part in parts], axis=0)


def owner_of(row, pack, ids, piece_rows):
    index = jnp.zeros_like(row)
    for step in range(1, 8):
        index = index + (row >= step * piece_rows).astype(jnp.int32)
    chip, low = index >> 1, index & 1
    shard = (((chip >> 1) ^ ids[2]) * 2 + (low ^ pack)) * 2 + ((chip & 1) ^ ids[1])
    return shard, row - index * piece_rows


def padded(rows):
    return -(-rows // LANES) * LANES


def mask_kernel(lengths_ref, near_ref, out_ref):
    ids = position()
    segment = ids[1]
    rows = out_ref.shape[0] // 2
    piece_rows = rows // 8
    tail = near_ref[:, near_ref.shape[1] - LANES:].astype(F32)[:1].astype(jnp.int32)
    for pack in range(2):
        def place(row):
            shard, inner = owner_of(row, pack, ids, piece_rows)
            place_in_pack = shard * piece_rows + inner
            end = jnp.zeros((1, 1), jnp.int32)
            doc = jnp.zeros_like(place_in_pack)
            for index in range(lengths_ref.shape[1]):
                at = LENGTHS_AT + index
                end = end + jnp.where(segment == pack, lengths_ref[0, index], tail[:, at:at + 1])
                doc = doc + (place_in_pack >= end).astype(jnp.int32)
            return place_in_pack, doc

        row_position, row_doc = place(iota((rows, 1), 0))
        column = iota((1, out_ref.shape[1]), 1)
        col_position, col_doc = place(column)
        visible = jnp.logical_and(row_doc == col_doc, col_position <= row_position)
        visible = jnp.logical_and(visible, column < rows)
        out_ref[pack * rows:(pack + 1) * rows, :] = jnp.where(visible, 0.0, -1e30)


def masks(lengths, near, rows):
    return pl.pallas_call(
        mask_kernel,
        out_shape=shape_of(2 * rows, padded(rows), kind=F32),
        in_specs=[whole(pltpu.SMEM), whole()],
        out_specs=whole(),
        compiler_params=pltpu.CompilerParams(vmem_limit_bytes=4 << 20),
        name="masks",
    )(lengths, near)


def place_rows(chosen, spread):
    high = spread.astype(BF16)
    rest = spread - high.astype(F32)
    middle = rest.astype(BF16)
    low = (rest - middle.astype(F32)).astype(BF16)
    parts = jnp.concatenate([high, middle, low], axis=1)
    placed = jnp.dot(chosen, parts, preferred_element_type=F32)
    wide = spread.shape[1]
    return placed[:, :wide] + placed[:, wide:2 * wide] + placed[:, 2 * wide:]


def placement_kernel(*refs, starts):
    directs, (direct_ref, chosen_ref, hit_ref) = refs[:-3], refs[-3:]
    ids = position()
    devices = direct_ref.shape[0]
    rows = hit_ref.shape[0] // 2
    slab = rows // 2
    piece_rows = rows // 8
    lane = iota((rows, LANES), 1)
    for pack in range(2):
        _, inner = owner_of(iota((rows, 1), 0), pack, ids, piece_rows)
        shard_row, _ = owner_of(iota((1, rows), 1), pack, ids, piece_rows)
        chosen = jnp.where((iota((devices, 1), 0) >> 2) == shard_row, 1.0, 0.0).astype(BF16)
        hit = jnp.where(lane == inner + pack * piece_rows, 1.0, 0.0)
        column = jnp.sum(by_pack(slabs(directs, starts, slab), pack), axis=1, keepdims=True)
        placed = place_rows(chosen, hit * column)
        direct_ref[...] = placed if pack == 0 else direct_ref[...] + placed
        chosen_ref[:, pack * rows:(pack + 1) * rows] = chosen
        hit_ref[pack * rows:(pack + 1) * rows, :] = hit


def placement(directs, starts, rows, devices):
    return pl.pallas_call(
        functools.partial(placement_kernel, starts=starts),
        out_shape=(
            shape_of(devices, LANES, kind=F32), shape_of(devices, 2 * rows), shape_of(2 * rows, LANES, kind=F32)),
        in_specs=[whole()] * len(directs),
        out_specs=(whole(),) * 3,
        compiler_params=pltpu.CompilerParams(vmem_limit_bytes=6 << 20),
        name="placement",
    )(*directs)


def attention_kernel(bias_ref, *refs, starts, recv_starts):
    chips = len(starts)
    owns, recvs, refs = refs[:chips], refs[chips:2 * chips], refs[2 * chips:]
    direct_ref, chosen_ref, hit_ref = refs[:3]
    nears, fars, gain_ref, out_ref = refs[3:6], refs[6:8], refs[8], refs[9]
    expo_ref, weight_ref = refs[10:]
    ids = position()
    segment, tp = ids[1], ids[3]
    rows = bias_ref.shape[0] // 2
    keys_wide = bias_ref.shape[1]
    slab = rows // 2
    heads = owns[0].shape[1] // HEAD
    wide = out_ref.shape[1] // 2
    scale = math.log2(math.e) / math.sqrt(HEAD)
    lane = iota((rows, wide), 1)
    used = lane < 2 * heads
    gains = [gain_ref[:, pl.ds(pl.multiple_of((segment * heads + head) * HEAD, HEAD), HEAD)].astype(F32)
             for head in range(heads)]
    gains = jnp.concatenate(gains * 2 + [jnp.zeros((LANES - 2 * heads, HEAD), F32)], axis=0).astype(BF16)

    def chosen_keys(refs):
        keep, first, second = (ref[...].astype(F32) for ref in refs)
        return (jnp.where(tp == 0, keep, jnp.where(tp == 2, second, first)),
                jnp.where(tp == 3, keep, jnp.where(tp == 1, second, first)))

    def pack_part(part, pack):
        count = part.shape[0] // 2
        return part[pack * count:(pack + 1) * count]

    far_first, far_second = (ref[...].astype(F32) for ref in fars)
    odd = (tp & 1) == 1
    far = (jnp.where(odd, far_first, far_second), jnp.where(odd, far_second, far_first))
    near = chosen_keys(nears)
    totals = []
    for pack in range(2):
        keys, values = (
            jnp.concatenate([
                pack_part(near_part, pack)[:slab],
                pack_part(near_part, pack)[slab:slab + slab // 2] + pack_part(far_part, pack),
                pack_part(near_part, pack)[slab + slab // 2:]], axis=0)
            for near_part, far_part in zip(near, far))
        keys = jnp.concatenate([keys, jnp.zeros((keys_wide - rows, HEAD), F32)], axis=0).astype(BF16)
        high = values.astype(BF16)
        rest = (values - high.astype(F32)).astype(BF16)
        product = (((1,), (1,)), ((), ()))
        score = (lax.dot_general(high, gains, product, preferred_element_type=F32)
                 + lax.dot_general(rest, gains, product, preferred_element_type=F32))
        high = score.astype(BF16).astype(F32)
        score = jnp.where(lane < heads, high, score - high)
        for head in range(heads):
            here = jnp.logical_and(used, (lane & (heads - 1)) == head)
            block = jnp.concatenate([jnp.where(here, score, 0.0), jnp.where(here, 1.0, 0.0)], axis=1)
            block = jnp.concatenate([block, jnp.zeros((keys_wide - rows, 2 * LANES), F32)], axis=0)
            weight_ref[head * keys_wide:(head + 1) * keys_wide, :] = block.astype(BF16)

            at = slice(head * HEAD, (head + 1) * HEAD)
            parts = [own + recv for own, recv in zip(
                slabs(owns, starts, slab, at), slabs(recvs, recv_starts, slab, at))]
            query = (by_pack(parts, pack) * scale).astype(BF16)
            logits = lax.dot_general(query, keys, product, preferred_element_type=F32)
            logits = logits + bias_ref[pack * rows:(pack + 1) * rows, :]
            expo = jnp.exp2(logits - jnp.max(logits, axis=1, keepdims=True)).astype(BF16)
            expo_ref[:, head * keys_wide:(head + 1) * keys_wide] = expo
        both = jnp.dot(expo_ref[...], weight_ref[...], preferred_element_type=F32)
        total = both[:, :LANES] / jnp.where(used, both[:, LANES:], 1.0)

        totals.append(jnp.sum(total, axis=1, keepdims=True))
    spread = hit_ref[...] * jnp.concatenate(totals, axis=0)
    out_ref[:, :wide] = place_rows(chosen_ref[...], spread)
    out_ref[:, wide:] = direct_ref[...]


def attention(bias, owns, starts, recvs, recv_starts, places, near, far, gain, devices):
    heads = owns[0].shape[1] // HEAD
    return pl.pallas_call(
        functools.partial(attention_kernel, starts=starts, recv_starts=recv_starts),
        out_shape=shape_of(devices, 2 * LANES, kind=F32),
        in_specs=[whole()] * (10 + 2 * len(owns)),
        out_specs=whole(),
        scratch_shapes=[
            pltpu.VMEM((bias.shape[0] // 2, heads * bias.shape[1]), BF16),
            pltpu.VMEM((heads * bias.shape[1], 2 * LANES), BF16),
        ],
        compiler_params=pltpu.CompilerParams(vmem_limit_bytes=14 << 20),
        name="attend",
    )(bias, *owns, *recvs, *places, *near, *far, gain)


def finish_kernel(recv_ref, send_ref, out_ref):
    models, count = out_ref.shape
    devices, width = recv_ref.shape
    model_of = iota((models, devices), 1) // (devices // models)
    chosen = (model_of == iota((models, devices), 0)).astype(F32)
    sums = jnp.dot(chosen, recv_ref[...], precision=HIGHEST, preferred_element_type=F32)
    pick = (iota((count, count), 0) == send_ref[...]).astype(F32)
    half = width // 2
    both = sums[:, :count] + sums[:, half:half + count]
    out_ref[...] = lax.dot_general(
        both, pick, (((1,), (1,)), ((), ())), precision=HIGHEST, preferred_element_type=F32)


def finish(recv, send, models):
    count = send.shape[1]
    return pl.pallas_call(
        finish_kernel,
        out_shape=jax.ShapeDtypeStruct((models, count), F32),
        in_specs=[whole()] * 2,
        out_specs=whole(),
        compiler_params=pltpu.CompilerParams(vmem_limit_bytes=8 << 20),
        name="finish",
    )(recv, send)


def paired(rollout, send_rows, seq_lengths, attn_gain, w_query, w_keyval, head_weight, head_attn):
    n_branch = lax.axis_size("branch")
    send = send_rows.reshape(1, -1)

    core_pairs = [(i, i ^ 1) for i in range(n_branch)]
    y_pairs = [(i, i ^ 2) for i in range(n_branch)]
    x_pairs = [(0, 1), (1, 0)]

    def swap(piece):
        return lax.ppermute(piece, "branch", core_pairs)

    def across(part):
        return lax.ppermute(part, "segment", x_pairs)

    def in_hbm(array):
        return pltpu.with_memory_space_constraint(array, pltpu.HBM)

    packing = send
    rollout, send, attn_gain, head_weight, seq_lengths = map(
        in_hbm, (rollout, send, attn_gain, head_weight, seq_lengths))
    wq, wkv = in_hbm(w_query[0]), in_hbm(w_keyval[0])
    mine, theirs = prepare(seq_lengths, rollout, send)
    from_x = across(theirs)
    from_y = lax.ppermute(mine, "branch", y_pairs)
    from_d = lax.ppermute(from_x, "branch", y_pairs)

    slab = 2 * mine.shape[0]

    def with_swapped(*pieces):
        return [part for piece in pieces for part in (piece, swap(piece))]

    pieces = with_swapped(mine)
    (rows, direct_own, local_own, part), weights, own_weights = first_chunk(
        *pieces, attn_gain, head_weight, wkv, wq)
    received_own = across(part)
    query_own = own_queries(rows, own_weights)
    bias = masks(seq_lengths, from_x, 2 * slab)

    pieces = with_swapped(from_x) + with_swapped(from_y)
    rows, direct_xy, local_xy, part, keyval = next_chunk(pieces, weights)
    keyval_xy = across(keyval)
    received_xy = across(part)
    query_xy = own_queries(rows, own_weights)

    hand_first, hand_second = (1, 3, 0, 2), (0, 2, 1, 3)
    n_tp = len(hand_first)

    def hand(array, targets):
        return lax.ppermute(array, "tp", [(i, to) for i, to in enumerate(targets) if i != to])

    def hand_across(array, targets):
        return lax.ppermute(array, ("segment", "tp"), [
            (side * n_tp + i, (1 - side) * n_tp + to) for side in range(2) for i, to in enumerate(targets)])

    pieces = with_swapped(from_d)
    rows, direct_d, part, keep, first, second, far_first, far_second = last_chunk(
        pieces, weights, (local_own, local_xy, keyval_xy, received_own))
    received_d = across(part)
    first = hand(first, hand_first)
    second = hand(second, hand_second)
    far_first = hand_across(far_first, hand_first)
    far_second = hand_across(far_second, hand_second)
    query_d = own_queries(rows, own_weights)
    devices = n_branch * 2 * n_tp
    places = placement([direct_own, direct_xy, direct_xy, direct_d], (0, 0, slab, 0), 2 * slab, devices)
    outgoing = attention(
        bias, [query_own, query_xy, query_xy, query_d], (0, 0, slab, 0),
        [received_xy, received_own, received_d, received_xy], (0, 0, 0, slab),
        places, (keep, first, second), (far_first, far_second), head_attn, devices)
    incoming = lax.all_to_all(outgoing, ALL_AXES, split_axis=0, concat_axis=0, tiled=True)
    return finish(incoming, packing, n_branch)


def general(rollout, send_rows, seq_lengths, attn_gain, w_query, w_keyval, head_weight, head_attn):
    n_branch = lax.axis_size("branch")
    n_segment = lax.axis_size("segment")
    gen_rows = rollout.shape[0]
    piece_rows = gen_rows // n_segment
    row_width = rollout.shape[1]
    ordered = jnp.take(rollout, send_rows, axis=0).reshape(n_segment, piece_rows, row_width)
    copies = jnp.broadcast_to(ordered[None], (n_branch, n_segment, piece_rows, row_width))
    copies = copies.reshape(n_branch * n_segment, piece_rows, row_width)
    arrived = lax.all_to_all(copies, ("branch", "segment"), split_axis=0, concat_axis=0, tiled=True)
    packed = arrived.reshape(-1, row_width)
    pack_rows = packed.shape[0]
    rows_float = packed.astype(jnp.float32)
    mean_square = jnp.mean(rows_float * rows_float, axis=-1, keepdims=True)
    normed = (
        rows_float * lax.rsqrt(mean_square + epsilon) * attn_gain[0].astype(jnp.float32)
    ).astype(jnp.bfloat16)
    query_acc = jnp.dot(
        normed,
        lax.all_gather(w_query, "segment", axis=1, tiled=True)[0],
        preferred_element_type=jnp.float32,
    )
    keyval_acc = jnp.dot(
        normed,
        lax.all_gather(w_keyval, "segment", axis=1, tiled=True)[0],
        preferred_element_type=jnp.float32,
    )
    queries = query_acc.astype(jnp.bfloat16)
    keyval_part = keyval_acc.astype(jnp.bfloat16)
    keyval = lax.all_gather(keyval_part, "tp", axis=1, tiled=True)
    tp_index = lax.axis_index("tp")
    heads_here = queries.shape[1] // HEAD
    group_size = HEADS // KV_HEADS
    per_group = min(heads_here, group_size)
    group_span = heads_here // per_group
    kv_first = tp_index * heads_here // group_size
    key_rows = lax.dynamic_slice_in_dim(keyval, kv_first * HEAD, group_span * HEAD, 1)
    value_rows = lax.dynamic_slice_in_dim(
        keyval, KV_HEADS * HEAD + kv_first * HEAD, group_span * HEAD, 1
    )
    key_rows = key_rows.reshape(pack_rows, group_span, HEAD)
    value_rows = value_rows.reshape(pack_rows, group_span, HEAD)
    queries = queries.reshape(pack_rows, group_span, per_group, HEAD)
    positions = jnp.arange(pack_rows, dtype=jnp.int32)
    doc_ends = jnp.cumsum(seq_lengths[0])
    doc_ids = jnp.sum((positions[:, None] >= doc_ends[None, :]).astype(jnp.int32), axis=-1)
    visible = (doc_ids[:, None] == doc_ids[None, :]) & (positions[None, :] <= positions[:, None])
    logits = jnp.einsum(
        "qgpc,kgc->gpqk", queries, key_rows, preferred_element_type=jnp.float32
    ) / math.sqrt(HEAD)
    logits = jnp.where(visible[None, None], logits, -1e30)
    row_max = jnp.max(logits, axis=-1, keepdims=True)
    expo = jnp.exp(logits - row_max)
    probabilities = (expo / jnp.sum(expo, axis=-1, keepdims=True)).astype(jnp.bfloat16)
    attended = jnp.einsum(
        "gpqk,kgc->qgpc", probabilities, value_rows, preferred_element_type=jnp.float32
    )
    attended = attended.reshape(pack_rows, heads_here * HEAD)
    slice_width = head_weight.shape[1]
    own_columns = lax.dynamic_slice_in_dim(packed, tp_index * slice_width, slice_width, 1)
    direct = jnp.dot(own_columns, head_weight[0], preferred_element_type=jnp.float32)
    through = jnp.dot(attended, head_attn[0].astype(jnp.float32), precision=lax.Precision.HIGHEST)
    totals = lax.psum(direct + through, "tp")
    outgoing = totals.reshape(n_branch * n_segment, piece_rows)
    incoming = lax.all_to_all(
        outgoing, ("branch", "segment"), split_axis=0, concat_axis=0, tiled=True
    )
    incoming = incoming.reshape(n_branch, n_segment * piece_rows)
    scores = jnp.zeros((n_branch, gen_rows), jnp.float32).at[:, send_rows].set(incoming)
    return scores


def solution(mesh):
    sizes = tuple(mesh.shape[axis] for axis in ALL_AXES)
    pairwise = sizes == (4, 2, 4)
    local = paired if pairwise else general
    return jax.shard_map(
        local,
        mesh=mesh,
        in_specs=(
            P(("branch", "segment"), None),
            P(("branch", "segment")),
            P("segment", None),
            P("branch", None),
            P("branch", "segment", "tp"),
            P("branch", "segment", "tp"),
            P("branch", "tp"),
            P("branch", "tp"),
        ),
        out_specs=P(None, ("branch", "segment")),
        check_vma=False,
    )
```

```python
import functools
import math

import jax
import jax.numpy as jnp
from jax import lax
from jax.experimental import pallas as pl
from jax.experimental.pallas import tpu as pltpu
from jax.sharding import PartitionSpec as P


HEAD = 128
HEADS = 64
KV_HEADS = 8
LANES = 128
LENGTHS_AT = 8

epsilon = 1e-05

ALL_AXES = ("branch", "segment", "tp")
HIGHEST = lax.Precision.HIGHEST
F32 = jnp.float32
BF16 = jnp.bfloat16


def whole(memory_space=pltpu.VMEM):
    return pl.BlockSpec(memory_space=memory_space)


def position():
    branch = lax.axis_index("branch")
    return branch & 1, lax.axis_index("segment"), branch >> 1, lax.axis_index("tp")


def iota(shape, dimension):
    return lax.broadcasted_iota(jnp.int32, shape, dimension)


def prepare_kernel(lengths_hbm, rows_hbm, send_hbm, mine_ref, theirs_ref, rows_ref, send_ref, lengths_ref, sems):
    ids = position()
    count, width = rows_ref.shape
    half = width // 2
    parts = sems.shape[0] - 2
    step = width // parts
    core, segment = ids[0], ids[1]
    copies = [pltpu.make_async_copy(send_hbm, send_ref, sems.at[parts])]
    for part in range(parts):
        at = pl.ds(part * step, step)
        copies.append(pltpu.make_async_copy(rows_hbm.at[:, at], rows_ref.at[:, at], sems.at[part]))
    lengths_copy = pltpu.make_async_copy(lengths_hbm, lengths_ref, sems.at[parts + 1])
    for copy in copies + [lengths_copy]:
        copy.start()
    copies[0].wait()
    send = send_ref[...]
    rolled = jnp.concatenate([send[:, count // 2:], send[:, :count // 2]], axis=1)
    order = jnp.where(core == 1, rolled, send)
    pick = (iota((count, count), 0) == order).astype(BF16)

    def ordered(part):
        out = lax.dot_general(pick, part, (((0,), (0,)), ((), ())), preferred_element_type=F32)
        return out.astype(BF16)

    lanes = jnp.zeros((count, LANES), F32)
    for part in range(parts):
        copies[1 + part].wait()
        square = rows_ref[:, part * step:(part + 1) * step].astype(F32)
        square = square * square
        for lane in range(0, step, LANES):
            lanes = lanes + square[:, lane:lane + LANES]
    chunk = 1024
    for start in range(0, half, chunk):
        for out_ref, which in ((theirs_ref, 1 - segment), (mine_ref, segment)):
            at = pl.multiple_of(which * half + start, chunk)
            out_ref[:, start:start + chunk] = ordered(rows_ref[:, pl.ds(at, chunk)])
    scale = lax.rsqrt(jnp.sum(lanes, axis=1, keepdims=True) * (1.0 / width) + epsilon)
    high = scale.astype(BF16).astype(F32)
    middle = (scale - high).astype(BF16).astype(F32)
    low = scale - high - middle
    lane = iota((count, LANES), 1)
    tail = jnp.where(lane == 0, high, jnp.where(lane == 1, middle, jnp.where(lane == 2, low, 0.0)))
    tail = ordered(tail.astype(BF16))
    lengths_copy.wait()
    for index in range(lengths_ref.shape[1]):
        length = lengths_ref[0, index].astype(F32).astype(BF16)
        tail = jnp.where(lane == LENGTHS_AT + index, length, tail)
    theirs_ref[:, half:] = tail
    mine_ref[:, half:] = tail


def prepare(lengths, rows, send):
    count, width = rows.shape
    shape = jax.ShapeDtypeStruct((count, width // 2 + LANES), BF16)
    return pl.pallas_call(
        prepare_kernel,
        out_shape=(shape, shape),
        in_specs=[whole(pltpu.HBM)] * 3,
        out_specs=(whole(), whole()),
        scratch_shapes=[
            pltpu.VMEM((count, width), BF16),
            pltpu.VMEM((1, count), jnp.int32),
            pltpu.SMEM(lengths.shape, jnp.int32),
            pltpu.SemaphoreType.DMA((6,)),
        ],
        compiler_params=pltpu.CompilerParams(vmem_limit_bytes=12 << 20),
        name="prepare",
    )(lengths, rows, send)


BLOCK = 256
IN_FLIGHT = 4


def column_copies(source, first, target, sems):
    blocks = target.shape[1] // BLOCK
    return [
        pltpu.make_async_copy(
            source.at[:, pl.ds(pl.multiple_of(first + index * BLOCK, BLOCK), BLOCK)],
            target.at[:, pl.ds(index * BLOCK, BLOCK)], sems.at[index])
        for index in range(blocks)]


def split_slots(values):
    return values[:, :HEAD], values[:, HEAD:]


def chunk_body(pieces, gain_ref, head_ref, keyval_ref, query_ref, outs, waits, recv=None):
    rows_ref, direct_ref = outs[:2]
    count = pieces[0].shape[0]
    half = rows_ref.shape[1]
    core, segment, _, tp = position()
    columns = query_ref.shape[1]
    top = (iota((count, 1), 0) < count // 2).astype(jnp.int32)
    mask = (top ^ core) == 1

    def sorted_rows(values):
        near, far = values[0::2], values[1::2]
        return jnp.concatenate(
            [part for n, f in zip(near, far) for part in (jnp.where(mask, n, f), jnp.where(mask, f, n))], axis=0)

    first_lanes = iota((count, LANES), 1) < 3
    scale = sorted_rows([
        jnp.sum(jnp.where(first_lanes, ref[:, half:].astype(F32), 0.0), axis=1, keepdims=True) for ref in pieces])
    chunk = 512
    direct = jnp.zeros((direct_ref.shape[0], LANES), F32)
    for start in range(0, half, chunk):
        at = slice(start, start + chunk)
        rows = sorted_rows([ref[:, at].astype(F32) for ref in pieces])
        weight = head_ref[:, at].astype(F32)
        for lane in range(0, chunk, LANES):
            direct = direct + rows[:, lane:lane + LANES] * weight[:, lane:lane + LANES]
        rows_ref[:, at] = (rows * scale * gain_ref[:, at].astype(F32)).astype(BF16)
    direct_ref[...] = direct

    for wait in waits[:keyval_ref.shape[1] // BLOCK]:
        wait()
    keyval = jnp.dot(rows_ref[...], keyval_ref[...], preferred_element_type=F32)
    even = jnp.concatenate([keyval[:, :HEAD], keyval[:, 2 * HEAD:3 * HEAD]], axis=1)
    odd = jnp.concatenate([keyval[:, HEAD:2 * HEAD], keyval[:, 3 * HEAD:]], axis=1)
    own = jnp.where(segment == 0, even, odd)
    other = jnp.where(segment == 0, odd, even)
    if recv is None:
        own_ref, send_ref = outs[2:4]
        own_ref[...] = own
        if len(outs) > 4:
            outs[4][...] = other.astype(BF16)
        else:
            send_ref[:, columns:] = other.astype(BF16)
    else:
        send_ref, keep_ref, first_ref, second_ref, far_first_ref, far_second_ref = outs[2:]
        own_part_ref, pair_part_ref, recv_own_ref, recv_next_ref = recv
        slab = 2 * count
        mine, x_part, y_part = slabs((own_part_ref, pair_part_ref, pair_part_ref), (0, 0, slab), slab)
        at = slice(columns, columns + 2 * HEAD)
        sums = [mine + recv_own_ref[:slab, :].astype(F32), x_part + recv_next_ref[:, at].astype(F32), y_part,
                own + recv_own_ref[slab:, :].astype(F32)]
        low, high = split_slots(jnp.concatenate([by_pack(sums, pack) for pack in range(2)], axis=0))
        keep_ref[...] = jnp.where(tp == 3, high, low).astype(BF16)
        first_ref[...] = jnp.where(tp < 2, high, low).astype(BF16)
        second_ref[...] = jnp.where(tp == 2, high, low).astype(BF16)
        low, high = split_slots(other)
        far_first_ref[...] = jnp.where(tp < 2, high, low).astype(BF16)
        far_second_ref[...] = jnp.where(tp < 2, low, high).astype(BF16)
    waits = waits[keyval_ref.shape[1] // BLOCK:]
    for index in range(columns // BLOCK):
        if waits:
            waits[index]()
        at = slice(index * BLOCK, (index + 1) * BLOCK)
        send_ref[:, at] = jnp.dot(rows_ref[...], query_ref[:, at], preferred_element_type=F32).astype(BF16)


def first_chunk_kernel(near_ref, far_ref, gain_hbm, head_hbm, keyval_hbm, query_hbm, *refs):
    outs, (gain_ref, head_ref, keyval_ref, query_ref) = refs[:4], refs[4:8]
    own_query_ref, part_ref, small_sems, sems, own_sems = refs[8:]
    rows_ref = outs[0]
    half = rows_ref.shape[1]
    _, segment, _, tp = position()
    small = [
        pltpu.make_async_copy(
            gain_hbm.at[:, pl.ds(pl.multiple_of(segment * half, half), half)], gain_ref, small_sems.at[0]),
        pltpu.make_async_copy(head_hbm, part_ref, small_sems.at[1]),
    ]
    blocks = keyval_ref.shape[1] // BLOCK
    large = column_copies(keyval_hbm, 0, keyval_ref, sems)
    large += column_copies(query_hbm, (1 - segment) * query_ref.shape[1], query_ref, sems.at[pl.ds(blocks, query_ref.shape[1] // BLOCK)])
    owns = column_copies(query_hbm, segment * query_ref.shape[1], own_query_ref, own_sems)
    copies = large + owns
    for copy in small + copies[:IN_FLIGHT]:
        copy.start()

    def waiter(index):
        def wait():
            copies[index].wait()
            if index + IN_FLIGHT < len(copies):
                copies[index + IN_FLIGHT].start()

        return wait

    waits = [waiter(index) for index in range(len(copies))]
    for copy in small:
        copy.wait()
    width = part_ref.shape[1]
    head_ref[...] = jnp.zeros_like(head_ref)

    @pl.when((tp * width) // half == segment)
    def _():
        head_ref[:, pl.ds(pl.multiple_of((tp * width) % half, width), width)] = part_ref[...]

    chunk_body((near_ref, far_ref), gain_ref, head_ref, keyval_ref, query_ref, outs,
               waits[:len(large)])
    for wait in waits[len(large):]:
        wait()


def next_chunk_kernel(*refs, chips):
    pieces, refs = refs[:2 * chips], refs[2 * chips:]
    chunk_body(pieces, *refs[:4], refs[4:], [])


def last_chunk_kernel(*refs):
    chunk_body(refs[:2], *refs[2:6], refs[10:], [], refs[6:10])


def shape_of(*shape, kind=BF16):
    return jax.ShapeDtypeStruct(shape, kind)


def chunk_shapes(rows, half):
    return (shape_of(rows, half), shape_of(rows, LANES, kind=F32))


def first_chunk(near, far, gain, head, keyval, query):
    count, wide = near.shape
    half = wide - LANES
    columns = query.shape[1] // 2
    rows = 2 * count
    shapes = chunk_shapes(rows, half) + (
        shape_of(rows, 2 * HEAD, kind=F32), shape_of(rows, columns + 2 * HEAD),
        shape_of(1, half), shape_of(1, half), shape_of(*keyval.shape), shape_of(half, columns),
        shape_of(half, columns))
    out = pl.pallas_call(
        first_chunk_kernel,
        out_shape=shapes,
        in_specs=[whole(), whole()] + [whole(pltpu.HBM)] * 4,
        out_specs=(whole(),) * len(shapes),
        scratch_shapes=[
            pltpu.VMEM(head.shape, BF16),
            pltpu.SemaphoreType.DMA((2,)),
            pltpu.SemaphoreType.DMA(((columns + keyval.shape[1]) // BLOCK,)),
            pltpu.SemaphoreType.DMA((columns // BLOCK,)),
        ],
        compiler_params=pltpu.CompilerParams(vmem_limit_bytes=14 << 20),
        name="first_chunk",
    )(near, far, gain, head, keyval, query)
    return out[:4], out[4:8], out[8]


def next_chunk(pieces, weights):
    count, wide = pieces[0].shape
    chips = len(pieces) // 2
    rows = 2 * chips * count
    shapes = chunk_shapes(rows, wide - LANES) + (
        shape_of(rows, 2 * HEAD, kind=F32), shape_of(rows, weights[3].shape[1]), shape_of(rows, 2 * HEAD))
    return pl.pallas_call(
        functools.partial(next_chunk_kernel, chips=chips),
        out_shape=shapes,
        in_specs=[whole()] * (len(pieces) + 4),
        out_specs=(whole(),) * len(shapes),
        compiler_params=pltpu.CompilerParams(vmem_limit_bytes=14 << 20),
        name="next_chunk",
    )(*pieces, *weights)


def last_chunk(pieces, weights, parts):
    count, wide = pieces[0].shape
    rows = 2 * count
    shapes = chunk_shapes(rows, wide - LANES) + (
        shape_of(rows, weights[3].shape[1]),) + (shape_of(4 * rows, HEAD),) * 3 + (shape_of(rows, HEAD),) * 2
    return pl.pallas_call(
        last_chunk_kernel,
        out_shape=shapes,
        in_specs=[whole()] * (len(pieces) + 8),
        out_specs=(whole(),) * len(shapes),
        compiler_params=pltpu.CompilerParams(vmem_limit_bytes=14 << 20),
        name="last_chunk",
    )(*pieces, *weights, *parts)


def own_body(rows_ref, query_ref, out_ref, waits=()):
    for index in range(query_ref.shape[1] // BLOCK):
        if waits:
            waits[index]()
        at = slice(index * BLOCK, (index + 1) * BLOCK)
        out_ref[:, at] = jnp.dot(rows_ref[...], query_ref[:, at], preferred_element_type=F32)


def own_queries(rows, query):
    return pl.pallas_call(
        own_body,
        out_shape=shape_of(rows.shape[0], query.shape[1], kind=F32),
        in_specs=[whole(), whole()],
        out_specs=whole(),
        compiler_params=pltpu.CompilerParams(vmem_limit_bytes=10 << 20),
        name="own_queries",
    )(rows, query)


def slabs(refs, starts, count, at=slice(None)):
    return [ref[start:start + count, at].astype(F32) for ref, start in zip(refs, starts)]


def by_pack(parts, pack):
    count = parts[0].shape[0] // 2
    return jnp.concatenate([part[pack * count:(pack + 1) * count] for part in parts], axis=0)


def owner_of(row, pack, ids, piece_rows):
    index = jnp.zeros_like(row)
    for step in range(1, 8):
        index = index + (row >= step * piece_rows).astype(jnp.int32)
    chip, low = index >> 1, index & 1
    shard = (((chip >> 1) ^ ids[2]) * 2 + (low ^ pack)) * 2 + ((chip & 1) ^ ids[1])
    return shard, row - index * piece_rows


def padded(rows):
    return -(-rows // LANES) * LANES


def mask_kernel(lengths_ref, near_ref, out_ref):
    ids = position()
    segment = ids[1]
    rows = out_ref.shape[0] // 2
    piece_rows = rows // 8
    tail = near_ref[:, near_ref.shape[1] - LANES:].astype(F32)[:1].astype(jnp.int32)
    for pack in range(2):
        def place(row):
            shard, inner = owner_of(row, pack, ids, piece_rows)
            place_in_pack = shard * piece_rows + inner
            end = jnp.zeros((1, 1), jnp.int32)
            doc = jnp.zeros_like(place_in_pack)
            for index in range(lengths_ref.shape[1]):
                at = LENGTHS_AT + index
                end = end + jnp.where(segment == pack, lengths_ref[0, index], tail[:, at:at + 1])
                doc = doc + (place_in_pack >= end).astype(jnp.int32)
            return place_in_pack, doc

        row_position, row_doc = place(iota((rows, 1), 0))
        column = iota((1, out_ref.shape[1]), 1)
        col_position, col_doc = place(column)
        visible = jnp.logical_and(row_doc == col_doc, col_position <= row_position)
        visible = jnp.logical_and(visible, column < rows)
        out_ref[pack * rows:(pack + 1) * rows, :] = jnp.where(visible, 0.0, -1e30)


def masks(lengths, near, rows):
    return pl.pallas_call(
        mask_kernel,
        out_shape=shape_of(2 * rows, padded(rows), kind=F32),
        in_specs=[whole(pltpu.SMEM), whole()],
        out_specs=whole(),
        compiler_params=pltpu.CompilerParams(vmem_limit_bytes=4 << 20),
        name="masks",
    )(lengths, near)


def place_rows(chosen, spread):
    high = spread.astype(BF16)
    rest = spread - high.astype(F32)
    middle = rest.astype(BF16)
    low = (rest - middle.astype(F32)).astype(BF16)
    parts = jnp.concatenate([high, middle, low], axis=1)
    placed = jnp.dot(chosen, parts, preferred_element_type=F32)
    wide = spread.shape[1]
    return placed[:, :wide] + placed[:, wide:2 * wide] + placed[:, 2 * wide:]


def placement_kernel(*refs, starts):
    directs, (direct_ref, chosen_ref, hit_ref) = refs[:-3], refs[-3:]
    ids = position()
    devices = direct_ref.shape[0]
    rows = hit_ref.shape[0] // 2
    slab = rows // 2
    piece_rows = rows // 8
    lane = iota((rows, LANES), 1)
    for pack in range(2):
        _, inner = owner_of(iota((rows, 1), 0), pack, ids, piece_rows)
        shard_row, _ = owner_of(iota((1, rows), 1), pack, ids, piece_rows)
        chosen = jnp.where((iota((devices, 1), 0) >> 2) == shard_row, 1.0, 0.0).astype(BF16)
        hit = jnp.where(lane == inner + pack * piece_rows, 1.0, 0.0)
        column = jnp.sum(by_pack(slabs(directs, starts, slab), pack), axis=1, keepdims=True)
        placed = place_rows(chosen, hit * column)
        direct_ref[...] = placed if pack == 0 else direct_ref[...] + placed
        chosen_ref[:, pack * rows:(pack + 1) * rows] = chosen
        hit_ref[pack * rows:(pack + 1) * rows, :] = hit


def placement(directs, starts, rows, devices):
    return pl.pallas_call(
        functools.partial(placement_kernel, starts=starts),
        out_shape=(
            shape_of(devices, LANES, kind=F32), shape_of(devices, 2 * rows), shape_of(2 * rows, LANES, kind=F32)),
        in_specs=[whole()] * len(directs),
        out_specs=(whole(),) * 3,
        compiler_params=pltpu.CompilerParams(vmem_limit_bytes=6 << 20),
        name="placement",
    )(*directs)


def attention_kernel(bias_ref, *refs, starts, recv_starts):
    chips = len(starts)
    owns, recvs, refs = refs[:chips], refs[chips:2 * chips], refs[2 * chips:]
    direct_ref, chosen_ref, hit_ref = refs[:3]
    nears, fars, gain_ref, out_ref = refs[3:6], refs[6:8], refs[8], refs[9]
    expo_ref, weight_ref = refs[10:]
    ids = position()
    segment, tp = ids[1], ids[3]
    rows = bias_ref.shape[0] // 2
    keys_wide = bias_ref.shape[1]
    slab = rows // 2
    heads = owns[0].shape[1] // HEAD
    wide = out_ref.shape[1] // 2
    scale = math.log2(math.e) / math.sqrt(HEAD)
    lane = iota((rows, wide), 1)
    used = lane < 2 * heads
    gains = [gain_ref[:, pl.ds(pl.multiple_of((segment * heads + head) * HEAD, HEAD), HEAD)].astype(F32)
             for head in range(heads)]
    gains = jnp.concatenate(gains * 2 + [jnp.zeros((LANES - 2 * heads, HEAD), F32)], axis=0).astype(BF16)

    def chosen_keys(refs):
        keep, first, second = (ref[...].astype(F32) for ref in refs)
        return (jnp.where(tp == 0, keep, jnp.where(tp == 2, second, first)),
                jnp.where(tp == 3, keep, jnp.where(tp == 1, second, first)))

    def pack_part(part, pack):
        count = part.shape[0] // 2
        return part[pack * count:(pack + 1) * count]

    far_first, far_second = (ref[...].astype(F32) for ref in fars)
    odd = (tp & 1) == 1
    far = (jnp.where(odd, far_first, far_second), jnp.where(odd, far_second, far_first))
    near = chosen_keys(nears)
    totals = []
    for pack in range(2):
        keys, values = (
            jnp.concatenate([
                pack_part(near_part, pack)[:slab],
                pack_part(near_part, pack)[slab:slab + slab // 2] + pack_part(far_part, pack),
                pack_part(near_part, pack)[slab + slab // 2:]], axis=0)
            for near_part, far_part in zip(near, far))
        keys = jnp.concatenate([keys, jnp.zeros((keys_wide - rows, HEAD), F32)], axis=0).astype(BF16)
        high = values.astype(BF16)
        rest = (values - high.astype(F32)).astype(BF16)
        product = (((1,), (1,)), ((), ()))
        score = (lax.dot_general(high, gains, product, preferred_element_type=F32)
                 + lax.dot_general(rest, gains, product, preferred_element_type=F32))
        high = score.astype(BF16).astype(F32)
        score = jnp.where(lane < heads, high, score - high)
        for head in range(heads):
            here = jnp.logical_and(used, (lane & (heads - 1)) == head)
            block = jnp.concatenate([jnp.where(here, score, 0.0), jnp.where(here, 1.0, 0.0)], axis=1)
            block = jnp.concatenate([block, jnp.zeros((keys_wide - rows, 2 * LANES), F32)], axis=0)
            weight_ref[head * keys_wide:(head + 1) * keys_wide, :] = block.astype(BF16)

            at = slice(head * HEAD, (head + 1) * HEAD)
            parts = [own + recv for own, recv in zip(
                slabs(owns, starts, slab, at), slabs(recvs, recv_starts, slab, at))]
            query = (by_pack(parts, pack) * scale).astype(BF16)
            logits = lax.dot_general(query, keys, product, preferred_element_type=F32)
            logits = logits + bias_ref[pack * rows:(pack + 1) * rows, :]
            expo = jnp.exp2(logits - jnp.max(logits, axis=1, keepdims=True)).astype(BF16)
            expo_ref[:, head * keys_wide:(head + 1) * keys_wide] = expo
        both = jnp.dot(expo_ref[...], weight_ref[...], preferred_element_type=F32)
        total = both[:, :LANES] / jnp.where(used, both[:, LANES:], 1.0)

        totals.append(jnp.sum(total, axis=1, keepdims=True))
    spread = hit_ref[...] * jnp.concatenate(totals, axis=0)
    out_ref[:, :wide] = place_rows(chosen_ref[...], spread)
    out_ref[:, wide:] = direct_ref[...]


def attention(bias, owns, starts, recvs, recv_starts, places, near, far, gain, devices):
    heads = owns[0].shape[1] // HEAD
    return pl.pallas_call(
        functools.partial(attention_kernel, starts=starts, recv_starts=recv_starts),
        out_shape=shape_of(devices, 2 * LANES, kind=F32),
        in_specs=[whole()] * (10 + 2 * len(owns)),
        out_specs=whole(),
        scratch_shapes=[
            pltpu.VMEM((bias.shape[0] // 2, heads * bias.shape[1]), BF16),
            pltpu.VMEM((heads * bias.shape[1], 2 * LANES), BF16),
        ],
        compiler_params=pltpu.CompilerParams(vmem_limit_bytes=14 << 20),
        name="attend",
    )(bias, *owns, *recvs, *places, *near, *far, gain)


def finish_kernel(recv_ref, send_ref, out_ref):
    models, count = out_ref.shape
    devices, width = recv_ref.shape
    model_of = iota((models, devices), 1) // (devices // models)
    chosen = (model_of == iota((models, devices), 0)).astype(F32)
    sums = jnp.dot(chosen, recv_ref[...], precision=HIGHEST, preferred_element_type=F32)
    pick = (iota((count, count), 0) == send_ref[...]).astype(F32)
    half = width // 2
    both = sums[:, :count] + sums[:, half:half + count]
    out_ref[...] = lax.dot_general(
        both, pick, (((1,), (1,)), ((), ())), precision=HIGHEST, preferred_element_type=F32)


def finish(recv, send, models):
    count = send.shape[1]
    return pl.pallas_call(
        finish_kernel,
        out_shape=jax.ShapeDtypeStruct((models, count), F32),
        in_specs=[whole()] * 2,
        out_specs=whole(),
        compiler_params=pltpu.CompilerParams(vmem_limit_bytes=8 << 20),
        name="finish",
    )(recv, send)


def paired(rollout, send_rows, seq_lengths, attn_gain, w_query, w_keyval, head_weight, head_attn):
    n_branch = lax.axis_size("branch")
    send = send_rows.reshape(1, -1)

    core_pairs = [(i, i ^ 1) for i in range(n_branch)]
    y_pairs = [(i, i ^ 2) for i in range(n_branch)]
    x_pairs = [(0, 1), (1, 0)]

    def swap(piece):
        return lax.ppermute(piece, "branch", core_pairs)

    def across(part):
        return lax.ppermute(part, "segment", x_pairs)

    def in_hbm(array):
        return pltpu.with_memory_space_constraint(array, pltpu.HBM)

    packing = send
    rollout, send, attn_gain, head_weight, seq_lengths = map(
        in_hbm, (rollout, send, attn_gain, head_weight, seq_lengths))
    wq, wkv = in_hbm(w_query[0]), in_hbm(w_keyval[0])
    mine, theirs = prepare(seq_lengths, rollout, send)
    from_x = across(theirs)
    from_y = lax.ppermute(mine, "branch", y_pairs)
    from_d = lax.ppermute(from_x, "branch", y_pairs)

    slab = 2 * mine.shape[0]

    def with_swapped(*pieces):
        return [part for piece in pieces for part in (piece, swap(piece))]

    pieces = with_swapped(mine)
    (rows, direct_own, local_own, part), weights, own_weights = first_chunk(
        *pieces, attn_gain, head_weight, wkv, wq)
    received_own = across(part)
    query_own = own_queries(rows, own_weights)
    bias = masks(seq_lengths, from_x, 2 * slab)

    pieces = with_swapped(from_x) + with_swapped(from_y)
    rows, direct_xy, local_xy, part, keyval = next_chunk(pieces, weights)
    keyval_xy = across(keyval)
    received_xy = across(part)
    query_xy = own_queries(rows, own_weights)

    hand_first, hand_second = (1, 3, 0, 2), (0, 2, 1, 3)
    n_tp = len(hand_first)

    def hand(array, targets):
        return lax.ppermute(array, "tp", [(i, to) for i, to in enumerate(targets) if i != to])

    def hand_across(array, targets):
        return lax.ppermute(array, ("segment", "tp"), [
            (side * n_tp + i, (1 - side) * n_tp + to) for side in range(2) for i, to in enumerate(targets)])

    pieces = with_swapped(from_d)
    rows, direct_d, part, keep, first, second, far_first, far_second = last_chunk(
        pieces, weights, (local_own, local_xy, keyval_xy, received_own))
    received_d = across(part)
    first = hand(first, hand_first)
    second = hand(second, hand_second)
    far_first = hand_across(far_first, hand_first)
    far_second = hand_across(far_second, hand_second)
    query_d = own_queries(rows, own_weights)
    devices = n_branch * 2 * n_tp
    places = placement([direct_own, direct_xy, direct_xy, direct_d], (0, 0, slab, 0), 2 * slab, devices)
    outgoing = attention(
        bias, [query_own, query_xy, query_xy, query_d], (0, 0, slab, 0),
        [received_xy, received_own, received_d, received_xy], (0, 0, 0, slab),
        places, (keep, first, second), (far_first, far_second), head_attn, devices)
    incoming = lax.all_to_all(outgoing, ALL_AXES, split_axis=0, concat_axis=0, tiled=True)
    return finish(incoming, packing, n_branch)


def general(rollout, send_rows, seq_lengths, attn_gain, w_query, w_keyval, head_weight, head_attn):
    n_branch = lax.axis_size("branch")
    n_segment = lax.axis_size("segment")
    gen_rows = rollout.shape[0]
    piece_rows = gen_rows // n_segment
    row_width = rollout.shape[1]
    ordered = jnp.take(rollout, send_rows, axis=0).reshape(n_segment, piece_rows, row_width)
    copies = jnp.broadcast_to(ordered[None], (n_branch, n_segment, piece_rows, row_width))
    copies = copies.reshape(n_branch * n_segment, piece_rows, row_width)
    arrived = lax.all_to_all(copies, ("branch", "segment"), split_axis=0, concat_axis=0, tiled=True)
    packed = arrived.reshape(-1, row_width)
    pack_rows = packed.shape[0]
    rows_float = packed.astype(jnp.float32)
    mean_square = jnp.mean(rows_float * rows_float, axis=-1, keepdims=True)
    normed = (
        rows_float * lax.rsqrt(mean_square + epsilon) * attn_gain[0].astype(jnp.float32)
    ).astype(jnp.bfloat16)
    query_acc = jnp.dot(
        normed,
        lax.all_gather(w_query, "segment", axis=1, tiled=True)[0],
        preferred_element_type=jnp.float32,
    )
    keyval_acc = jnp.dot(
        normed,
        lax.all_gather(w_keyval, "segment", axis=1, tiled=True)[0],
        preferred_element_type=jnp.float32,
    )
    queries = query_acc.astype(jnp.bfloat16)
    keyval_part = keyval_acc.astype(jnp.bfloat16)
    keyval = lax.all_gather(keyval_part, "tp", axis=1, tiled=True)
    tp_index = lax.axis_index("tp")
    heads_here = queries.shape[1] // HEAD
    group_size = HEADS // KV_HEADS
    per_group = min(heads_here, group_size)
    group_span = heads_here // per_group
    kv_first = tp_index * heads_here // group_size
    key_rows = lax.dynamic_slice_in_dim(keyval, kv_first * HEAD, group_span * HEAD, 1)
    value_rows = lax.dynamic_slice_in_dim(
        keyval, KV_HEADS * HEAD + kv_first * HEAD, group_span * HEAD, 1
    )
    key_rows = key_rows.reshape(pack_rows, group_span, HEAD)
    value_rows = value_rows.reshape(pack_rows, group_span, HEAD)
    queries = queries.reshape(pack_rows, group_span, per_group, HEAD)
    positions = jnp.arange(pack_rows, dtype=jnp.int32)
    doc_ends = jnp.cumsum(seq_lengths[0])
    doc_ids = jnp.sum((positions[:, None] >= doc_ends[None, :]).astype(jnp.int32), axis=-1)
    visible = (doc_ids[:, None] == doc_ids[None, :]) & (positions[None, :] <= positions[:, None])
    logits = jnp.einsum(
        "qgpc,kgc->gpqk", queries, key_rows, preferred_element_type=jnp.float32
    ) / math.sqrt(HEAD)
    logits = jnp.where(visible[None, None], logits, -1e30)
    row_max = jnp.max(logits, axis=-1, keepdims=True)
    expo = jnp.exp(logits - row_max)
    probabilities = (expo / jnp.sum(expo, axis=-1, keepdims=True)).astype(jnp.bfloat16)
    attended = jnp.einsum(
        "gpqk,kgc->qgpc", probabilities, value_rows, preferred_element_type=jnp.float32
    )
    attended = attended.reshape(pack_rows, heads_here * HEAD)
    slice_width = head_weight.shape[1]
    own_columns = lax.dynamic_slice_in_dim(packed, tp_index * slice_width, slice_width, 1)
    direct = jnp.dot(own_columns, head_weight[0], preferred_element_type=jnp.float32)
    through = jnp.dot(attended, head_attn[0].astype(jnp.float32), precision=lax.Precision.HIGHEST)
    totals = lax.psum(direct + through, "tp")
    outgoing = totals.reshape(n_branch * n_segment, piece_rows)
    incoming = lax.all_to_all(
        outgoing, ("branch", "segment"), split_axis=0, concat_axis=0, tiled=True
    )
    incoming = incoming.reshape(n_branch, n_segment * piece_rows)
    scores = jnp.zeros((n_branch, gen_rows), jnp.float32).at[:, send_rows].set(incoming)
    return scores


def solution(mesh):
    sizes = tuple(mesh.shape[axis] for axis in ALL_AXES)
    pairwise = sizes == (4, 2, 4)
    local = paired if pairwise else general
    return jax.shard_map(
        local,
        mesh=mesh,
        in_specs=(
            P(("branch", "segment"), None),
            P(("branch", "segment")),
            P("segment", None),
            P("branch", None),
            P("branch", "segment", "tp"),
            P("branch", "segment", "tp"),
            P("branch", "tp"),
            P("branch", "tp"),
        ),
        out_specs=P(None, ("branch", "segment")),
        check_vma=False,
    )
```
